32 devices in a mesh: dp: 4 (over y, core), ctx: 8 (over z, x).
Axes of the slice: x: 2, y: 2, z: 4, core: 2. Of those that a mesh axis runs over, the one named last changes fastest.
Arguments:
- tokens: bfloat16 [4, 2048, 768], P('dp', 'ctx'), may hold values from -6 to 6
- qkv_weight: bfloat16 [768, 2304], P(('dp', 'ctx')), may hold values from -0.21875 to 0.21875
- query_bias: bfloat16 [768], P(('dp', 'ctx')), may hold values from -3 to 3
- value_bias: bfloat16 [768], P(('dp', 'ctx')), may hold values from -3 to 3
- out_weight: bfloat16 [768, 768], P(('dp', 'ctx')), may hold values from -1.25 to 1.25
- out_bias: bfloat16 [768], P(('dp', 'ctx')), may hold values from -2 to 2
- attn_gain: bfloat16 [768], P(('dp', 'ctx')), may hold values from 0.5 to 1.5
- attn_shift: bfloat16 [768], P(('dp', 'ctx')), may hold values from -2 to 2
- up_weight: bfloat16 [768, 3072], P(('dp', 'ctx')), may hold values from -0.21875 to 0.21875
- up_bias: bfloat16 [3072], P(('dp', 'ctx')), may hold values from -3 to 3
- down_weight: bfloat16 [3072, 768], P(('dp', 'ctx')), may hold values from -0.109375 to 0.109375
- down_bias: bfloat16 [768], P(('dp', 'ctx')), may hold values from -2 to 2
- ffn_gain: bfloat16 [768], P(('dp', 'ctx')), may hold values from 0.5 to 1.5
- ffn_shift: bfloat16 [768], P(('dp', 'ctx')), may hold values from -2 to 2
- random_blocks: int32 [4, 32, 12, 3], P('dp', 'ctx'), may hold values from 0 to 31, as said below
- cotangent: bfloat16 [4, 2048, 768], P('dp', 'ctx'), may hold values from -6 to 6
Outputs:
- output: bfloat16 [4, 2048, 768], P('dp', 'ctx')
- tokens_grad: float32 [4, 2048, 768], P('dp', 'ctx')
- qkv_weight_grad: float32 [768, 2304], P(('dp', 'ctx'))
- query_bias_grad: float32 [768], P(('dp', 'ctx'))
- value_bias_grad: float32 [768], P(('dp', 'ctx'))
- out_weight_grad: float32 [768, 768], P(('dp', 'ctx'))
- out_bias_grad: float32 [768], P(('dp', 'ctx'))
- attn_gain_grad: float32 [768], P(('dp', 'ctx'))
- attn_shift_grad: float32 [768], P(('dp', 'ctx'))
- up_weight_grad: float32 [768, 3072], P(('dp', 'ctx'))
- up_bias_grad: float32 [3072], P(('dp', 'ctx'))
- down_weight_grad: float32 [3072, 768], P(('dp', 'ctx'))
- down_bias_grad: float32 [768], P(('dp', 'ctx'))
- ffn_gain_grad: float32 [768], P(('dp', 'ctx'))
- ffn_shift_grad: float32 [768], P(('dp', 'ctx'))
The draws below stay inside these ranges and needn't reach their ends.
Inputs may be any that keep to these rules, and one draw needn't show every extreme that they name: `random_blocks`: key blocks j * 4 to (j + 1) * 4 - 1 of a sequence are those of index j of ctx. Over the query blocks of one sequence on one index of ctx (all heads and all 3 entries), the blocks of any one index of ctx are named at most 24 times, and exactly 24 times for one index.
All inputs are finite; a program needn't handle non-finite values.
Results may differ from the reference program's by a relative error of at most 0.014.
Values may be sent and summed in bfloat16 or wider, within the bound.
No kernel may reach another device: no remote copies, remote signals or barrier semaphores. Data moves between devices by JAX's collectives and lax.ppermute only.
A program may use at most 192 MiB of HBM per device.

```python
import jax
import jax.numpy as jnp
from jax import lax

D = 768
H = 12
FF = 3072
HD = 64
BLK = 64
RAND = 3
LEN = 2048
SEQS = 4
BPD = 4
CAP = 24
N_CTX = 8


def draw_random_blocks(key, part):
    entries = BPD * H * RAND

    def draw_group(subkey):
        key_hot, key_pool, key_mix, key_inner = jax.random.split(subkey, 4)
        hottest = jax.random.randint(key_hot, (), 0, N_CTX, dtype=jnp.int32)
        others = jnp.arange((N_CTX - 1) * CAP, dtype=jnp.int32) // CAP
        others = others + (others >= hottest).astype(jnp.int32)
        picked = jax.random.permutation(key_pool, others)[:entries - CAP]
        owners = jnp.concatenate([jnp.full((CAP,), hottest, dtype=jnp.int32), picked])
        owners = jax.random.permutation(key_mix, owners)
        within = jax.random.randint(key_inner, (entries,), 0, BPD, dtype=jnp.int32)
        return (owners * BPD + within).reshape(BPD, H, RAND)
    subkeys = jax.random.split(key, SEQS * N_CTX)
    blocks = jax.vmap(draw_group)(subkeys)
    return blocks.reshape(SEQS, N_CTX * BPD, H, RAND).astype(jnp.int32)


def block_scale(rng, dims, cuts, smallest, top_value):
    loudness, own = 1.0, jax.random.fold_in(rng, 6)
    for position, shards_of in cuts:
        steps = jnp.exp(jax.random.uniform(jax.random.fold_in(own, position), (shards_of,), jnp.float32, smallest / len(cuts), top_value / len(cuts)))
        loudness = loudness * jnp.repeat(steps, dims[position] // shards_of).reshape([-1 if axis == position else 1 for axis in range(len(dims))])
    return loudness


def bell_draw(key, shape, scale, reach, pieces=(), kind=jnp.bfloat16):
    level = block_scale(key, shape, pieces, -0.22, 0.18) if pieces else 1.0
    values = jax.random.normal(key, shape, jnp.float32) * scale * level
    return jnp.minimum(jnp.maximum(values, -reach), reach).astype(kind)


def setup_inputs(seed: int = 0) -> dict:
    splits = jax.random.split(jax.random.key(seed), 17)
    return {
        "tokens": bell_draw(splits[0], (SEQS, LEN, D), 1.0, 6.0, ((0, 4), (1, 8))),
        "qkv_weight": bell_draw(splits[1], (D, 3 * D), D ** -0.5, 0.21875, ((0, 32),)),
        "query_bias": bell_draw(splits[2], (D,), 0.5, 3.0, ((0, 32),)),
        "value_bias": bell_draw(splits[3], (D,), 0.5, 3.0, ((0, 32),)),
        "out_weight": bell_draw(splits[4], (D, D), (D // 32) ** -0.5, 1.25, ((0, 32),)),
        "out_bias": bell_draw(splits[5], (D,), 0.3, 2.0, ((0, 32),)),
        "attn_gain": jnp.clip(1.0 + 0.1 * jax.random.normal(splits[6], (D,), jnp.float32), 0.5, 1.5).astype(jnp.bfloat16),
        "attn_shift": bell_draw(splits[7], (D,), 0.3, 2.0, ((0, 32),)),
        "up_weight": bell_draw(splits[8], (D, FF), D ** -0.5, 0.21875, ((0, 32),)),
        "up_bias": bell_draw(splits[9], (FF,), 0.5, 3.0, ((0, 32),)),
        "down_weight": bell_draw(splits[10], (FF, D), FF ** -0.5, 0.109375, ((0, 32),)),
        "down_bias": bell_draw(splits[11], (D,), 0.3, 2.0, ((0, 32),)),
        "ffn_gain": jnp.clip(1.0 + 0.1 * jax.random.normal(splits[12], (D,), jnp.float32), 0.5, 1.5).astype(jnp.bfloat16),
        "ffn_shift": bell_draw(splits[13], (D,), 0.3, 2.0, ((0, 32),)),
        "random_blocks": draw_random_blocks(jax.random.fold_in(splits[16], 71), 0),
        "cotangent": bell_draw(splits[15], (SEQS, LEN, D), 1.0, 6.0, ((0, 4), (1, 8))),
    }


@jax.custom_vjp
def low(v):
    return lax.optimization_barrier(v.astype(jnp.bfloat16)).astype(jnp.float32)

@jax.custom_vjp
def low_back(v):
    return v

def low_keep(v):
    return (low(v), None)

def low_pass(kept, grad):
    return (grad,)

def back_keep(v):
    return (v, None)

def back_low(kept, grad):
    return (low(grad),)
low.defvjp(low_keep, low_pass)
low_back.defvjp(back_keep, back_low)

def matmul_high(left_side, right_side):
    return jnp.dot(left_side, right_side, precision=lax.Precision.HIGHEST, preferred_element_type=jnp.float32)

def rounded(values):
    return low(low_back(values))

def gelu_tanh(values):
    return 0.5 * values * (1.0 + jnp.tanh(0.7978845608028654 * (values + 0.044715 * values * values * values)))

def layer_norm(values, norm_gain, norm_shift):
    center = values - lax.optimization_barrier(jnp.mean(values, axis=-1, keepdims=True))
    spread = lax.optimization_barrier(jnp.mean(center * center, axis=-1, keepdims=True))
    return center * lax.rsqrt(spread + 1e-06) * norm_gain + norm_shift

def softmax_rows(scores):
    shifted = scores - lax.optimization_barrier(jnp.max(scores, axis=-1, keepdims=True))
    exponent = jnp.exp(shifted)
    return exponent / lax.optimization_barrier(jnp.sum(exponent, axis=-1, keepdims=True))

def sequence_layer(seq_x, rand_seq, params):
    qkv_weight, query_bias, value_bias, out_weight, out_bias, attn_gain, attn_shift, up_weight, up_bias, down_weight, down_bias, ffn_gain, ffn_shift = params
    length = seq_x.shape[0]
    block_count = length // BLK
    qkv_rows = matmul_high(seq_x, qkv_weight)
    query_rows = rounded(qkv_rows[:, :D] + query_bias)
    key_rows = rounded(qkv_rows[:, D:2 * D])
    value_rows = rounded(qkv_rows[:, 2 * D:] + value_bias)

    def as_tiles(columns):
        return columns.reshape(block_count, BLK, H, HD).transpose(0, 2, 1, 3)
    query_tiles = as_tiles(query_rows)
    key_tiles = as_tiles(key_rows)
    value_tiles = as_tiles(value_rows)
    block_index = jnp.arange(block_count, dtype=jnp.int32)
    fixed_blocks = jnp.stack([block_index - 1, block_index, block_index + 1, jnp.zeros_like(block_index), jnp.full_like(block_index, block_count - 1)], axis=1)
    fixed_blocks = jnp.clip(fixed_blocks, 0, block_count - 1).astype(jnp.int32)
    chosen = jnp.concatenate([jnp.broadcast_to(fixed_blocks[:, None, :], (block_count, H, 5)), rand_seq.astype(jnp.int32)], axis=2)
    head_index = jnp.arange(H, dtype=jnp.int32)[None, :, None]
    score_scale = HD ** (-0.5)

    def block_group(group_items):
        query_grp, chosen_grp = group_items
        key_sel = key_tiles[chosen_grp, head_index]
        value_sel = value_tiles[chosen_grp, head_index]
        raw_scores = jnp.einsum('ghqd,ghjkd->ghqjk', query_grp, key_sel, precision=lax.Precision.HIGHEST)
        scores = score_scale * low_back(raw_scores)
        attn_probs = low(softmax_rows(scores.reshape(scores.shape[:3] + (-1,)))).reshape(scores.shape)
        return jnp.einsum('ghqjk,ghjkd->ghqd', attn_probs, value_sel, precision=lax.Precision.HIGHEST)
    regular = lax.map(jax.checkpoint(block_group), (query_tiles.reshape(N_CTX, BPD, H, BLK, HD), chosen.reshape(N_CTX, BPD, H, 5 + RAND)))
    regular = regular.reshape(block_count, H, BLK, HD)
    edge_query = query_tiles[jnp.array([0, block_count - 1], dtype=jnp.int32)]
    raw_global = jnp.einsum('ghqd,bhkd->ghqbk', edge_query, key_tiles, precision=lax.Precision.HIGHEST)
    global_scores = score_scale * low_back(raw_global)
    global_probs = low(softmax_rows(global_scores.reshape(2, H, BLK, length))).reshape(global_scores.shape)
    global_out = jnp.einsum('ghqbk,bhkd->ghqd', global_probs, value_tiles, precision=lax.Precision.HIGHEST)
    combined = regular.at[0].set(global_out[0]).at[block_count - 1].set(global_out[1])
    attn_rows = rounded(combined.transpose(0, 2, 1, 3).reshape(length, D))
    branch = low_back(matmul_high(attn_rows, out_weight) + out_bias)
    mid_norm = layer_norm(seq_x + branch, attn_gain, attn_shift)
    pre_act = low_back(matmul_high(low(mid_norm), up_weight) + up_bias)
    activation = low(gelu_tanh(pre_act))
    branch_two = low_back(matmul_high(activation, down_weight) + down_bias)
    return layer_norm(mid_norm + branch_two, ffn_gain, ffn_shift)

def reference(tokens, qkv_weight, query_bias, value_bias, out_weight, out_bias, attn_gain, attn_shift, up_weight, up_bias, down_weight, down_bias, ffn_gain, ffn_shift, random_blocks, cotangent):
    params = tuple((argument.astype(jnp.float32) for argument in (qkv_weight, query_bias, value_bias, out_weight, out_bias, attn_gain, attn_shift, up_weight, up_bias, down_weight, down_bias, ffn_gain, ffn_shift)))

    def forward(inputs, weights):

        def scan_step(scan_carry, seq_items):
            seq_x, rand_seq = seq_items
            return (scan_carry, jax.checkpoint(sequence_layer)(seq_x, rand_seq, weights))
        scan_carry, layer_outs = lax.scan(scan_step, jnp.zeros((), jnp.float32), (inputs, random_blocks))
        return layer_outs
    output, pullback = jax.vjp(forward, tokens.astype(jnp.float32), params)
    tokens_grad, weight_grads = pullback(cotangent.astype(jnp.float32))
    return (output.astype(jnp.bfloat16), tokens_grad, weight_grads[0], weight_grads[1], weight_grads[2], weight_grads[3], weight_grads[4], weight_grads[5], weight_grads[6], weight_grads[7], weight_grads[8], weight_grads[9], weight_grads[10], weight_grads[11], weight_grads[12])
```

```python
import functools

import jax
import jax.numpy as jnp
from jax import lax
from jax.experimental import pallas as pl
from jax.experimental.pallas import tpu as pltpu
from jax.sharding import Mesh, PartitionSpec as P

H = 12
HD = 64
BLK = 64
RAND = 3
GROUPS = 4
PER_GROUP = 3
PAD_ROWS = 16
EXTRA = 128
VMEM_BYTES = 56 * 1024 * 1024

bf16 = jnp.bfloat16
f32 = jnp.float32

norm_eps = 1e-06
gelu_root = 0.7978845608028654
gelu_cubic = 0.044715

ALL = ("y", "core", "z", "x")
CTX = ("z", "x")


def gelu_tanh(values):
    return (
        0.5
        * values
        * (1.0 + jnp.tanh(gelu_root * (values + gelu_cubic * values * values * values)))
    )


def layer_norm(values, norm_gain, norm_shift):
    center = values - jnp.mean(values, axis=-1, keepdims=True)
    spread = jnp.mean(center * center, axis=-1, keepdims=True)
    return center * lax.rsqrt(spread + norm_eps) * norm_gain + norm_shift


def contract_rows(left_side, right_side):
    return lax.dot_general(
        left_side, right_side, (((0,), (0,)), ((), ())), preferred_element_type=f32
    )


def contract_cols(left_side, right_side):
    return lax.dot_general(
        left_side, right_side, (((1,), (1,)), ((), ())), preferred_element_type=f32
    )


def plain(left_side, right_side):
    return jnp.dot(left_side, right_side, preferred_element_type=f32)


def heads_of(index, ranks):
    group, rank = index // ranks, index % ranks
    first = PER_GROUP * group + (0 if rank < ranks // 2 else 1)
    return first, PER_GROUP * group + 2


def qkv_kernel(count, ranks, x_ref, w_ref, b_ref, rnd_ref, out_ref):
    tok, width = x_ref.shape
    x = x_ref[...]
    for part in range(3):
        rows = plain(x, w_ref[:, part * width : (part + 1) * width]) + b_ref[part : part + 1, :]
        rows = rows.astype(bf16)
        for j in range(count):
            first, shared = heads_of(j, ranks)
            out_ref[j, 0:tok, part * 128 : (part + 1) * 128] = jnp.concatenate(
                [rows[:, first * HD : (first + 1) * HD], rows[:, shared * HD : (shared + 1) * HD]],
                axis=1,
            )
    for j in range(count):
        out_ref[j, tok : tok + PAD_ROWS, :] = rnd_ref[j]


def qkv_chunks(count, ranks, tokens, weights, bias, rnd):
    tok = tokens.shape[0]
    return pl.pallas_call(
        functools.partial(qkv_kernel, count, ranks),
        out_shape=jax.ShapeDtypeStruct((count, tok + PAD_ROWS, 384), bf16),
        in_specs=[pl.BlockSpec(memory_space=pltpu.VMEM)] * 4,
        out_specs=pl.BlockSpec(memory_space=pltpu.VMEM),
        compiler_params=pltpu.CompilerParams(vmem_limit_bytes=VMEM_BYTES),
        name="qkv_chunks",
    )(tokens, weights, bias, rnd)


class Plan:
    def __init__(self, count, ranks, blocks):
        self.count, self.ranks, self.blocks = count, ranks, blocks
        self.steps = (ranks // 2, ranks)
        self.owners = (count // self.steps[0], count // self.steps[1])
        self.total = count * blocks
        self.units = (self.owners[0] + self.owners[1]) * blocks
        self.stride = blocks * BLK + PAD_ROWS

    def key_rows(self, block):
        return pl.multiple_of(
            (block // self.blocks) * self.stride + (block % self.blocks) * BLK, 16
        )

    def sum_rows(self, block):
        return pl.multiple_of(block * BLK, BLK)

    def unit(self, half, turn, inner):
        return (half * self.owners[0] + turn) * self.blocks + inner

    def named(self, half, owner, inner, rand_ref):
        block = owner * self.blocks + inner
        ids = [
            jnp.maximum(block - 1, 0),
            block,
            jnp.minimum(block + 1, self.total - 1),
            0,
            self.total - 1,
        ]
        for t in range(RAND):
            ids.append(rand_ref[(block * 2 + half) * RAND + t])
        return ids


def lane_half(rows, half):
    lane = lax.broadcasted_iota(jnp.int32, (rows, 128), 1)
    return (lane < HD) if half == 0 else (lane >= HD)


def only_half(values, half):
    return jnp.where(lane_half(values.shape[0], half), values, jnp.zeros_like(values))


def attn_forward_kernel(plan, rand_ref, rank_ref, kv_ref, out_ref, lse_ref, score_ref):
    tok = plan.blocks * BLK
    rank = rank_ref[0]
    out_ref[...] = jnp.zeros_like(out_ref)

    def emit(half, owner, inner, unit, attended, lse):
        lanes = pl.ds(half * HD, HD)
        out_ref[pl.ds(pl.multiple_of(owner * tok + inner * BLK, BLK), BLK), lanes] = attended[
            :, half * HD : (half + 1) * HD
        ].astype(bf16)
        lse_ref[pl.ds(pl.multiple_of(unit * BLK, BLK), BLK), :] = jnp.broadcast_to(lse, (BLK, 128))

    def query(half, owner, inner):
        rows = pl.multiple_of(owner * plan.stride + inner * BLK, 16)
        return only_half(kv_ref[pl.ds(rows, BLK), 0:128], half) * 0.125

    for half in range(2):
        step = plan.steps[half]
        offset = lax.rem(rank, step) if step > 1 else 0

        def turn_body(turn, carry, half=half, step=step, offset=offset):
            owner = turn * step + offset
            for inner in range(plan.blocks):
                ids = plan.named(half, owner, inner, rand_ref)
                rows = [plan.key_rows(i) for i in ids]
                keys = jnp.concatenate([kv_ref[pl.ds(r, BLK), 128:256] for r in rows], axis=0)
                values = jnp.concatenate([kv_ref[pl.ds(r, BLK), 256:384] for r in rows], axis=0)
                scores = contract_cols(query(half, owner, inner), keys)
                top = jnp.max(scores, axis=-1, keepdims=True)
                grown = jnp.exp(scores - top)
                total = jnp.sum(grown, axis=-1, keepdims=True)
                probs = (grown * (1.0 / total)).astype(bf16)
                attended = plain(probs, values)
                emit(half, owner, inner, plan.unit(half, turn, inner), attended, top + jnp.log(total))
            return carry

        lax.fori_loop(0, plan.owners[half], turn_body, 0)

    for half in range(2):
        step = plan.steps[half]
        for owner, inner in ((0, 0), (plan.count - 1, plan.blocks - 1)):

            def whole(half=half, step=step, owner=owner, inner=inner):
                q = query(half, owner, inner)

                def score_body(o, top):
                    rows = pl.multiple_of(o * plan.stride, 16)
                    part = contract_cols(q, kv_ref[pl.ds(rows, tok), 128:256])
                    score_ref[o] = part
                    return jnp.maximum(top, jnp.max(part, axis=-1, keepdims=True))

                top = lax.fori_loop(
                    0, plan.count, score_body, jnp.full((BLK, 1), -jnp.inf, f32)
                )

                def sum_body(o, total):
                    grown = jnp.exp(score_ref[o] - top)
                    score_ref[o] = grown
                    return total + jnp.sum(grown, axis=-1, keepdims=True)

                total = lax.fori_loop(0, plan.count, sum_body, jnp.zeros((BLK, 1), f32))
                scale = 1.0 / total

                def value_body(o, attended):
                    rows = pl.multiple_of(o * plan.stride, 16)
                    probs = (score_ref[o] * scale).astype(bf16)
                    return attended + plain(probs, kv_ref[pl.ds(rows, tok), 256:384])

                attended = lax.fori_loop(0, plan.count, value_body, jnp.zeros((BLK, 128), f32))
                unit = plan.unit(half, owner // step, inner)
                emit(half, owner, inner, unit, attended, top + jnp.log(total))

            if step == 1:
                whole()
            else:
                pl.when(lax.rem(rank, step) == owner % step)(whole)


def attn_forward(plan, rand, rank, kv):
    tok = plan.blocks * BLK
    return pl.pallas_call(
        functools.partial(attn_forward_kernel, plan),
        out_shape=(
            jax.ShapeDtypeStruct((plan.count * tok, 128), bf16),
            jax.ShapeDtypeStruct((plan.units * BLK, 128), f32),
        ),
        in_specs=[
            pl.BlockSpec(memory_space=pltpu.SMEM),
            pl.BlockSpec(memory_space=pltpu.SMEM),
            pl.BlockSpec(memory_space=pltpu.VMEM),
        ],
        out_specs=(pl.BlockSpec(memory_space=pltpu.VMEM),) * 2,
        scratch_shapes=[pltpu.VMEM((plan.count, BLK, tok), f32)],
        compiler_params=pltpu.CompilerParams(vmem_limit_bytes=VMEM_BYTES),
        name="attn_forward",
    )(rand, rank, kv)


def attn_backward_kernel(
    plan, rand_ref, rank_ref, kv_ref, dout_ref, lse_ref, out_ref, sum_ref, prob_ref, dprob_ref
):
    tok = plan.blocks * BLK
    rank = rank_ref[0]
    out_ref[:, 0:128] = jnp.zeros((plan.count * tok, 128), bf16)
    sum_ref[...] = jnp.zeros_like(sum_ref)

    def operands(half, owner, inner, unit):
        rows = pl.multiple_of(owner * plan.stride + inner * BLK, 16)
        q = only_half(kv_ref[pl.ds(rows, BLK), 0:128], half) * 0.125
        drows = pl.multiple_of(owner * tok + inner * BLK, BLK)
        dout = only_half(dout_ref[pl.ds(drows, BLK), :], half)
        lse = lse_ref[pl.ds(pl.multiple_of(unit * BLK, BLK), BLK), :][:, 0:1]
        return q, dout, lse

    def emit(half, owner, inner, grad_query):
        out_ref[
            pl.ds(pl.multiple_of(owner * tok + inner * BLK, BLK), BLK), pl.ds(half * HD, HD)
        ] = (grad_query[:, half * HD : (half + 1) * HD] * 0.125).astype(bf16)

    for half in range(2):
        step = plan.steps[half]
        offset = lax.rem(rank, step) if step > 1 else 0

        def turn_body(turn, carry, half=half, step=step, offset=offset):
            owner = turn * step + offset
            found = []
            for inner in range(plan.blocks):
                ids = plan.named(half, owner, inner, rand_ref)
                rows = [plan.key_rows(i) for i in ids]
                keys = jnp.concatenate([kv_ref[pl.ds(r, BLK), 128:256] for r in rows], axis=0)
                values = jnp.concatenate([kv_ref[pl.ds(r, BLK), 256:384] for r in rows], axis=0)
                q, dout, lse = operands(half, owner, inner, plan.unit(half, turn, inner))
                if inner in (0, plan.blocks - 1):
                    block = owner * plan.blocks + inner
                    edge = (block == 0) | (block == plan.total - 1)
                    dout = dout * jnp.where(edge, 0.0, 1.0).astype(bf16)
                    kept = jnp.where(edge, 0.0, 1.0)
                else:
                    kept = None
                probs = jnp.exp(contract_cols(q, keys) - lse)
                grad_probs = contract_cols(dout, values)
                delta = jnp.sum(probs * grad_probs, axis=-1, keepdims=True)
                grad_scores = (probs * (grad_probs - delta)).astype(bf16)
                emit(half, owner, inner, plain(grad_scores, keys))
                grad_keys = contract_rows(grad_scores, q)
                grad_values = contract_rows(probs.astype(bf16), dout)
                found.append((ids, grad_keys, grad_values))
            for ids, grad_keys, grad_values in found:
                for t, i in enumerate(ids):
                    at = pl.ds(plan.sum_rows(i), BLK)
                    sum_ref[at, 0:128] += grad_keys[t * BLK : (t + 1) * BLK]
                    sum_ref[at, 128:256] += grad_values[t * BLK : (t + 1) * BLK]
            return carry

        lax.fori_loop(0, plan.owners[half], turn_body, 0)

    for half in range(2):
        step = plan.steps[half]
        for owner, inner in ((0, 0), (plan.count - 1, plan.blocks - 1)):

            def whole(half=half, step=step, owner=owner, inner=inner):
                unit = plan.unit(half, owner // step, inner)
                q, dout, lse = operands(half, owner, inner, unit)

                def first_body(o, delta):
                    rows = pl.ds(pl.multiple_of(o * plan.stride, 16), tok)
                    probs = jnp.exp(contract_cols(q, kv_ref[rows, 128:256]) - lse)
                    grad_probs = contract_cols(dout, kv_ref[rows, 256:384])
                    prob_ref[o] = probs
                    dprob_ref[o] = grad_probs
                    return delta + jnp.sum(probs * grad_probs, axis=-1, keepdims=True)

                delta = lax.fori_loop(0, plan.count, first_body, jnp.zeros((BLK, 1), f32))

                def second_body(o, grad_query):
                    rows = pl.ds(pl.multiple_of(o * plan.stride, 16), tok)
                    at = pl.ds(pl.multiple_of(o * tok, tok), tok)
                    probs = prob_ref[o]
                    grad_scores = (probs * (dprob_ref[o] - delta)).astype(bf16)
                    sum_ref[at, 0:128] += contract_rows(grad_scores, q)
                    sum_ref[at, 128:256] += contract_rows(probs.astype(bf16), dout)
                    return grad_query + plain(grad_scores, kv_ref[rows, 128:256])

                emit(
                    half,
                    owner,
                    inner,
                    lax.fori_loop(0, plan.count, second_body, jnp.zeros((BLK, 128), f32)),
                )

            if step == 1:
                whole()
            else:
                pl.when(lax.rem(rank, step) == owner % step)(whole)

    out_ref[:, 128:384] = sum_ref[...].astype(bf16)


def attn_backward(plan, rand, rank, kv, dout, lse):
    tok = plan.blocks * BLK
    return pl.pallas_call(
        functools.partial(attn_backward_kernel, plan),
        out_shape=jax.ShapeDtypeStruct((plan.count * tok, 384), bf16),
        in_specs=[
            pl.BlockSpec(memory_space=pltpu.SMEM),
            pl.BlockSpec(memory_space=pltpu.SMEM),
            pl.BlockSpec(memory_space=pltpu.VMEM),
            pl.BlockSpec(memory_space=pltpu.VMEM),
            pl.BlockSpec(memory_space=pltpu.VMEM),
        ],
        out_specs=pl.BlockSpec(memory_space=pltpu.VMEM),
        scratch_shapes=[
            pltpu.VMEM((plan.count * tok, 256), f32),
            pltpu.VMEM((plan.count, BLK, tok), f32),
            pltpu.VMEM((plan.count, BLK, tok), f32),
        ],
        compiler_params=pltpu.CompilerParams(vmem_limit_bytes=VMEM_BYTES),
        name="attn_backward",
    )(rand, rank, kv, dout, lse)


def swap(value, axis):
    return lax.all_to_all(value, axis, split_axis=0, concat_axis=0, tiled=True)


def gather_small(shard):
    ny, nc, nz, nx = (lax.axis_size(a) for a in ALL)
    rows, cols = shard.shape
    line = swap(jnp.broadcast_to(shard[None], (nz, rows, cols)), "z")
    plane = swap(jnp.broadcast_to(line[None], (ny * nx, nz, rows, cols)), ("y", "x"))
    both = swap(jnp.broadcast_to(plane[None], (nc, ny * nx, nz, rows, cols)), "core")
    return (
        both.reshape(nc, ny, nx, nz, rows, cols)
        .transpose(1, 0, 3, 2, 4, 5)
        .reshape(ny * nc * nz * nx * rows, cols)
    )


def scatter_small(value):
    ny, nc, nz, nx = (lax.axis_size(a) for a in ALL)
    cols = value.shape[1]
    rows = value.shape[0] // (ny * nc * nz * nx)
    parts = value.reshape(ny, nc, nz, nx, rows, cols).transpose(1, 0, 3, 2, 4, 5)
    parts = parts.astype(bf16).reshape(nc, ny * nx, nz, rows, cols)
    parts = jnp.sum(swap(parts, "core").astype(f32), axis=0).astype(bf16)
    parts = jnp.sum(swap(parts, ("y", "x")).astype(f32), axis=0).astype(bf16)
    return jnp.sum(swap(parts, "z").astype(f32), axis=0)


def body(
    tokens,
    qkv_weight,
    query_bias,
    value_bias,
    out_weight,
    out_bias,
    attn_gain,
    attn_shift,
    up_weight,
    up_bias,
    down_weight,
    down_bias,
    ffn_gain,
    ffn_shift,
    random_blocks,
    cotangent,
):
    count = lax.axis_size("z") * lax.axis_size("x")
    ranks = count // GROUPS
    _, tok, width = tokens.shape
    blocks = tok // BLK
    plan = Plan(count, ranks, blocks)
    ctx_index = lax.axis_index("z") * lax.axis_size("x") + lax.axis_index("x")
    rank = lax.rem(ctx_index, ranks).astype(jnp.int32).reshape(1)
    rows = qkv_weight.shape[0]
    hidden = up_weight.shape[1]
    flat_tokens = tokens.reshape(tok, width)

    small = [query_bias, value_bias, out_bias, attn_gain, attn_shift, down_bias, ffn_gain, ffn_shift]
    columns = jnp.concatenate(
        [jnp.stack(small, axis=1), up_bias.reshape(rows, hidden // width)], axis=1
    )
    columns = jnp.pad(columns, ((0, 0), (0, EXTRA - columns.shape[1])))
    qkv_ext = gather_small(jnp.concatenate([qkv_weight, columns], axis=1))
    qkv_full = qkv_ext[:, : 3 * width]
    biases = qkv_ext[:, 3 * width :].astype(f32)
    vectors = biases[:, :8].T
    up_bias_full = biases[:, 8 : 8 + hidden // width].reshape(1, hidden)
    packed = jnp.concatenate(
        [out_weight, up_weight, down_weight.reshape(rows, -1)], axis=1
    )
    packed_full = lax.all_gather(packed, ALL, axis=0, tiled=True)
    out_full = packed_full[:, :width]
    up_full = packed_full[:, width : width + hidden]
    down_full = packed_full[:, width + hidden :].reshape(hidden, width)

    picks = random_blocks[0].astype(bf16)
    rnd = []
    for j in range(count):
        first, shared = heads_of(j, ranks)
        rnd.append(jnp.stack([picks[:, first], picks[:, shared]], axis=1).reshape(-1))
    rnd = jnp.stack(rnd)
    entries = rnd.shape[1]
    rnd = jnp.pad(rnd[:, None, :], ((0, 0), (0, PAD_ROWS - 1), (0, 384 - entries)))

    qkv_bias = jnp.stack([vectors[0], jnp.zeros_like(vectors[0]), vectors[1]])
    chunks = qkv_chunks(count, ranks, flat_tokens, qkv_full, qkv_bias, rnd)
    kv = swap(chunks, CTX)
    rand = kv[:, tok, :entries].astype(jnp.int32).reshape(-1)
    kv = kv.reshape(count * plan.stride, 384)
    attended, lse = attn_forward(plan, rand, rank, kv)
    back = swap(attended.reshape(count, tok, 128), CTX)
    back = back.reshape(GROUPS, ranks, tok, 2, HD)
    half_ranks = ranks // 2

    def add(values):
        return values[:, 0] if values.shape[1] == 1 else jnp.sum(values, axis=1)

    attn_low = (
        jnp.stack(
            [
                add(back[:, :half_ranks, :, 0]),
                add(back[:, half_ranks:, :, 0]),
                add(back[:, :, :, 1]),
            ],
            axis=1,
        )
        .transpose(2, 0, 1, 3)
        .reshape(tok, width)
    )

    branch = plain(attn_low, out_full) + vectors[2]
    mid_norm, mid_pull = jax.vjp(
        layer_norm, flat_tokens.astype(f32) + branch, vectors[3], vectors[4]
    )
    mid_low = mid_norm.astype(bf16)
    pre_act = plain(mid_low, up_full) + up_bias_full
    activation, gelu_pull = jax.vjp(gelu_tanh, pre_act)
    act_low = activation.astype(bf16)
    branch_two = plain(act_low, down_full) + vectors[5]
    final_norm, final_pull = jax.vjp(layer_norm, mid_norm + branch_two, vectors[6], vectors[7])
    output = final_norm.astype(bf16).reshape(1, tok, width)
    grad_final, grad_ffn_gain, grad_ffn_shift = final_pull(
        cotangent.reshape(tok, width).astype(f32)
    )
    down_low = grad_final.astype(bf16)
    grad_down_bias = jnp.sum(down_low.astype(f32), axis=0)
    grad_down = contract_rows(act_low, down_low).astype(bf16)
    (grad_pre,) = gelu_pull(contract_cols(down_low, down_full))
    pre_low = grad_pre.astype(bf16)
    grad_up_bias = jnp.sum(pre_low.astype(f32), axis=0)
    grad_up = contract_rows(mid_low, pre_low).astype(bf16)
    grad_mid = grad_final + contract_cols(pre_low, up_full)
    grad_resid, grad_attn_gain, grad_attn_shift = mid_pull(grad_mid)
    branch_low = grad_resid.astype(bf16)
    grad_out_bias = jnp.sum(branch_low.astype(f32), axis=0)
    grad_out = contract_rows(attn_low, branch_low).astype(bf16)
    grad_attn = contract_cols(branch_low, out_full).astype(bf16)

    tiles = grad_attn.reshape(tok, H, HD)
    dout = []
    for j in range(count):
        first, shared = heads_of(j, ranks)
        dout.append(jnp.concatenate([tiles[:, first], tiles[:, shared]], axis=1))
    dout = swap(jnp.stack(dout), CTX).reshape(count * tok, 128)
    grads = attn_backward(plan, rand, rank, kv, dout, lse)
    grads = swap(grads.reshape(count, tok, 384), CTX)
    grads = grads.reshape(GROUPS, ranks, tok, 3, 2, HD).astype(f32)
    qkv_grad_low = (
        jnp.stack(
            [
                add(grads[:, :half_ranks, :, :, 0]),
                add(grads[:, half_ranks:, :, :, 0]),
                add(grads[:, :, :, :, 1]),
            ],
            axis=1,
        )
        .astype(bf16)
        .transpose(2, 3, 0, 1, 4)
        .reshape(tok, 3 * width)
    )
    column_sums = jnp.sum(qkv_grad_low.astype(f32), axis=0)
    grad_qkv = contract_rows(flat_tokens, qkv_grad_low).astype(bf16)
    tokens_grad = (grad_resid + contract_cols(qkv_grad_low, qkv_full)).reshape(1, tok, width)

    wide = lax.psum_scatter(
        jnp.concatenate([grad_out, grad_up, grad_down.reshape(width, -1)], axis=1),
        ALL,
        scatter_dimension=0,
        tiled=True,
    ).astype(f32)
    grad_small = jnp.stack(
        [
            column_sums[:width],
            column_sums[2 * width :],
            grad_out_bias,
            grad_attn_gain,
            grad_attn_shift,
            grad_down_bias,
            grad_ffn_gain,
            grad_ffn_shift,
        ],
        axis=1,
    )
    grad_columns = jnp.concatenate(
        [grad_small, grad_up_bias.reshape(width, hidden // width)], axis=1
    ).astype(bf16)
    grad_columns = jnp.pad(grad_columns, ((0, 0), (0, EXTRA - grad_columns.shape[1])))
    tail = scatter_small(jnp.concatenate([grad_qkv, grad_columns], axis=1))
    shards = tail[:, 3 * width :]
    return (
        output,
        tokens_grad,
        tail[:, : 3 * width],
        shards[:, 0],
        shards[:, 1],
        wide[:, :width],
        shards[:, 2],
        shards[:, 3],
        shards[:, 4],
        wide[:, width : width + hidden],
        shards[:, 8 : 8 + hidden // width].reshape(-1),
        wide[:, width + hidden :].reshape(-1, width),
        shards[:, 5],
        shards[:, 6],
        shards[:, 7],
    )


def solution(mesh):
    dp, ctx = (mesh.shape[a] for a in ("dp", "ctx"))
    fine = Mesh(mesh.devices.reshape(dp // 2, 2, ctx // 2, 2), ALL)
    seqs, ranges, shards = ("y", "core"), CTX, ALL
    token_spec = P(seqs, ranges, None)
    return jax.shard_map(
        body,
        mesh=fine,
        in_specs=(
            token_spec,
            P(shards, None),
            P(shards),
            P(shards),
            P(shards, None),
            P(shards),
            P(shards),
            P(shards),
            P(shards, None),
            P(shards),
            P(shards, None),
            P(shards),
            P(shards),
            P(shards),
            P(seqs, ranges, None, None),
            token_spec,
        ),
        out_specs=(
            token_spec,
            token_spec,
            P(shards, None),
            P(shards),
            P(shards),
            P(shards, None),
            P(shards),
            P(shards),
            P(shards),
            P(shards, None),
            P(shards),
            P(shards, None),
            P(shards),
            P(shards),
            P(shards),
        ),
        check_vma=False,
    )
```

```python
import functools

import jax
import jax.numpy as jnp
from jax import lax
from jax.experimental import pallas as pl
from jax.experimental.pallas import tpu as pltpu
from jax.sharding import Mesh, PartitionSpec as P

H = 12
HD = 64
BLK = 64
RAND = 3
GROUPS = 4
PER_GROUP = 3
SPAN = 3 * 2 * HD
VMEM_BYTES = 56 * 1024 * 1024

bf16 = jnp.bfloat16
f32 = jnp.float32

norm_eps = 1e-06
gelu_root = 0.7978845608028654
gelu_cubic = 0.044715

ALL = ("y", "core", "z", "x")
SEQ = ("y", "core")
CTX = ("z", "x")

VMEM = pl.BlockSpec(memory_space=pltpu.VMEM)
SMEM = pl.BlockSpec(memory_space=pltpu.SMEM)
ANY = pl.BlockSpec(memory_space=pl.ANY)


def call(kernel, name, out_shape, in_specs, out_specs, flops, moved, scratch=(), after=()):
    def ordered(*refs):
        kernel(*refs[len(after) :])

    built = pl.pallas_call(
        ordered,
        out_shape=out_shape,
        in_specs=[ANY] * len(after) + in_specs,
        out_specs=out_specs,
        scratch_shapes=scratch,
        cost_estimate=pl.CostEstimate(flops=flops, bytes_accessed=moved, transcendentals=0),
        compiler_params=pltpu.CompilerParams(vmem_limit_bytes=VMEM_BYTES),
        name=name,
    )
    return functools.partial(built, *after)


def tied(value, *others):
    return lax.optimization_barrier((value,) + others)[0]


def shape(dims, kind):
    return jax.ShapeDtypeStruct(dims, kind)


def contract_rows(left_side, right_side):
    return lax.dot_general(
        left_side, right_side, (((0,), (0,)), ((), ())), preferred_element_type=f32
    )


def contract_cols(left_side, right_side):
    return lax.dot_general(
        left_side, right_side, (((1,), (1,)), ((), ())), preferred_element_type=f32
    )


def plain(left_side, right_side):
    return jnp.dot(left_side, right_side, preferred_element_type=f32)


def heads_of(index, ranks):
    group, rank = index // ranks, index % ranks
    first = PER_GROUP * group + (0 if rank < ranks // 2 else 1)
    return first, PER_GROUP * group + 2


def qkv_kernel(count, owner_ref, *refs):
    x_refs, w_ref, b_ref, out_ref = refs[:count], refs[count], refs[count + 1], refs[count + 2]
    tok = x_refs[0].shape[0]
    for k in range(count):
        rows = plain(x_refs[k][...], w_ref[...]) + b_ref[...]
        at = pl.ds(pl.multiple_of(owner_ref[k] * tok, BLK), tok)
        out_ref[at, :] = rows.astype(bf16)


def qkv_project(owners, pieces, weights, bias):
    count = len(pieces)
    tok, width = pieces[0].shape
    return call(
        functools.partial(qkv_kernel, count),
        "qkv_project",
        shape((count * tok, SPAN), bf16),
        [SMEM] + [VMEM] * (count + 2),
        VMEM,
        2 * count * tok * width * SPAN,
        4 * count * tok * width,
    )(owners, *pieces, weights, bias)


def token_grad_kernel(count, owner_ref, grad_ref, w_ref, *out_refs):
    tok = out_refs[0].shape[0]
    for k in range(count):
        at = pl.ds(pl.multiple_of(owner_ref[k] * tok, BLK), tok)
        out_refs[k][...] = contract_cols(grad_ref[at, :], w_ref[...]).astype(bf16)


def token_grads(count, owners, grads, weights, after):
    tok, width = grads.shape[0] // count, weights.shape[0]
    return call(
        functools.partial(token_grad_kernel, count),
        "token_grads",
        [shape((tok, width), bf16)] * count,
        [SMEM, VMEM, VMEM],
        [VMEM] * count,
        2 * count * tok * width * SPAN,
        4 * count * tok * width,
        after=after,
    )(owners, grads, weights)


def qkv_grad_kernel(count, owner_ref, *refs):
    x_refs, grad_ref, out_ref, bias_ref = refs[:count], refs[count], refs[count + 1], refs[count + 2]
    tok = x_refs[0].shape[0]
    total = None
    for k in range(count):
        at = pl.ds(pl.multiple_of(owner_ref[k] * tok, BLK), tok)
        part = contract_rows(x_refs[k][...], grad_ref[at, :])
        total = part if total is None else total + part
    out_ref[...] = total.astype(bf16)
    bias_ref[...] = jnp.sum(grad_ref[...].astype(f32), axis=0, keepdims=True)


def qkv_grads(owners, pieces, grads, after):
    count = len(pieces)
    tok, width = pieces[0].shape
    return call(
        functools.partial(qkv_grad_kernel, count),
        "qkv_grads",
        [shape((width, SPAN), bf16), shape((1, SPAN), f32)],
        [SMEM] + [VMEM] * (count + 1),
        [VMEM, VMEM],
        2 * count * tok * width * SPAN,
        4 * count * tok * width,
        after=after,
    )(owners, *pieces, grads)


class Plan:
    def __init__(self, count, ranks, blocks):
        self.count, self.ranks, self.blocks = count, ranks, blocks
        self.steps = (ranks // 2, ranks)
        self.owners = (count // self.steps[0], count // self.steps[1])
        self.total = count * blocks
        self.units = (self.owners[0] + self.owners[1]) * blocks
        self.rows = self.total * BLK
        self.chunk = min(self.rows, 2048)

    def at(self, block):
        return pl.ds(pl.multiple_of(block * BLK, BLK), BLK)

    def unit(self, half, turn, inner):
        return (half * self.owners[0] + turn) * self.blocks + inner

    def named(self, half, block, rand_ref):
        ids = [
            jnp.maximum(block - 1, 0),
            block,
            jnp.minimum(block + 1, self.total - 1),
            0,
            self.total - 1,
        ]
        for t in range(RAND):
            ids.append(rand_ref[(block * 2 + half) * RAND + t])
        return ids

    def flops(self, products):
        return 2 * products * self.units * BLK * 128 * 8 * BLK


def only_half(values, half):
    lane = lax.broadcasted_iota(jnp.int32, values.shape, 1)
    return jnp.where((lane < HD) == (half == 0), values, jnp.zeros_like(values))


def attn_forward_kernel(plan, rand_ref, rank_ref, kv_ref, out_ref, lse_ref):
    rank = rank_ref[0]
    out_ref[...] = jnp.zeros_like(out_ref)

    def emit(half, block, unit, attended, lse):
        out_ref[plan.at(block), half * HD : (half + 1) * HD] = attended[
            :, half * HD : (half + 1) * HD
        ].astype(bf16)
        lse_ref[plan.at(unit), :] = jnp.broadcast_to(lse, (BLK, 128))

    def query(half, block):
        return only_half(kv_ref[plan.at(block), 0:128], half) * 0.125

    for half in range(2):
        step = plan.steps[half]
        offset = lax.rem(rank, step) if step > 1 else 0

        def turn_body(turn, carry, half=half, step=step, offset=offset):
            owner = turn * step + offset
            for inner in range(plan.blocks):
                block = owner * plan.blocks + inner
                ids = plan.named(half, block, rand_ref)
                keys = jnp.concatenate([kv_ref[plan.at(i), 128:256] for i in ids], axis=0)
                values = jnp.concatenate([kv_ref[plan.at(i), 256:384] for i in ids], axis=0)
                scores = contract_cols(query(half, block), keys)
                top = jnp.max(scores, axis=-1, keepdims=True)
                grown = jnp.exp(scores - top)
                total = jnp.sum(grown, axis=-1, keepdims=True)
                probs = (grown * (1.0 / total)).astype(bf16)
                attended = plain(probs, values)
                emit(half, block, plan.unit(half, turn, inner), attended, top + jnp.log(total))
            return carry

        lax.fori_loop(0, plan.owners[half], turn_body, 0)

    chunks = [pl.ds(c, plan.chunk) for c in range(0, plan.rows, plan.chunk)]
    for half in range(2):
        step = plan.steps[half]
        for block in (0, plan.total - 1):
            owner = block // plan.blocks

            def whole(half=half, step=step, owner=owner, block=block):
                q = query(half, block)
                scores = [contract_cols(q, kv_ref[c, 128:256]) for c in chunks]
                tops = [jnp.max(s, axis=-1, keepdims=True) for s in scores]
                top = functools.reduce(jnp.maximum, tops)
                grown = [jnp.exp(s - top) for s in scores]
                total = sum(jnp.sum(e, axis=-1, keepdims=True) for e in grown)
                scale = 1.0 / total
                attended = sum(
                    plain((e * scale).astype(bf16), kv_ref[c, 256:384])
                    for e, c in zip(grown, chunks)
                )
                unit = plan.unit(half, owner // step, block % plan.blocks)
                emit(half, block, unit, attended, top + jnp.log(total))

            if step == 1:
                whole()
            else:
                pl.when(lax.rem(rank, step) == owner % step)(whole)


def attn_forward(plan, rand, rank, kv):
    return call(
        functools.partial(attn_forward_kernel, plan),
        "attn_forward",
        (shape((plan.rows, 128), bf16), shape((plan.units * BLK, 128), f32)),
        [SMEM, SMEM, VMEM],
        (VMEM, VMEM),
        plan.flops(2),
        8 * plan.rows * 128,
    )(rand, rank, kv)


def attn_backward_kernel(
    plan, rand_ref, rank_ref, kv_ref, dout_ref, lse_ref, out_ref, sum_ref
):
    rank = rank_ref[0]
    out_ref[:, 0:128] = jnp.zeros((plan.rows, 128), bf16)
    sum_ref[...] = jnp.zeros_like(sum_ref)

    def operands(half, block, unit):
        q = only_half(kv_ref[plan.at(block), 0:128], half) * 0.125
        dout = only_half(dout_ref[plan.at(block), :], half)
        return q, dout, lse_ref[plan.at(unit), :][:, 0:1]

    def emit(half, block, grad_query):
        out_ref[plan.at(block), half * HD : (half + 1) * HD] = (
            grad_query[:, half * HD : (half + 1) * HD] * 0.125
        ).astype(bf16)

    for half in range(2):
        step = plan.steps[half]
        offset = lax.rem(rank, step) if step > 1 else 0

        def turn_body(turn, carry, half=half, step=step, offset=offset):
            owner = turn * step + offset
            found = []
            for inner in range(plan.blocks):
                block = owner * plan.blocks + inner
                ids = plan.named(half, block, rand_ref)
                keys = jnp.concatenate([kv_ref[plan.at(i), 128:256] for i in ids], axis=0)
                values = jnp.concatenate([kv_ref[plan.at(i), 256:384] for i in ids], axis=0)
                q, dout, lse = operands(half, block, plan.unit(half, turn, inner))
                if inner in (0, plan.blocks - 1):
                    edge = (block == 0) | (block == plan.total - 1)
                    dout = dout * jnp.where(edge, 0.0, 1.0).astype(bf16)
                probs = jnp.exp(contract_cols(q, keys) - lse)
                grad_probs = contract_cols(dout, values)
                delta = jnp.sum(probs * grad_probs, axis=-1, keepdims=True)
                grad_scores = (probs * (grad_probs - delta)).astype(bf16)
                emit(half, block, plain(grad_scores, keys))
                grad_keys = contract_rows(grad_scores, q)
                grad_values = contract_rows(probs.astype(bf16), dout)
                found.append((ids, grad_keys, grad_values))
            for ids, grad_keys, grad_values in found:
                for t, i in enumerate(ids):
                    sum_ref[plan.at(i), 0:128] += grad_keys[t * BLK : (t + 1) * BLK]
                    sum_ref[plan.at(i), 128:256] += grad_values[t * BLK : (t + 1) * BLK]
            return carry

        lax.fori_loop(0, plan.owners[half], turn_body, 0)

    chunks = [pl.ds(c, plan.chunk) for c in range(0, plan.rows, plan.chunk)]
    for half in range(2):
        step = plan.steps[half]
        for block in (0, plan.total - 1):
            owner = block // plan.blocks

            def whole(half=half, step=step, owner=owner, block=block):
                unit = plan.unit(half, owner // step, block % plan.blocks)
                q, dout, lse = operands(half, block, unit)
                probs = [jnp.exp(contract_cols(q, kv_ref[c, 128:256]) - lse) for c in chunks]
                grad_probs = [contract_cols(dout, kv_ref[c, 256:384]) for c in chunks]
                delta = sum(
                    jnp.sum(p * g, axis=-1, keepdims=True) for p, g in zip(probs, grad_probs)
                )
                grad_query = jnp.zeros((BLK, 128), f32)
                for p, g, c in zip(probs, grad_probs, chunks):
                    grad_scores = (p * (g - delta)).astype(bf16)
                    sum_ref[c, 0:128] += contract_rows(grad_scores, q)
                    sum_ref[c, 128:256] += contract_rows(p.astype(bf16), dout)
                    grad_query += plain(grad_scores, kv_ref[c, 128:256])
                emit(half, block, grad_query)

            if step == 1:
                whole()
            else:
                pl.when(lax.rem(rank, step) == owner % step)(whole)

    out_ref[:, 128:384] = sum_ref[...].astype(bf16)


def attn_backward(plan, rand, rank, kv, dout, lse, after):
    return call(
        functools.partial(attn_backward_kernel, plan),
        "attn_backward",
        shape((plan.rows, SPAN), bf16),
        [SMEM, SMEM, VMEM, VMEM, VMEM],
        VMEM,
        plan.flops(5),
        16 * plan.rows * 128,
        [pltpu.VMEM((plan.rows, 256), f32)],
        after,
    )(rand, rank, kv, dout, lse)


def reorder_kernel(outer, inner, rows, in_ref, out_ref):
    value = in_ref[...].astype(f32)
    out_ref[...] = jnp.concatenate(
        [
            value[:, (o * inner + i) * rows : (o * inner + i + 1) * rows]
            for i in range(inner)
            for o in range(outer)
        ],
        axis=1,
    ).astype(out_ref.dtype)


def reordered(value, outer, inner):
    rows, cols = value.shape
    run = cols // (outer * inner)
    if run < 8:
        return value.reshape(rows, outer, inner, run).transpose(0, 2, 1, 3).reshape(rows, cols)
    return call(
        functools.partial(reorder_kernel, outer, inner, run),
        "reorder",
        shape((rows, cols), value.dtype),
        [VMEM],
        VMEM,
        rows * cols,
        4 * rows * cols,
    )(value)


def normalized(values):
    center = values - jnp.mean(values, axis=-1, keepdims=True)
    spread = jnp.mean(center * center, axis=-1, keepdims=True)
    scale = lax.rsqrt(spread + norm_eps)
    return center * scale, scale


def normalized_grad(normal, scale, grad):
    return scale * (
        grad
        - jnp.mean(grad, axis=-1, keepdims=True)
        - normal * jnp.mean(grad * normal, axis=-1, keepdims=True)
    )


def column_sum(values):
    return jnp.sum(values.astype(f32), axis=0, keepdims=True)


def middle_kernel(
    ranks,
    back_ref,
    tok_ref,
    cot_ref,
    vec_ref,
    pack_ref,
    output_ref,
    resid_ref,
    dout_ref,
    attn_ref,
    mid_ref,
    act_ref,
    down_ref,
    pre_ref,
    branch_ref,
    sums_ref,
    out_w,
    up_w,
    down_w,
    slope_ref,
    sems,
):
    count = back_ref.shape[0]
    width = tok_ref.shape[1]
    turns = up_w.shape[1] // width
    half_ranks = ranks // 2

    copies = [pltpu.make_async_copy(pack_ref.at[:, pl.ds(0, width)], out_w, sems.at[0])]
    for t in range(turns):
        cols = pl.ds(t * width, width)
        copies.append(
            pltpu.make_async_copy(
                pack_ref.at[:, pl.ds((1 + t) * width, width)], up_w.at[:, cols], sems.at[1 + t]
            )
        )
        copies.append(
            pltpu.make_async_copy(
                pack_ref.at[:, pl.ds((1 + turns + t) * width, width)],
                down_w.at[t],
                sems.at[1 + turns + t],
            )
        )
    for copy in copies:
        copy.start()

    for g in range(GROUPS):
        own = [back_ref[g * ranks + r][:, 0:HD] for r in range(ranks)]
        shared = [back_ref[g * ranks + r][:, HD : 2 * HD] for r in range(ranks)]
        trio = [sum(own[1:half_ranks], own[0]), sum(own[half_ranks + 1 :], own[half_ranks])]
        trio.append(sum(shared[1:], shared[0]))
        attn_ref[:, g * PER_GROUP * HD : (g + 1) * PER_GROUP * HD] = jnp.concatenate(trio, axis=1)

    out_bias, attn_gain, attn_shift, down_bias, ffn_gain, ffn_shift = (
        vec_ref[k : k + 1, :] for k in range(2, 8)
    )
    copies[0].wait()
    branch = plain(attn_ref[...], out_w[...]) + out_bias
    normal, scale = normalized(tok_ref[...].astype(f32) + branch)
    mid = normal * attn_gain + attn_shift
    mid_low = mid.astype(bf16)
    mid_ref[...] = mid_low
    final = mid + down_bias
    for t in range(turns):
        cols = slice(t * width, (t + 1) * width)
        copies[1 + 2 * t].wait()
        pre = plain(mid_low, up_w[:, cols]) + vec_ref[8 + t : 9 + t, :]
        square = pre * pre
        bend = jnp.tanh(gelu_root * (pre + gelu_cubic * pre * square))
        rise = 0.5 * (1.0 + bend)
        slope_ref[:, cols] = rise + 0.5 * pre * (1.0 - bend * bend) * (
            gelu_root * (1.0 + 3.0 * gelu_cubic * square)
        )
        act = (pre * rise).astype(bf16)
        act_ref[:, cols] = act
        copies[2 + 2 * t].wait()
        final = final + plain(act, down_w[t])
    normal_two, scale_two = normalized(final)
    output_ref[...] = (normal_two * ffn_gain + ffn_shift).astype(bf16)
    cot = cot_ref[...].astype(f32)
    sums_ref[4:5, :] = column_sum(cot * normal_two)
    sums_ref[5:6, :] = column_sum(cot)
    grad_final = normalized_grad(normal_two, scale_two, cot * ffn_gain)
    down_low = grad_final.astype(bf16)
    down_ref[...] = down_low
    sums_ref[3:4, :] = column_sum(down_low)
    grad_mid = grad_final
    for t in range(turns):
        cols = slice(t * width, (t + 1) * width)
        grad_pre = (contract_cols(down_low, down_w[t]) * slope_ref[:, cols]).astype(bf16)
        pre_ref[:, cols] = grad_pre
        sums_ref[6 + t : 7 + t, :] = column_sum(grad_pre)
        grad_mid = grad_mid + contract_cols(grad_pre, up_w[:, cols])
    sums_ref[1:2, :] = column_sum(grad_mid * normal)
    sums_ref[2:3, :] = column_sum(grad_mid)
    resid = normalized_grad(normal, scale, grad_mid * attn_gain)
    resid_ref[...] = resid
    branch_low = resid.astype(bf16)
    branch_ref[...] = branch_low
    sums_ref[0:1, :] = column_sum(branch_low)
    grad_attn = contract_cols(branch_low, out_w[...]).astype(bf16)
    for j in range(count):
        first, shared = heads_of(j, ranks)
        dout_ref[j] = jnp.concatenate(
            [
                grad_attn[:, first * HD : (first + 1) * HD],
                grad_attn[:, shared * HD : (shared + 1) * HD],
            ],
            axis=1,
        )


def middle(ranks, back, tokens, cotangent, vectors, packed):
    count, (tok, width) = back.shape[0], tokens.shape
    turns = vectors.shape[0] - 8
    hidden = turns * width
    return call(
        functools.partial(middle_kernel, ranks),
        "middle",
        [
            shape((tok, width), bf16),
            shape((tok, width), f32),
            shape((count, tok, 128), bf16),
            shape((tok, width), bf16),
            shape((tok, width), bf16),
            shape((tok, hidden), bf16),
            shape((tok, width), bf16),
            shape((tok, hidden), bf16),
            shape((tok, width), bf16),
            shape((6 + turns, width), f32),
        ],
        [VMEM] * 4 + [ANY],
        [VMEM] * 10,
        4 * tok * width * (width + 2 * hidden),
        2 * width * (width + 2 * hidden),
        [
            pltpu.VMEM((width, width), bf16),
            pltpu.VMEM((width, hidden), bf16),
            pltpu.VMEM((turns, width, width), bf16),
            pltpu.VMEM((tok, hidden), f32),
            pltpu.SemaphoreType.DMA((1 + 2 * turns,)),
        ],
    )(back, tokens, cotangent, vectors, packed)


def weight_grad_kernel(lead, waits, *refs):
    where_ref, left_ref, right_ref, keep_ref, send_ref, total_ref = refs[waits:]
    ny = keep_ref.shape[0]
    rows = total_ref.shape[0] // (2 * ny)
    total_ref[...] = contract_rows(left_ref[...], right_ref[...])
    mine, core = where_ref[0], where_ref[1]
    for d in range(ny):
        base = lax.rem(mine + d, ny) * 2
        for ref, c in ((keep_ref, core), (send_ref, 1 - core)):
            part = total_ref[pl.ds(pl.multiple_of((base + c) * rows, 16), rows), :].astype(bf16)
            if lead:
                ref[d, 0] = part
            else:
                ref[d] = part


def weight_grad(where, left, right, ny, lead, after=()):
    tok, width = left.shape[0], right.shape[1] if lead else left.shape[1]
    turns = (left.shape[1] if lead else right.shape[1]) // width
    rows = width // (2 * ny)
    if lead:
        dims, block, index = (ny, turns, rows, width), (ny, 1, rows, width), lambda t: (0, t, 0, 0)
    else:
        dims, block, index = (ny, rows, turns * width), (ny, rows, width), lambda t: (0, 0, t)
    tiled = pl.BlockSpec((tok, width), lambda t: (0, t))
    fixed = pl.BlockSpec((tok, width), lambda t: (0, 0))
    return pl.pallas_call(
        functools.partial(weight_grad_kernel, lead, len(after)),
        grid=(turns,),
        out_shape=[shape(dims, bf16)] * 2,
        in_specs=[ANY] * len(after) + [SMEM, tiled if lead else fixed, fixed if lead else tiled],
        out_specs=[pl.BlockSpec(block, index)] * 2,
        scratch_shapes=[pltpu.VMEM((width, width), f32)],
        cost_estimate=pl.CostEstimate(
            flops=2 * tok * width * width * turns,
            bytes_accessed=2 * width * width * turns,
            transcendentals=0,
        ),
        compiler_params=pltpu.CompilerParams(vmem_limit_bytes=VMEM_BYTES),
        name="weight_grad",
    )(*after, where, left, right)


def swap(value, axis):
    return lax.all_to_all(value, axis, split_axis=0, concat_axis=0, tiled=True)


def shifted(value, axis, by):
    size = lax.axis_size(axis)
    return lax.ppermute(value, axis, [(i, (i + by) % size) for i in range(size)])


def far_first(size):
    return sorted(range(1, size), key=lambda d: -min(d, size - d))


def picked(value, axis, dim):
    size, here = lax.axis_size(axis), lax.axis_index(axis)

    def part(d):
        return lax.dynamic_index_in_dim(
            value, lax.rem(here + d, size), dim, keepdims=False
        ).astype(f32)

    return part


def core_stage(keep, send):
    nz, nx = lax.axis_size("z"), lax.axis_size("x")
    value = keep.astype(f32) + shifted(send, "core", 1).astype(f32)
    lead, (rows, cols) = value.shape[:-2], value.shape[-2:]
    return value.reshape(lead + (nz, nx, rows // (nz * nx), cols))


def along_y(value):
    return lambda d: value[d]


def along_x(value):
    return picked(value, "x", value.ndim - 3)


def along_z(value):
    return picked(value, "z", value.ndim - 3)


def ends(parts, size):
    return parts(0), [parts(d).astype(bf16) for d in far_first(size)]


def received(kept, sent, axis):
    got = [shifted(part, axis, d) for d, part in zip(far_first(len(sent) + 1), sent)]
    return got, functools.reduce(lambda total, part: total + part.astype(f32), got, kept)


def summed(parts, axis):
    return received(*ends(parts, lax.axis_size(axis)), axis)[1]


def body(
    tokens,
    qkv_weight,
    query_bias,
    value_bias,
    out_weight,
    out_bias,
    attn_gain,
    attn_shift,
    up_weight,
    up_bias,
    down_weight,
    down_bias,
    ffn_gain,
    ffn_shift,
    random_blocks,
    cotangent,
):
    ny, nc, nz, nx = (lax.axis_size(a) for a in ALL)
    count, devices = nz * nx, ny * nc * nz * nx
    ranks = count // GROUPS
    half_ranks = ranks // 2
    _, tok, width = tokens.shape
    blocks = tok // BLK
    plan = Plan(count, ranks, blocks)
    z, x = lax.axis_index("z"), lax.axis_index("x")
    ctx_index = z * nx + x
    rank = lax.rem(ctx_index, ranks).astype(jnp.int32).reshape(1)
    where = jnp.stack([lax.axis_index("y"), lax.axis_index("core")]).astype(jnp.int32)
    rows = qkv_weight.shape[0]
    hidden = up_weight.shape[1]
    turns = hidden // width
    flat_tokens = tokens.reshape(tok, width)

    up_shard = reordered(up_weight, devices, turns)
    down_shard = down_weight.reshape(turns, rows, width).transpose(1, 0, 2)
    packed = jnp.concatenate(
        [out_weight, up_shard, down_shard.reshape(rows, hidden)], axis=1
    )
    packed = lax.all_gather(packed, ALL, axis=0, tiled=True)

    def by_index(values):
        grouped = values.reshape(values.shape[:-2] + (GROUPS, PER_GROUP, values.shape[-1]))
        pairs = [
            jnp.stack([grouped[..., 0 if r < half_ranks else 1, :], grouped[..., 2, :]], axis=-2)
            for r in range(ranks)
        ]
        return jnp.moveaxis(jnp.stack(pairs, axis=-3), (-4, -3), (0, 1)).reshape(
            (count,) + values.shape[:-2] + (2, values.shape[-1])
        )

    weight_rows = by_index(qkv_weight.reshape(rows, 3, H, HD)).reshape(count, rows, SPAN)
    picks = by_index(random_blocks[0].astype(bf16)).reshape(count, 1, -1)
    entries = picks.shape[2]
    small = jnp.concatenate(
        [
            query_bias,
            value_bias,
            out_bias,
            attn_gain,
            attn_shift,
            down_bias,
            ffn_gain,
            ffn_shift,
            up_bias,
        ]
    )
    many = small.shape[0] // rows
    extra = -(-(rows + 2) // 8) * 8
    sent = jnp.concatenate(
        [
            weight_rows,
            jnp.pad(picks, ((0, 0), (0, 0), (0, SPAN - entries))),
            jnp.broadcast_to(jnp.pad(small, (0, SPAN - small.shape[0])), (count, 1, SPAN)),
            jnp.zeros((count, extra - rows - 2, SPAN), bf16),
        ],
        axis=1,
    )
    near = [d for d in range(1, nz) if min(d, nz - d) == 1]
    held = {0: flat_tokens}
    over = {}
    for e in range(1, nx):
        over[0, e] = shifted(flat_tokens, "x", e)
    for d in near:
        held[d] = shifted(flat_tokens, "z", d)
    line = swap(sent, CTX)
    for d in far_first(nz):
        if d not in held:
            held[d] = shifted(tied(flat_tokens, line), "z", d)
    shifts = [0] + near + [d for d in far_first(nz) if d not in near]
    order = [(d, e) for e in range(nx) for d in shifts]
    pieces = []
    for d, e in order:
        if e and d:
            over[d, e] = shifted(held[d], "x", e)
        pieces.append(over[d, e] if e else held[d])
    owners = jnp.stack(
        [lax.rem(z + nz - d, nz) * nx + lax.rem(x + nx - e, nx) for d, e in order]
    ).astype(jnp.int32)
    targets = jnp.stack(
        [lax.rem(z + d, nz) * nx + lax.rem(x + e, nx) for d, e in order]
    ).astype(jnp.int32)
    rand = line[:, rows, :entries].astype(jnp.int32).reshape(-1)
    seqs = ny * nc
    full = swap(
        tied(jnp.broadcast_to(line[None], (seqs,) + line.shape), over[0, 1], *(held[d] for d in near)), SEQ
    )
    columns = full[:, :, :rows].reshape(width, SPAN)
    vectors = full[:, :, rows + 1, : small.shape[0]].astype(f32)
    vectors = vectors.reshape(devices, many, rows).transpose(1, 0, 2).reshape(many, width)
    bias_table = by_index(
        jnp.stack([vectors[0], jnp.zeros_like(vectors[0]), vectors[1]]).reshape(3, H, HD)
    ).reshape(count, 1, SPAN)
    bias = lax.dynamic_index_in_dim(bias_table, ctx_index, 0, keepdims=False)

    kv = qkv_project(owners, pieces, columns, bias)
    attended, lse = attn_forward(plan, rand, rank, kv)
    back = swap(attended.reshape(count, tok, 128), CTX)

    output, resid, dout, attn_low, mid_low, act_low, down_low, pre_low, branch_low, sums = middle(
        ranks, back, flat_tokens, cotangent.reshape(tok, width), vectors, packed
    )
    dout = swap(dout, CTX).reshape(plan.rows, 128)
    down_kept, down_sent = ends(along_y(core_stage(*weight_grad(where, act_low, down_low, ny, True))), ny)
    up_kept, up_sent = ends(along_x(core_stage(*weight_grad(where, mid_low, pre_low, ny, False))), nx)
    out_kept, out_sent = ends(along_y(core_stage(*weight_grad(where, attn_low, branch_low, ny, False))), ny)

    grads = attn_backward(plan, rand, rank, kv, dout, lse, down_sent + up_sent + out_sent)
    down_got, down_sum = received(tied(down_kept, grads), down_sent, "y")
    up_got, up_sum = received(tied(up_kept, grads), up_sent, "x")
    out_got, out_sum = received(tied(out_kept, grads), out_sent, "y")
    terms = token_grads(count, targets, grads, columns, down_got + up_got + out_got)

    def over_x(d, *others):
        k = shifts.index(d)
        return functools.reduce(
            lambda total, e: total + shifted(tied(terms[e * nz + k], *others), "x", e).astype(f32),
            range(1, nx),
            terms[k].astype(f32),
        )

    line_order = far_first(nz)
    line_sums = [over_x(d).astype(bf16) for d in line_order]
    line_own = over_x(0, line_sums[0])
    line_got = [shifted(part, "z", d) for d, part in zip(line_order, line_sums)]
    total = functools.reduce(lambda acc, part: acc + part.astype(f32), line_got, resid + line_own)
    tokens_grad = total.reshape(1, tok, width)
    column_grads, bias_grads = qkv_grads(owners, pieces, grads, line_sums[:1])
    up_part = summed(along_y(tied(up_sum, terms[0])), "y")
    down_part = summed(along_x(tied(down_sum, line_sums[1])), "x")
    out_part = summed(along_x(tied(out_sum, line_sums[-1])), "x")

    listed = sums.shape[0]
    vector_sums = sums.reshape(listed, ny, nc, count, rows).transpose(1, 2, 3, 0, 4)
    vector_sums = vector_sums.reshape(ny, nc, count, 1, listed * rows).astype(bf16)
    table = jnp.concatenate(
        [
            column_grads.reshape(ny, nc, count, rows, SPAN),
            jnp.broadcast_to(bias_grads.astype(bf16), (ny, nc, count, 1, SPAN)),
            jnp.pad(vector_sums, ((0, 0),) * 4 + ((0, SPAN - listed * rows),)),
            jnp.zeros((ny, nc, count, extra - rows - 2, SPAN), bf16),
        ],
        axis=3,
    )
    table = summed(picked(table, "core", 1), "core")
    table = summed(picked(table, "y", 0), "y")
    table = swap(table.astype(bf16), CTX).astype(f32)[:, : rows + 2]
    shards = jnp.sum(table[:, rows + 1, : listed * rows], axis=0).reshape(listed, rows)
    table = table[:, : rows + 1].reshape(GROUPS, ranks, rows + 1, 3, 2, HD)
    table = jnp.stack(
        [
            jnp.sum(table[:, :half_ranks, :, :, 0], axis=1),
            jnp.sum(table[:, half_ranks:, :, :, 0], axis=1),
            jnp.sum(table[:, :, :, :, 1], axis=1),
        ],
        axis=1,
    )
    table = table.transpose(2, 3, 0, 1, 4).reshape(rows + 1, 3, width)
    qkv_grad = table[:rows].reshape(rows, 3 * width)
    device = (lax.axis_index("y") * nc + lax.axis_index("core")) * count + ctx_index
    query_bias_grad = lax.dynamic_slice_in_dim(table[rows, 0], device * rows, rows)
    value_bias_grad = lax.dynamic_slice_in_dim(table[rows, 2], device * rows, rows)

    up_grad = summed(along_z(up_part), "z")
    up_grad = reordered(up_grad, turns, devices)
    down_grad = summed(along_z(tied(down_part, line_got[0])), "z").reshape(turns * rows, width)
    out_grad = summed(along_z(tied(out_part, line_got[0])), "z")

    return (
        output.reshape(1, tok, width),
        tokens_grad,
        qkv_grad,
        query_bias_grad,
        value_bias_grad,
        out_grad,
        shards[0],
        shards[1],
        shards[2],
        up_grad,
        shards[6:].reshape(-1),
        down_grad,
        shards[3],
        shards[4],
        shards[5],
    )


def solution(mesh):
    dp, ctx = (mesh.shape[a] for a in ("dp", "ctx"))
    fine = Mesh(mesh.devices.reshape(dp // 2, 2, ctx // 2, 2), ALL)
    token_spec = P(SEQ, CTX, None)
    matrix, vector = P(ALL, None), P(ALL)
    return jax.shard_map(
        body,
        mesh=fine,
        in_specs=(
            token_spec,
            matrix,
            vector,
            vector,
            matrix,
            vector,
            vector,
            vector,
            matrix,
            vector,
            matrix,
            vector,
            vector,
            vector,
            P(SEQ, CTX, None, None),
            token_spec,
        ),
        out_specs=(
            token_spec,
            token_spec,
            matrix,
            vector,
            vector,
            matrix,
            vector,
            vector,
            vector,
            matrix,
            vector,
            matrix,
            vector,
            vector,
            vector,
        ),
        check_vma=False,
    )
```

```python
import functools

import jax
import jax.numpy as jnp
from jax import lax
from jax.experimental import pallas as pl
from jax.experimental.pallas import tpu as pltpu
from jax.sharding import Mesh, PartitionSpec as P

H = 12
HD = 64
BLK = 64
RAND = 3
GROUPS = 4
PER_GROUP = 3
SPAN = 3 * 2 * HD
VMEM_BYTES = 56 * 1024 * 1024

bf16 = jnp.bfloat16
f32 = jnp.float32

norm_eps = 1e-06
gelu_root = 0.7978845608028654
gelu_cubic = 0.044715

ALL = ("y", "core", "z", "x")
SEQ = ("y", "core")
CTX = ("z", "x")

VMEM = pl.BlockSpec(memory_space=pltpu.VMEM)
SMEM = pl.BlockSpec(memory_space=pltpu.SMEM)
ANY = pl.BlockSpec(memory_space=pl.ANY)


def call(kernel, name, out_shape, in_specs, out_specs, flops, moved, scratch=(), after=()):
    def ordered(*refs):
        kernel(*refs[len(after) :])

    built = pl.pallas_call(
        ordered,
        out_shape=out_shape,
        in_specs=[ANY] * len(after) + in_specs,
        out_specs=out_specs,
        scratch_shapes=scratch,
        cost_estimate=pl.CostEstimate(flops=flops, bytes_accessed=moved, transcendentals=0),
        compiler_params=pltpu.CompilerParams(vmem_limit_bytes=VMEM_BYTES),
        name=name,
    )
    return functools.partial(built, *after)


def tied(value, *others):
    return lax.optimization_barrier((value,) + others)[0]


def shape(dims, kind):
    return jax.ShapeDtypeStruct(dims, kind)


def contract_rows(left_side, right_side):
    return lax.dot_general(
        left_side, right_side, (((0,), (0,)), ((), ())), preferred_element_type=f32
    )


def contract_cols(left_side, right_side):
    return lax.dot_general(
        left_side, right_side, (((1,), (1,)), ((), ())), preferred_element_type=f32
    )


def plain(left_side, right_side):
    return jnp.dot(left_side, right_side, preferred_element_type=f32)


def heads_of(index, ranks):
    group, rank = index // ranks, index % ranks
    first = PER_GROUP * group + (0 if rank < ranks // 2 else 1)
    return first, PER_GROUP * group + 2


def qkv_kernel(count, owner_ref, *refs):
    x_refs, w_ref, b_ref, out_ref = refs[:count], refs[count], refs[count + 1], refs[count + 2]
    tok = x_refs[0].shape[0]
    for k in range(count):
        rows = plain(x_refs[k][...], w_ref[...]) + b_ref[...]
        at = pl.ds(pl.multiple_of(owner_ref[k] * tok, BLK), tok)
        out_ref[at, :] = rows.astype(bf16)


def qkv_project(owners, pieces, weights, bias):
    count = len(pieces)
    tok, width = pieces[0].shape
    return call(
        functools.partial(qkv_kernel, count),
        "qkv_project",
        shape((count * tok, SPAN), bf16),
        [SMEM] + [VMEM] * (count + 2),
        VMEM,
        2 * count * tok * width * SPAN,
        4 * count * tok * width,
    )(owners, *pieces, weights, bias)


def token_grad_kernel(count, owner_ref, grad_ref, w_ref, *out_refs):
    tok = out_refs[0].shape[0]
    for k in range(count):
        at = pl.ds(pl.multiple_of(owner_ref[k] * tok, BLK), tok)
        out_refs[k][...] = contract_cols(grad_ref[at, :], w_ref[...]).astype(bf16)


def token_grads(count, owners, grads, weights, after):
    tok, width = grads.shape[0] // count, weights.shape[0]
    return call(
        functools.partial(token_grad_kernel, count),
        "token_grads",
        [shape((tok, width), bf16)] * count,
        [SMEM, VMEM, VMEM],
        [VMEM] * count,
        2 * count * tok * width * SPAN,
        4 * count * tok * width,
        after=after,
    )(owners, grads, weights)


def add_kernel(counts, *refs):
    at = sum(counts)
    for k, n in enumerate(counts):
        parts = [ref[...].astype(f32) for ref in refs[sum(counts[:k]) : sum(counts[: k + 1])]]
        refs[at + k][...] = functools.reduce(jnp.add, parts).astype(bf16)


def added(groups, after):
    counts = [len(group) for group in groups]
    size = groups[0][0].size
    return call(
        functools.partial(add_kernel, counts),
        "added",
        [shape(group[0].shape, bf16) for group in groups],
        [VMEM] * sum(counts),
        [VMEM] * len(groups),
        size * sum(counts),
        2 * size * sum(counts),
        after=after,
    )(*[part for group in groups for part in group])


def qkv_grad_kernel(count, owner_ref, *refs):
    x_refs, grad_ref, out_ref, bias_ref = refs[:count], refs[count], refs[count + 1], refs[count + 2]
    tok = x_refs[0].shape[0]
    total = None
    for k in range(count):
        at = pl.ds(pl.multiple_of(owner_ref[k] * tok, BLK), tok)
        part = contract_rows(x_refs[k][...], grad_ref[at, :])
        total = part if total is None else total + part
    out_ref[...] = total.astype(bf16)
    bias_ref[...] = jnp.sum(grad_ref[...].astype(f32), axis=0, keepdims=True)


def qkv_grads(owners, pieces, grads, after):
    count = len(pieces)
    tok, width = pieces[0].shape
    return call(
        functools.partial(qkv_grad_kernel, count),
        "qkv_grads",
        [shape((width, SPAN), bf16), shape((1, SPAN), f32)],
        [SMEM] + [VMEM] * (count + 1),
        [VMEM, VMEM],
        2 * count * tok * width * SPAN,
        4 * count * tok * width,
        after=after,
    )(owners, *pieces, grads)


class Plan:
    def __init__(self, count, ranks, blocks):
        self.count, self.ranks, self.blocks = count, ranks, blocks
        self.steps = (ranks // 2, ranks)
        self.owners = (count // self.steps[0], count // self.steps[1])
        self.total = count * blocks
        self.units = (self.owners[0] + self.owners[1]) * blocks
        self.rows = self.total * BLK
        self.chunk = min(self.rows, 2048)

    def at(self, block):
        return pl.ds(pl.multiple_of(block * BLK, BLK), BLK)

    def unit(self, half, turn, inner):
        return (half * self.owners[0] + turn) * self.blocks + inner

    def named(self, half, block, rand_ref):
        ids = [
            jnp.maximum(block - 1, 0),
            block,
            jnp.minimum(block + 1, self.total - 1),
            0,
            self.total - 1,
        ]
        for t in range(RAND):
            ids.append(rand_ref[(block * 2 + half) * RAND + t])
        return ids

    def flops(self, products):
        return 2 * products * self.units * BLK * 128 * 8 * BLK


def only_half(values, half):
    lane = lax.broadcasted_iota(jnp.int32, values.shape, 1)
    return jnp.where((lane < HD) == (half == 0), values, jnp.zeros_like(values))


def attn_forward_kernel(plan, rand_ref, rank_ref, kv_ref, out_ref, lse_ref):
    rank = rank_ref[0]
    out_ref[...] = jnp.zeros_like(out_ref)

    def emit(half, block, unit, attended, lse):
        out_ref[plan.at(block), half * HD : (half + 1) * HD] = attended[
            :, half * HD : (half + 1) * HD
        ].astype(bf16)
        lse_ref[plan.at(unit), :] = jnp.broadcast_to(lse, (BLK, 128))

    def query(half, block):
        return only_half(kv_ref[plan.at(block), 0:128], half) * 0.125

    for half in range(2):
        step = plan.steps[half]
        offset = lax.rem(rank, step) if step > 1 else 0

        def turn_body(turn, carry, half=half, step=step, offset=offset):
            inners = range(2 * plan.blocks)
            listed = [
                ((2 * turn + i // plan.blocks) * step + offset) * plan.blocks + i % plan.blocks
                for i in inners
            ]
            named = [plan.named(half, block, rand_ref) for block in listed]
            scores = []
            for inner, ids in zip(inners, named):
                keys = jnp.concatenate([kv_ref[plan.at(i), 128:256] for i in ids], axis=0)
                scores.append(contract_cols(query(half, listed[inner]), keys))
            probs, lses = [], []
            for part in scores:
                top = jnp.max(part, axis=-1, keepdims=True)
                grown = jnp.exp(part - top)
                total = jnp.sum(grown, axis=-1, keepdims=True)
                probs.append((grown * (1.0 / total)).astype(bf16))
                lses.append(top + jnp.log(total))
            for inner, ids in zip(inners, named):
                values = jnp.concatenate([kv_ref[plan.at(i), 256:384] for i in ids], axis=0)
                attended = plain(probs[inner], values)
                block = listed[inner]
                emit(half, block, plan.unit(half, 2 * turn, inner), attended, lses[inner])
            return carry

        lax.fori_loop(0, plan.owners[half] // 2, turn_body, 0)

    chunks = [pl.ds(c, plan.chunk) for c in range(0, plan.rows, plan.chunk)]
    for half in range(2):
        step = plan.steps[half]
        for block in (0, plan.total - 1):
            owner = block // plan.blocks

            def whole(half=half, step=step, owner=owner, block=block):
                q = query(half, block)
                scores = [contract_cols(q, kv_ref[c, 128:256]) for c in chunks]
                tops = [jnp.max(s, axis=-1, keepdims=True) for s in scores]
                top = functools.reduce(jnp.maximum, tops)
                grown = [jnp.exp(s - top) for s in scores]
                total = sum(jnp.sum(e, axis=-1, keepdims=True) for e in grown)
                scale = 1.0 / total
                attended = sum(
                    plain((e * scale).astype(bf16), kv_ref[c, 256:384])
                    for e, c in zip(grown, chunks)
                )
                unit = plan.unit(half, owner // step, block % plan.blocks)
                emit(half, block, unit, attended, top + jnp.log(total))

            if step == 1:
                whole()
            else:
                pl.when(lax.rem(rank, step) == owner % step)(whole)


def attn_forward(plan, rand, rank, kv):
    return call(
        functools.partial(attn_forward_kernel, plan),
        "attn_forward",
        (shape((plan.rows, 128), bf16), shape((plan.units * BLK, 128), f32)),
        [SMEM, SMEM, VMEM],
        (VMEM, VMEM),
        plan.flops(2),
        8 * plan.rows * 128,
    )(rand, rank, kv)


def attn_backward_kernel(
    plan, rand_ref, rank_ref, kv_ref, dout_ref, lse_ref, out_ref, sum_ref
):
    rank = rank_ref[0]
    out_ref[:, 0:128] = jnp.zeros((plan.rows, 128), bf16)
    sum_ref[...] = jnp.zeros_like(sum_ref)

    def operands(half, block, unit):
        q = only_half(kv_ref[plan.at(block), 0:128], half) * 0.125
        dout = only_half(dout_ref[plan.at(block), :], half)
        return q, dout, lse_ref[plan.at(unit), :][:, 0:1]

    def emit(half, block, grad_query):
        out_ref[plan.at(block), half * HD : (half + 1) * HD] = (
            grad_query[:, half * HD : (half + 1) * HD] * 0.125
        ).astype(bf16)

    for half in range(2):
        step = plan.steps[half]
        offset = lax.rem(rank, step) if step > 1 else 0

        def turn_body(turn, carry, half=half, step=step, offset=offset):
            inners = range(2 * plan.blocks)
            listed = [
                ((2 * turn + i // plan.blocks) * step + offset) * plan.blocks + i % plan.blocks
                for i in inners
            ]
            named = [plan.named(half, block, rand_ref) for block in listed]
            given, scores, grad_probs = [], [], []
            for inner, ids in zip(inners, named):
                block = listed[inner]
                q, dout, lse = operands(half, block, plan.unit(half, 2 * turn, inner))
                if inner % plan.blocks in (0, plan.blocks - 1):
                    edge = (block == 0) | (block == plan.total - 1)
                    dout = dout * jnp.where(edge, 0.0, 1.0).astype(bf16)
                given.append((q, dout, lse))
                keys = jnp.concatenate([kv_ref[plan.at(i), 128:256] for i in ids], axis=0)
                scores.append(contract_cols(q, keys))
            for inner, ids in zip(inners, named):
                values = jnp.concatenate([kv_ref[plan.at(i), 256:384] for i in ids], axis=0)
                grad_probs.append(contract_cols(given[inner][1], values))
            low_probs, grad_scores = [], []
            for inner in inners:
                probs = jnp.exp(scores[inner] - given[inner][2])
                delta = jnp.sum(probs * grad_probs[inner], axis=-1, keepdims=True)
                grad_scores.append((probs * (grad_probs[inner] - delta)).astype(bf16))
                low_probs.append(probs.astype(bf16))
            for inner, ids in zip(inners, named):
                keys = jnp.concatenate([kv_ref[plan.at(i), 128:256] for i in ids], axis=0)
                emit(half, listed[inner], plain(grad_scores[inner], keys))
            grad_keys = [contract_rows(grad_scores[i], given[i][0]) for i in inners]
            grad_values = [contract_rows(low_probs[i], given[i][1]) for i in inners]
            for inner, ids in zip(inners, named):
                for t, i in enumerate(ids):
                    sum_ref[plan.at(i), 0:128] += grad_keys[inner][t * BLK : (t + 1) * BLK]
                    sum_ref[plan.at(i), 128:256] += grad_values[inner][t * BLK : (t + 1) * BLK]
            return carry

        lax.fori_loop(0, plan.owners[half] // 2, turn_body, 0)

    chunks = [pl.ds(c, plan.chunk) for c in range(0, plan.rows, plan.chunk)]
    for half in range(2):
        step = plan.steps[half]
        for block in (0, plan.total - 1):
            owner = block // plan.blocks

            def whole(half=half, step=step, owner=owner, block=block):
                unit = plan.unit(half, owner // step, block % plan.blocks)
                q, dout, lse = operands(half, block, unit)
                probs = [jnp.exp(contract_cols(q, kv_ref[c, 128:256]) - lse) for c in chunks]
                grad_probs = [contract_cols(dout, kv_ref[c, 256:384]) for c in chunks]
                delta = sum(
                    jnp.sum(p * g, axis=-1, keepdims=True) for p, g in zip(probs, grad_probs)
                )
                grad_query = jnp.zeros((BLK, 128), f32)
                for p, g, c in zip(probs, grad_probs, chunks):
                    grad_scores = (p * (g - delta)).astype(bf16)
                    sum_ref[c, 0:128] += contract_rows(grad_scores, q)
                    sum_ref[c, 128:256] += contract_rows(p.astype(bf16), dout)
                    grad_query += plain(grad_scores, kv_ref[c, 128:256])
                emit(half, block, grad_query)

            if step == 1:
                whole()
            else:
                pl.when(lax.rem(rank, step) == owner % step)(whole)

    out_ref[:, 128:384] = sum_ref[...].astype(bf16)


def attn_backward(plan, rand, rank, kv, dout, lse, after):
    return call(
        functools.partial(attn_backward_kernel, plan),
        "attn_backward",
        shape((plan.rows, SPAN), bf16),
        [SMEM, SMEM, VMEM, VMEM, VMEM],
        VMEM,
        plan.flops(5),
        16 * plan.rows * 128,
        [pltpu.VMEM((plan.rows, 256), f32)],
        after,
    )(rand, rank, kv, dout, lse)


def reorder_kernel(outer, inner, rows, in_ref, out_ref):
    value = in_ref[...].astype(f32)
    out_ref[...] = jnp.concatenate(
        [
            value[:, (o * inner + i) * rows : (o * inner + i + 1) * rows]
            for i in range(inner)
            for o in range(outer)
        ],
        axis=1,
    ).astype(out_ref.dtype)


def reordered(value, outer, inner):
    rows, cols = value.shape
    run = cols // (outer * inner)
    if run < 8:
        return value.reshape(rows, outer, inner, run).transpose(0, 2, 1, 3).reshape(rows, cols)
    return call(
        functools.partial(reorder_kernel, outer, inner, run),
        "reorder",
        shape((rows, cols), value.dtype),
        [VMEM],
        VMEM,
        rows * cols,
        4 * rows * cols,
    )(value)


def normalized(values):
    center = values - jnp.mean(values, axis=-1, keepdims=True)
    spread = jnp.mean(center * center, axis=-1, keepdims=True)
    scale = lax.rsqrt(spread + norm_eps)
    return center * scale, scale


def normalized_grad(normal, scale, grad):
    return scale * (
        grad
        - jnp.mean(grad, axis=-1, keepdims=True)
        - normal * jnp.mean(grad * normal, axis=-1, keepdims=True)
    )


def column_sum(values):
    return jnp.sum(values.astype(f32), axis=0, keepdims=True)


def middle_kernel(
    ranks,
    back_ref,
    tok_ref,
    cot_ref,
    vec_ref,
    pack_ref,
    output_ref,
    resid_ref,
    dout_ref,
    attn_ref,
    mid_ref,
    act_ref,
    down_ref,
    pre_ref,
    branch_ref,
    sums_ref,
    out_w,
    up_w,
    down_w,
    slope_ref,
    sems,
):
    count = back_ref.shape[0]
    width = tok_ref.shape[1]
    turns = up_w.shape[1] // width
    half_ranks = ranks // 2

    copies = [pltpu.make_async_copy(pack_ref.at[:, pl.ds(0, width)], out_w, sems.at[0])]
    for t in range(turns):
        cols = pl.ds(t * width, width)
        copies.append(
            pltpu.make_async_copy(
                pack_ref.at[:, pl.ds((1 + t) * width, width)], up_w.at[:, cols], sems.at[1 + t]
            )
        )
        copies.append(
            pltpu.make_async_copy(
                pack_ref.at[:, pl.ds((1 + turns + t) * width, width)],
                down_w.at[t],
                sems.at[1 + turns + t],
            )
        )
    for copy in copies:
        copy.start()

    for g in range(GROUPS):
        own = [back_ref[g * ranks + r][:, 0:HD] for r in range(ranks)]
        shared = [back_ref[g * ranks + r][:, HD : 2 * HD] for r in range(ranks)]
        trio = [sum(own[1:half_ranks], own[0]), sum(own[half_ranks + 1 :], own[half_ranks])]
        trio.append(sum(shared[1:], shared[0]))
        attn_ref[:, g * PER_GROUP * HD : (g + 1) * PER_GROUP * HD] = jnp.concatenate(trio, axis=1)

    out_bias, attn_gain, attn_shift, down_bias, ffn_gain, ffn_shift = (
        vec_ref[k : k + 1, :] for k in range(2, 8)
    )
    copies[0].wait()
    branch = plain(attn_ref[...], out_w[...]) + out_bias
    normal, scale = normalized(tok_ref[...].astype(f32) + branch)
    mid = normal * attn_gain + attn_shift
    mid_low = mid.astype(bf16)
    mid_ref[...] = mid_low
    final = mid + down_bias
    for t in range(turns):
        cols = slice(t * width, (t + 1) * width)
        copies[1 + 2 * t].wait()
        pre = plain(mid_low, up_w[:, cols]) + vec_ref[8 + t : 9 + t, :]
        square = pre * pre
        bend = jnp.tanh(gelu_root * (pre + gelu_cubic * pre * square))
        rise = 0.5 * (1.0 + bend)
        slope_ref[:, cols] = rise + 0.5 * pre * (1.0 - bend * bend) * (
            gelu_root * (1.0 + 3.0 * gelu_cubic * square)
        )
        act = (pre * rise).astype(bf16)
        act_ref[:, cols] = act
        copies[2 + 2 * t].wait()
        final = final + plain(act, down_w[t])
    normal_two, scale_two = normalized(final)
    output_ref[...] = (normal_two * ffn_gain + ffn_shift).astype(bf16)
    cot = cot_ref[...].astype(f32)
    sums_ref[4:5, :] = column_sum(cot * normal_two)
    sums_ref[5:6, :] = column_sum(cot)
    grad_final = normalized_grad(normal_two, scale_two, cot * ffn_gain)
    down_low = grad_final.astype(bf16)
    down_ref[...] = down_low
    sums_ref[3:4, :] = column_sum(down_low)
    grad_mid = grad_final
    for t in range(turns):
        cols = slice(t * width, (t + 1) * width)
        grad_pre = (contract_cols(down_low, down_w[t]) * slope_ref[:, cols]).astype(bf16)
        pre_ref[:, cols] = grad_pre
        sums_ref[6 + t : 7 + t, :] = column_sum(grad_pre)
        grad_mid = grad_mid + contract_cols(grad_pre, up_w[:, cols])
    sums_ref[1:2, :] = column_sum(grad_mid * normal)
    sums_ref[2:3, :] = column_sum(grad_mid)
    resid = normalized_grad(normal, scale, grad_mid * attn_gain)
    resid_ref[...] = resid
    branch_low = resid.astype(bf16)
    branch_ref[...] = branch_low
    sums_ref[0:1, :] = column_sum(branch_low)
    grad_attn = contract_cols(branch_low, out_w[...]).astype(bf16)
    for j in range(count):
        first, shared = heads_of(j, ranks)
        dout_ref[j] = jnp.concatenate(
            [
                grad_attn[:, first * HD : (first + 1) * HD],
                grad_attn[:, shared * HD : (shared + 1) * HD],
            ],
            axis=1,
        )


def middle(ranks, back, tokens, cotangent, vectors, packed):
    count, (tok, width) = back.shape[0], tokens.shape
    turns = vectors.shape[0] - 8
    hidden = turns * width
    return call(
        functools.partial(middle_kernel, ranks),
        "middle",
        [
            shape((tok, width), bf16),
            shape((tok, width), f32),
            shape((count, tok, 128), bf16),
            shape((tok, width), bf16),
            shape((tok, width), bf16),
            shape((tok, hidden), bf16),
            shape((tok, width), bf16),
            shape((tok, hidden), bf16),
            shape((tok, width), bf16),
            shape((6 + turns, width), f32),
        ],
        [VMEM] * 4 + [ANY],
        [VMEM] * 10,
        4 * tok * width * (width + 2 * hidden),
        2 * width * (width + 2 * hidden),
        [
            pltpu.VMEM((width, width), bf16),
            pltpu.VMEM((width, hidden), bf16),
            pltpu.VMEM((turns, width, width), bf16),
            pltpu.VMEM((tok, hidden), f32),
            pltpu.SemaphoreType.DMA((1 + 2 * turns,)),
        ],
    )(back, tokens, cotangent, vectors, packed)


def weight_grad_kernel(pairs, where_ref, *refs):
    operands, (keep_ref, send_ref, total_ref) = refs[: 2 * len(pairs)], refs[2 * len(pairs) :]
    turn = pl.program_id(0)
    first = 0
    for k, turns in enumerate(pairs):

        def product(left_ref=operands[2 * k], right_ref=operands[2 * k + 1]):
            total_ref[...] = contract_rows(left_ref[...], right_ref[...])

        pl.when((turn >= first) & (turn < first + turns))(product)
        first += turns
    ny = keep_ref.shape[0]
    rows = total_ref.shape[0] // (2 * ny)
    mine, core = where_ref[0], where_ref[1]
    for d in range(ny):
        base = lax.rem(mine + d, ny) * 2
        for ref, c in ((keep_ref, core), (send_ref, 1 - core)):
            ref[d, 0] = total_ref[pl.ds(pl.multiple_of((base + c) * rows, 16), rows), :].astype(bf16)


def weight_grad(where, ny, *pairs):
    tok = pairs[0][0].shape[0]
    width = min(min(left.shape[1], right.shape[1]) for left, right in pairs)
    counts, specs, first = [], [], 0
    for pair in pairs:
        turns = max(operand.shape[1] for operand in pair) // width
        for operand in pair:
            if operand.shape[1] == width:
                specs.append(pl.BlockSpec((tok, width), lambda t: (0, 0)))
            else:
                specs.append(
                    pl.BlockSpec(
                        (tok, width),
                        lambda t, first=first, turns=turns: (0, jnp.clip(t - first, 0, turns - 1)),
                    )
                )
        counts.append(turns)
        first += turns
    rows = width // (2 * ny)
    return pl.pallas_call(
        functools.partial(weight_grad_kernel, counts),
        grid=(first,),
        out_shape=[shape((ny, first, rows, width), bf16)] * 2,
        in_specs=[SMEM] + specs,
        out_specs=[pl.BlockSpec((ny, 1, rows, width), lambda t: (0, t, 0, 0))] * 2,
        scratch_shapes=[pltpu.VMEM((width, width), f32)],
        cost_estimate=pl.CostEstimate(
            flops=2 * tok * width * width * first,
            bytes_accessed=2 * width * width * first,
            transcendentals=0,
        ),
        compiler_params=pltpu.CompilerParams(vmem_limit_bytes=VMEM_BYTES),
        name="weight_grad",
    )(where, *[operand for pair in pairs for operand in pair])


def swap(value, axis):
    return lax.all_to_all(value, axis, split_axis=0, concat_axis=0, tiled=True)


def shifted(value, axis, by):
    size = lax.axis_size(axis)
    return lax.ppermute(value, axis, [(i, (i + by) % size) for i in range(size)])


def far_first(size):
    return sorted(range(1, size), key=lambda d: -min(d, size - d))


def picked(value, axis, dim):
    size, here = lax.axis_size(axis), lax.axis_index(axis)

    def part(d):
        return lax.dynamic_index_in_dim(
            value, lax.rem(here + d, size), dim, keepdims=False
        ).astype(f32)

    return part


def split(value, nz, nx):
    return value.reshape(value.shape[:-2] + (nz, nx, value.shape[-2] // (nz * nx), value.shape[-1]))


def along_y(value):
    return lambda d: value[d]


def along_x(value):
    return picked(value, "x", value.ndim - 3)


def sends(parts, size):
    return [parts(d).astype(bf16) for d in far_first(size)]


def arrivals(sent, axis):
    return [shifted(part, axis, d) for d, part in zip(far_first(len(sent) + 1), sent)]


def plus(kept, got):
    return functools.reduce(lambda total, part: total + part.astype(f32), got, kept)


def summed(parts, axis):
    return plus(parts(0), arrivals(sends(parts, lax.axis_size(axis)), axis))


def body(
    tokens,
    qkv_weight,
    query_bias,
    value_bias,
    out_weight,
    out_bias,
    attn_gain,
    attn_shift,
    up_weight,
    up_bias,
    down_weight,
    down_bias,
    ffn_gain,
    ffn_shift,
    random_blocks,
    cotangent,
):
    ny, nc, nz, nx = (lax.axis_size(a) for a in ALL)
    count, devices = nz * nx, ny * nc * nz * nx
    ranks = count // GROUPS
    half_ranks = ranks // 2
    _, tok, width = tokens.shape
    blocks = tok // BLK
    plan = Plan(count, ranks, blocks)
    z, x = lax.axis_index("z"), lax.axis_index("x")
    ctx_index = z * nx + x
    rank = lax.rem(ctx_index, ranks).astype(jnp.int32).reshape(1)
    where = jnp.stack([lax.axis_index("y"), lax.axis_index("core")]).astype(jnp.int32)
    rows = qkv_weight.shape[0]
    hidden = up_weight.shape[1]
    turns = hidden // width
    flat_tokens = tokens.reshape(tok, width)

    up_shard = reordered(up_weight, devices, turns)
    down_shard = down_weight.reshape(turns, rows, width).transpose(1, 0, 2)
    packed = jnp.concatenate(
        [out_weight, up_shard, down_shard.reshape(rows, hidden)], axis=1
    )
    packed = lax.all_gather(packed, ALL, axis=0, tiled=True)

    def by_index(values):
        grouped = values.reshape(values.shape[:-2] + (GROUPS, PER_GROUP, values.shape[-1]))
        pairs = [
            jnp.stack([grouped[..., 0 if r < half_ranks else 1, :], grouped[..., 2, :]], axis=-2)
            for r in range(ranks)
        ]
        return jnp.moveaxis(jnp.stack(pairs, axis=-3), (-4, -3), (0, 1)).reshape(
            (count,) + values.shape[:-2] + (2, values.shape[-1])
        )

    weight_rows = by_index(qkv_weight.reshape(rows, 3, H, HD)).reshape(count, rows, SPAN)
    picks = by_index(random_blocks[0].astype(bf16)).reshape(count, 1, -1)
    entries = picks.shape[2]
    small = jnp.concatenate(
        [
            query_bias,
            value_bias,
            out_bias,
            attn_gain,
            attn_shift,
            down_bias,
            ffn_gain,
            ffn_shift,
            up_bias,
        ]
    )
    many = small.shape[0] // rows
    extra = -(-(rows + 2) // 8) * 8
    sent = jnp.concatenate(
        [
            weight_rows,
            jnp.pad(picks, ((0, 0), (0, 0), (0, SPAN - entries))),
            jnp.broadcast_to(jnp.pad(small, (0, SPAN - small.shape[0])), (count, 1, SPAN)),
            jnp.zeros((count, extra - rows - 2, SPAN), bf16),
        ],
        axis=1,
    )
    near = [d for d in range(1, nz) if min(d, nz - d) == 1]
    held = {0: flat_tokens}
    over = {}
    for e in range(1, nx):
        over[0, e] = shifted(flat_tokens, "x", e)
    for d in range(1, nz):
        held[d] = shifted(flat_tokens, "z", d)
    line = swap(sent, CTX)
    shifts = [0] + near + [d for d in far_first(nz) if d not in near]
    order = [(d, e) for e in range(nx) for d in shifts]
    pieces = []
    for d, e in order:
        if e and d:
            over[d, e] = shifted(held[d], "x", e)
        pieces.append(over[d, e] if e else held[d])
    owners = jnp.stack(
        [lax.rem(z + nz - d, nz) * nx + lax.rem(x + nx - e, nx) for d, e in order]
    ).astype(jnp.int32)
    targets = jnp.stack(
        [lax.rem(z + d, nz) * nx + lax.rem(x + e, nx) for d, e in order]
    ).astype(jnp.int32)
    rand = line[:, rows, :entries].astype(jnp.int32).reshape(-1)
    seqs = ny * nc
    full = swap(
        tied(jnp.broadcast_to(line[None], (seqs,) + line.shape), over[0, 1], *(over[d, 1] for d in near), *held.values()), SEQ
    )
    columns = full[:, :, :rows].reshape(width, SPAN)
    vectors = full[:, :, rows + 1, : small.shape[0]].astype(f32)
    vectors = vectors.reshape(devices, many, rows).transpose(1, 0, 2).reshape(many, width)
    bias_table = by_index(
        jnp.stack([vectors[0], jnp.zeros_like(vectors[0]), vectors[1]]).reshape(3, H, HD)
    ).reshape(count, 1, SPAN)
    bias = lax.dynamic_index_in_dim(bias_table, ctx_index, 0, keepdims=False)

    kv = qkv_project(owners, pieces, columns, bias)
    attended, lse = attn_forward(plan, rand, rank, kv)
    back = swap(attended.reshape(count, tok, 128), CTX)

    output, resid, dout, attn_low, mid_low, act_low, down_low, pre_low, branch_low, sums = middle(
        ranks, back, flat_tokens, cotangent.reshape(tok, width), vectors, packed
    )
    dout = swap(dout, CTX).reshape(plan.rows, 128)

    first_keep, first_send = weight_grad(where, ny, (act_low, down_low), (attn_low, branch_low))
    second_keep, second_send = weight_grad(where, ny, (mid_low, pre_low))
    first_got, second_got = shifted(first_send, "core", 1), shifted(second_send, "core", 1)

    def both(keep, got):
        return split(keep.astype(f32) + got.astype(f32), nz, nx)

    first_sent = sends(along_y(both(first_keep, first_got)), ny)
    second_sent = sends(along_x(both(second_keep, second_got)), nx)

    grads = attn_backward(plan, rand, rank, kv, dout, lse, first_sent + second_sent)
    first_more, second_more = arrivals(first_sent, "y"), arrivals(second_sent, "x")
    terms = token_grads(count, targets, grads, columns, ())
    first_kept = along_y(both(*tied((first_keep, first_got), terms[0])))(0)
    second_kept = along_x(both(*tied((second_keep, second_got), terms[0])))(0)
    first_parts = along_x(plus(first_kept, first_more))
    second_parts = along_y(plus(second_kept, second_more))
    first_more = arrivals(sends(first_parts, nx), "x")
    second_more = arrivals(sends(second_parts, ny), "y")
    column_grads, bias_grads = qkv_grads(owners, pieces, grads, first_more + second_more)

    line = jnp.concatenate(
        [
            plus(first_parts(0), first_more).astype(bf16).transpose(1, 0, 2, 3),
            plus(second_parts(0), second_more).astype(bf16).transpose(1, 0, 2, 3),
        ],
        axis=1,
    )
    line = swap(line, "z")

    def over_x(d, *others):
        return [
            shifted(tied(terms[e * nz + shifts.index(d)], *others), "x", e) for e in range(1, nx)
        ]

    line_order = far_first(nz)
    total = added(
        [[terms[shifts.index(d)]] + over_x(d) for d in line_order], [line, column_grads]
    )
    line_got = [shifted(part, "z", d) for d, part in zip(line_order, total)]
    own = plus(terms[0].astype(f32), over_x(0, *total))
    tokens_grad = plus(resid + own, line_got).reshape(1, tok, width)

    listed = sums.shape[0]
    vector_sums = sums.reshape(listed, ny, nc, count, rows).transpose(1, 2, 3, 0, 4)
    vector_sums = vector_sums.reshape(ny, nc, nz, nx, 1, listed * rows).astype(bf16)
    units = -(-(rows + 2) // rows)
    table = jnp.concatenate(
        [
            tied(column_grads, total[0]).reshape(ny, nc, nz, nx, rows, SPAN),
            jnp.broadcast_to(bias_grads.astype(bf16), (ny, nc, nz, nx, 1, SPAN)),
            jnp.pad(vector_sums, ((0, 0),) * 5 + ((0, SPAN - listed * rows),)),
            jnp.zeros((ny, nc, nz, nx, units * rows - rows - 2, SPAN), bf16),
        ],
        axis=4,
    )
    table = summed(picked(table, "core", 1), "core")
    table = summed(picked(table, "y", 0), "y").astype(bf16)
    mine = picked(table, "x", 1)
    own, other = mine(0).astype(bf16), shifted(mine(1).astype(bf16), "x", 1)
    table = jnp.where(x == 0, jnp.stack([own, other], 2), jnp.stack([other, own], 2))

    table = swap(table.reshape(nz, units * rows, nx * SPAN), "z")
    table = table.reshape(nz, units * rows, nx, SPAN)[:, : rows + 2].astype(f32)
    weight_sums = jnp.sum(line.astype(f32), axis=0)
    down_grad = weight_sums[:turns].reshape(turns * rows, width)
    out_grad = weight_sums[turns]
    up_grad = weight_sums[turns + 1 :].transpose(1, 0, 2).reshape(rows, hidden)
    up_grad = reordered(up_grad, turns, devices)
    table = table.transpose(0, 2, 1, 3).reshape(count, rows + 2, SPAN)
    shards = jnp.sum(table[:, rows + 1, : listed * rows], axis=0).reshape(listed, rows)
    table = table[:, : rows + 1].reshape(GROUPS, ranks, rows + 1, 3, 2, HD)
    table = jnp.stack(
        [
            jnp.sum(table[:, :half_ranks, :, :, 0], axis=1),
            jnp.sum(table[:, half_ranks:, :, :, 0], axis=1),
            jnp.sum(table[:, :, :, :, 1], axis=1),
        ],
        axis=1,
    )
    table = table.transpose(2, 3, 0, 1, 4).reshape(rows + 1, 3, width)
    qkv_grad = table[:rows].reshape(rows, 3 * width)
    device = (lax.axis_index("y") * nc + lax.axis_index("core")) * count + ctx_index
    query_bias_grad = lax.dynamic_slice_in_dim(table[rows, 0], device * rows, rows)
    value_bias_grad = lax.dynamic_slice_in_dim(table[rows, 2], device * rows, rows)

    return (
        output.reshape(1, tok, width),
        tokens_grad,
        qkv_grad,
        query_bias_grad,
        value_bias_grad,
        out_grad,
        shards[0],
        shards[1],
        shards[2],
        up_grad,
        shards[6:].reshape(-1),
        down_grad,
        shards[3],
        shards[4],
        shards[5],
    )


def solution(mesh):
    dp, ctx = (mesh.shape[a] for a in ("dp", "ctx"))
    fine = Mesh(mesh.devices.reshape(dp // 2, 2, ctx // 2, 2), ALL)
    token_spec = P(SEQ, CTX, None)
    matrix, vector = P(ALL, None), P(ALL)
    return jax.shard_map(
        body,
        mesh=fine,
        in_specs=(
            token_spec,
            matrix,
            vector,
            vector,
            matrix,
            vector,
            vector,
            vector,
            matrix,
            vector,
            matrix,
            vector,
            vector,
            vector,
            P(SEQ, CTX, None, None),
            token_spec,
        ),
        out_specs=(
            token_spec,
            token_spec,
            matrix,
            vector,
            vector,
            matrix,
            vector,
            vector,
            vector,
            matrix,
            vector,
            matrix,
            vector,
            vector,
            vector,
        ),
        check_vma=False,
    )
```

```python
import functools

import jax
import jax.numpy as jnp
from jax import lax
from jax.experimental import pallas as pl
from jax.experimental.pallas import tpu as pltpu
from jax.sharding import Mesh, PartitionSpec as P

H = 12
HD = 64
BLK = 64
RAND = 3
GROUPS = 4
PER_GROUP = 3
SPAN = 3 * 2 * HD
VMEM_BYTES = 56 * 1024 * 1024

bf16 = jnp.bfloat16
f32 = jnp.float32

norm_eps = 1e-06
gelu_root = 0.7978845608028654
gelu_cubic = 0.044715

ALL = ("y", "core", "z", "x")
SEQ = ("y", "core")
CTX = ("z", "x")

VMEM = pl.BlockSpec(memory_space=pltpu.VMEM)
SMEM = pl.BlockSpec(memory_space=pltpu.SMEM)
ANY = pl.BlockSpec(memory_space=pl.ANY)


def call(kernel, name, out_shape, in_specs, out_specs, flops, moved, scratch=(), after=()):
    def ordered(*refs):
        kernel(*refs[len(after) :])

    built = pl.pallas_call(
        ordered,
        out_shape=out_shape,
        in_specs=[ANY] * len(after) + in_specs,
        out_specs=out_specs,
        scratch_shapes=scratch,
        cost_estimate=pl.CostEstimate(flops=flops, bytes_accessed=moved, transcendentals=0),
        compiler_params=pltpu.CompilerParams(vmem_limit_bytes=VMEM_BYTES),
        name=name,
    )
    return functools.partial(built, *after)


def tied(value, *others):
    return lax.optimization_barrier((value,) + others)[0]


def shape(dims, kind):
    return jax.ShapeDtypeStruct(dims, kind)


def contract_rows(left_side, right_side):
    return lax.dot_general(
        left_side, right_side, (((0,), (0,)), ((), ())), preferred_element_type=f32
    )


def contract_cols(left_side, right_side):
    return lax.dot_general(
        left_side, right_side, (((1,), (1,)), ((), ())), preferred_element_type=f32
    )


def plain(left_side, right_side):
    return jnp.dot(left_side, right_side, preferred_element_type=f32)


def heads_of(index, ranks):
    group, rank = index // ranks, index % ranks
    first = PER_GROUP * group + (0 if rank < ranks // 2 else 1)
    return first, PER_GROUP * group + 2


def qkv_kernel(count, owner_ref, *refs):
    x_refs, w_ref, b_ref, out_ref = refs[:count], refs[count], refs[count + 1], refs[count + 2]
    tok = x_refs[0].shape[0]
    for k in range(count):
        rows = plain(x_refs[k][...], w_ref[...]) + b_ref[...]
        at = pl.ds(pl.multiple_of(owner_ref[k] * tok, BLK), tok)
        out_ref[at, :] = rows.astype(bf16)


def qkv_project(owners, pieces, weights, bias):
    count = len(pieces)
    tok, width = pieces[0].shape
    return call(
        functools.partial(qkv_kernel, count),
        "qkv_project",
        shape((count * tok, SPAN), bf16),
        [SMEM] + [VMEM] * (count + 2),
        VMEM,
        2 * count * tok * width * SPAN,
        4 * count * tok * width,
    )(owners, *pieces, weights, bias)


def token_grad_kernel(count, owner_ref, grad_ref, w_ref, *out_refs):
    tok = out_refs[0].shape[0]
    for k in range(count):
        at = pl.ds(pl.multiple_of(owner_ref[k] * tok, BLK), tok)
        out_refs[k][...] = contract_cols(grad_ref[at, :], w_ref[...]).astype(bf16)


def token_grads(count, owners, grads, weights, after):
    tok, width = grads.shape[0] // count, weights.shape[0]
    return call(
        functools.partial(token_grad_kernel, count),
        "token_grads",
        [shape((tok, width), bf16)] * count,
        [SMEM, VMEM, VMEM],
        [VMEM] * count,
        2 * count * tok * width * SPAN,
        4 * count * tok * width,
        after=after,
    )(owners, grads, weights)


def add_kernel(counts, *refs):
    at = sum(counts)
    for k, n in enumerate(counts):
        parts = [ref[...].astype(f32) for ref in refs[sum(counts[:k]) : sum(counts[: k + 1])]]
        refs[at + k][...] = functools.reduce(jnp.add, parts).astype(bf16)


def added(groups, after):
    counts = [len(group) for group in groups]
    size = groups[0][0].size
    return call(
        functools.partial(add_kernel, counts),
        "added",
        [shape(group[0].shape, bf16) for group in groups],
        [VMEM] * sum(counts),
        [VMEM] * len(groups),
        size * sum(counts),
        2 * size * sum(counts),
        after=after,
    )(*[part for group in groups for part in group])


def qkv_grad_kernel(count, owner_ref, *refs):
    x_refs, grad_ref, out_ref, bias_ref = refs[:count], refs[count], refs[count + 1], refs[count + 2]
    tok = x_refs[0].shape[0]
    total = None
    for k in range(count):
        at = pl.ds(pl.multiple_of(owner_ref[k] * tok, BLK), tok)
        part = contract_rows(x_refs[k][...], grad_ref[at, :])
        total = part if total is None else total + part
    out_ref[...] = total.astype(bf16)
    bias_ref[...] = jnp.sum(grad_ref[...].astype(f32), axis=0, keepdims=True)


def qkv_grads(owners, pieces, grads, after):
    count = len(pieces)
    tok, width = pieces[0].shape
    return call(
        functools.partial(qkv_grad_kernel, count),
        "qkv_grads",
        [shape((width, SPAN), bf16), shape((1, SPAN), f32)],
        [SMEM] + [VMEM] * (count + 1),
        [VMEM, VMEM],
        2 * count * tok * width * SPAN,
        4 * count * tok * width,
        after=after,
    )(owners, *pieces, grads)


class Plan:
    def __init__(self, count, ranks, blocks):
        self.count, self.ranks, self.blocks = count, ranks, blocks
        self.steps = (ranks // 2, ranks)
        self.owners = (count // self.steps[0], count // self.steps[1])
        self.total = count * blocks
        self.units = (self.owners[0] + self.owners[1]) * blocks
        self.rows = self.total * BLK
        self.chunk = min(self.rows, 2048)

    def at(self, block):
        return pl.ds(pl.multiple_of(block * BLK, BLK), BLK)

    def unit(self, half, turn, inner):
        return (half * self.owners[0] + turn) * self.blocks + inner

    def named(self, half, block, rand_ref):
        ids = [
            jnp.maximum(block - 1, 0),
            block,
            jnp.minimum(block + 1, self.total - 1),
            0,
            self.total - 1,
        ]
        for t in range(RAND):
            ids.append(rand_ref[(block * 2 + half) * RAND + t])
        return ids

    def flops(self, products):
        return 2 * products * self.units * BLK * 128 * 8 * BLK


def only_half(values, half):
    lane = lax.broadcasted_iota(jnp.int32, values.shape, 1)
    return jnp.where((lane < HD) == (half == 0), values, jnp.zeros_like(values))


def attn_forward_kernel(plan, rand_ref, rank_ref, kv_ref, out_ref, lse_ref):
    rank = rank_ref[0]
    out_ref[...] = jnp.zeros_like(out_ref)

    def emit(half, block, unit, attended, lse):
        out_ref[plan.at(block), half * HD : (half + 1) * HD] = attended[
            :, half * HD : (half + 1) * HD
        ].astype(bf16)
        lse_ref[plan.at(unit), :] = jnp.broadcast_to(lse, (BLK, 128))

    def query(half, block):
        return only_half(kv_ref[plan.at(block), 0:128], half) * 0.125

    for half in range(2):
        step = plan.steps[half]
        offset = lax.rem(rank, step) if step > 1 else 0

        def turn_body(turn, carry, half=half, step=step, offset=offset):
            inners = range(2 * plan.blocks)
            listed = [
                ((2 * turn + i // plan.blocks) * step + offset) * plan.blocks + i % plan.blocks
                for i in inners
            ]
            named = [plan.named(half, block, rand_ref) for block in listed]
            scores = []
            for inner, ids in zip(inners, named):
                keys = jnp.concatenate([kv_ref[plan.at(i), 128:256] for i in ids], axis=0)
                scores.append(contract_cols(query(half, listed[inner]), keys))
            probs, lses = [], []
            for part in scores:
                top = jnp.max(part, axis=-1, keepdims=True)
                grown = jnp.exp(part - top)
                total = jnp.sum(grown, axis=-1, keepdims=True)
                probs.append((grown * (1.0 / total)).astype(bf16))
                lses.append(top + jnp.log(total))
            for inner, ids in zip(inners, named):
                values = jnp.concatenate([kv_ref[plan.at(i), 256:384] for i in ids], axis=0)
                attended = plain(probs[inner], values)
                block = listed[inner]
                emit(half, block, plan.unit(half, 2 * turn, inner), attended, lses[inner])
            return carry

        lax.fori_loop(0, plan.owners[half] // 2, turn_body, 0)

    chunks = [pl.ds(c, plan.chunk) for c in range(0, plan.rows, plan.chunk)]
    for half in range(2):
        step = plan.steps[half]
        for block in (0, plan.total - 1):
            owner = block // plan.blocks

            def whole(half=half, step=step, owner=owner, block=block):
                q = query(half, block)
                scores = [contract_cols(q, kv_ref[c, 128:256]) for c in chunks]
                tops = [jnp.max(s, axis=-1, keepdims=True) for s in scores]
                top = functools.reduce(jnp.maximum, tops)
                grown = [jnp.exp(s - top) for s in scores]
                total = sum(jnp.sum(e, axis=-1, keepdims=True) for e in grown)
                scale = 1.0 / total
                attended = sum(
                    plain((e * scale).astype(bf16), kv_ref[c, 256:384])
                    for e, c in zip(grown, chunks)
                )
                unit = plan.unit(half, owner // step, block % plan.blocks)
                emit(half, block, unit, attended, top + jnp.log(total))

            if step == 1:
                whole()
            else:
                pl.when(lax.rem(rank, step) == owner % step)(whole)


def attn_forward(plan, rand, rank, kv):
    return call(
        functools.partial(attn_forward_kernel, plan),
        "attn_forward",
        (shape((plan.rows, 128), bf16), shape((plan.units * BLK, 128), f32)),
        [SMEM, SMEM, VMEM],
        (VMEM, VMEM),
        plan.flops(2),
        8 * plan.rows * 128,
    )(rand, rank, kv)


def attn_backward_kernel(
    plan, rand_ref, rank_ref, kv_ref, dout_ref, lse_ref, out_ref, sum_ref
):
    rank = rank_ref[0]
    out_ref[:, 0:128] = jnp.zeros((plan.rows, 128), bf16)
    sum_ref[...] = jnp.zeros_like(sum_ref)

    def operands(half, block, unit):
        q = only_half(kv_ref[plan.at(block), 0:128], half) * 0.125
        dout = only_half(dout_ref[plan.at(block), :], half)
        return q, dout, lse_ref[plan.at(unit), :][:, 0:1]

    def emit(half, block, grad_query):
        out_ref[plan.at(block), half * HD : (half + 1) * HD] = (
            grad_query[:, half * HD : (half + 1) * HD] * 0.125
        ).astype(bf16)

    for half in range(2):
        step = plan.steps[half]
        offset = lax.rem(rank, step) if step > 1 else 0

        def turn_body(turn, carry, half=half, step=step, offset=offset):
            inners = range(2 * plan.blocks)
            listed = [
                ((2 * turn + i // plan.blocks) * step + offset) * plan.blocks + i % plan.blocks
                for i in inners
            ]
            named = [plan.named(half, block, rand_ref) for block in listed]
            given, scores, grad_probs = [], [], []
            for inner, ids in zip(inners, named):
                block = listed[inner]
                q, dout, lse = operands(half, block, plan.unit(half, 2 * turn, inner))
                if inner % plan.blocks in (0, plan.blocks - 1):
                    edge = (block == 0) | (block == plan.total - 1)
                    dout = dout * jnp.where(edge, 0.0, 1.0).astype(bf16)
                given.append((q, dout, lse))
                keys = jnp.concatenate([kv_ref[plan.at(i), 128:256] for i in ids], axis=0)
                scores.append(contract_cols(q, keys))
            for inner, ids in zip(inners, named):
                values = jnp.concatenate([kv_ref[plan.at(i), 256:384] for i in ids], axis=0)
                grad_probs.append(contract_cols(given[inner][1], values))
            low_probs, grad_scores = [], []
            for inner in inners:
                probs = jnp.exp(scores[inner] - given[inner][2])
                delta = jnp.sum(probs * grad_probs[inner], axis=-1, keepdims=True)
                grad_scores.append((probs * (grad_probs[inner] - delta)).astype(bf16))
                low_probs.append(probs.astype(bf16))
            for inner, ids in zip(inners, named):
                keys = jnp.concatenate([kv_ref[plan.at(i), 128:256] for i in ids], axis=0)
                emit(half, listed[inner], plain(grad_scores[inner], keys))
            grad_keys = [contract_rows(grad_scores[i], given[i][0]) for i in inners]
            grad_values = [contract_rows(low_probs[i], given[i][1]) for i in inners]
            for inner, ids in zip(inners, named):
                for t, i in enumerate(ids):
                    sum_ref[plan.at(i), 0:128] += grad_keys[inner][t * BLK : (t + 1) * BLK]
                    sum_ref[plan.at(i), 128:256] += grad_values[inner][t * BLK : (t + 1) * BLK]
            return carry

        lax.fori_loop(0, plan.owners[half] // 2, turn_body, 0)

    chunks = [pl.ds(c, plan.chunk) for c in range(0, plan.rows, plan.chunk)]
    for half in range(2):
        step = plan.steps[half]
        for block in (0, plan.total - 1):
            owner = block // plan.blocks

            def whole(half=half, step=step, owner=owner, block=block):
                unit = plan.unit(half, owner // step, block % plan.blocks)
                q, dout, lse = operands(half, block, unit)
                probs = [jnp.exp(contract_cols(q, kv_ref[c, 128:256]) - lse) for c in chunks]
                grad_probs = [contract_cols(dout, kv_ref[c, 256:384]) for c in chunks]
                delta = sum(
                    jnp.sum(p * g, axis=-1, keepdims=True) for p, g in zip(probs, grad_probs)
                )
                grad_query = jnp.zeros((BLK, 128), f32)
                for p, g, c in zip(probs, grad_probs, chunks):
                    grad_scores = (p * (g - delta)).astype(bf16)
                    sum_ref[c, 0:128] += contract_rows(grad_scores, q)
                    sum_ref[c, 128:256] += contract_rows(p.astype(bf16), dout)
                    grad_query += plain(grad_scores, kv_ref[c, 128:256])
                emit(half, block, grad_query)

            if step == 1:
                whole()
            else:
                pl.when(lax.rem(rank, step) == owner % step)(whole)

    out_ref[:, 128:384] = sum_ref[...].astype(bf16)


def attn_backward(plan, rand, rank, kv, dout, lse, after):
    return call(
        functools.partial(attn_backward_kernel, plan),
        "attn_backward",
        shape((plan.rows, SPAN), bf16),
        [SMEM, SMEM, VMEM, VMEM, VMEM],
        VMEM,
        plan.flops(5),
        16 * plan.rows * 128,
        [pltpu.VMEM((plan.rows, 256), f32)],
        after,
    )(rand, rank, kv, dout, lse)


def table_kernel(ranks, rows, table_ref, grad_ref, bias_ref, sums_ref):
    nz, width = table_ref.shape[0], table_ref.shape[2]
    nx = width // SPAN
    tiles = [
        table_ref[k // nx][:, k % nx * SPAN : (k % nx + 1) * SPAN].astype(f32)
        for k in range(nz * nx)
    ]
    sums_ref[...] = functools.reduce(jnp.add, [tile[rows + 1 : rows + 2] for tile in tiles])
    for part in range(3):
        heads = []
        for g in range(GROUPS):
            own = [tiles[g * ranks + r][:, part * 128 : part * 128 + HD] for r in range(ranks)]
            shared = [tiles[g * ranks + r][:, part * 128 + HD : (part + 1) * 128] for r in range(ranks)]
            for group in (own[: ranks // 2], own[ranks // 2 :], shared):
                heads.append(functools.reduce(jnp.add, group))
        whole = jnp.concatenate(heads, axis=1)
        grad_ref[:, part * H * HD : (part + 1) * H * HD] = whole[0:rows]
        bias_ref[part : part + 1, :] = whole[rows : rows + 1]


def table_grads(ranks, rows, table):
    return call(
        functools.partial(table_kernel, ranks, rows),
        "table_grads",
        [shape((rows, 3 * H * HD), f32), shape((3, H * HD), f32), shape((1, SPAN), f32)],
        [VMEM],
        [VMEM] * 3,
        table.size,
        2 * table.size,
    )(table)


def reorder_kernel(outer, inner, rows, in_ref, out_ref):
    value = in_ref[...].astype(f32)
    out_ref[...] = jnp.concatenate(
        [
            value[:, (o * inner + i) * rows : (o * inner + i + 1) * rows]
            for i in range(inner)
            for o in range(outer)
        ],
        axis=1,
    ).astype(out_ref.dtype)


def reordered(value, outer, inner):
    rows, cols = value.shape
    run = cols // (outer * inner)
    if run < 8:
        return value.reshape(rows, outer, inner, run).transpose(0, 2, 1, 3).reshape(rows, cols)
    return call(
        functools.partial(reorder_kernel, outer, inner, run),
        "reorder",
        shape((rows, cols), value.dtype),
        [VMEM],
        VMEM,
        rows * cols,
        4 * rows * cols,
    )(value)


def pack_kernel(outer, inner, out_w_ref, up_ref, down_ref, packed_ref):
    rows, width = out_w_ref.shape
    packed_ref[:, 0:width] = out_w_ref[...]
    up = up_ref[...].astype(f32)
    down = down_ref[...].astype(f32)
    for i in range(inner):
        packed_ref[:, (1 + i) * width : (2 + i) * width] = jnp.concatenate(
            [
                up[:, (o * inner + i) * rows : (o * inner + i + 1) * rows]
                for o in range(outer)
            ],
            axis=1,
        ).astype(bf16)
        packed_ref[:, (1 + inner + i) * width : (2 + inner + i) * width] = down[
            i * rows : (i + 1) * rows
        ].astype(bf16)


def packed_weights(out_weight, up_weight, down_weight, devices):
    rows, width = out_weight.shape
    turns = up_weight.shape[1] // width
    if rows < 8:
        up = reordered(up_weight, devices, turns)
        down = down_weight.reshape(turns, rows, width).transpose(1, 0, 2)
        return jnp.concatenate([out_weight, up, down.reshape(rows, turns * width)], axis=1)
    return call(
        functools.partial(pack_kernel, devices, turns),
        "packed_weights",
        shape((rows, (1 + 2 * turns) * width), bf16),
        [VMEM] * 3,
        VMEM,
        rows * width,
        rows * width,
    )(out_weight, up_weight, down_weight)


def normalized(values):
    center = values - jnp.mean(values, axis=-1, keepdims=True)
    spread = jnp.mean(center * center, axis=-1, keepdims=True)
    scale = lax.rsqrt(spread + norm_eps)
    return center * scale, scale


def normalized_grad(normal, scale, grad):
    return scale * (
        grad
        - jnp.mean(grad, axis=-1, keepdims=True)
        - normal * jnp.mean(grad * normal, axis=-1, keepdims=True)
    )


def column_sum(values):
    return jnp.sum(values.astype(f32), axis=0, keepdims=True)


def middle_kernel(
    ranks,
    back_ref,
    tok_ref,
    cot_ref,
    vec_ref,
    pack_ref,
    output_ref,
    resid_ref,
    dout_ref,
    attn_ref,
    mid_ref,
    act_ref,
    down_ref,
    pre_ref,
    branch_ref,
    sums_ref,
    out_w,
    up_w,
    down_w,
    slope_ref,
    sems,
):
    count = back_ref.shape[0]
    width = tok_ref.shape[1]
    turns = up_w.shape[1] // width
    half_ranks = ranks // 2

    copies = [pltpu.make_async_copy(pack_ref.at[:, pl.ds(0, width)], out_w, sems.at[0])]
    for t in range(turns):
        cols = pl.ds(t * width, width)
        copies.append(
            pltpu.make_async_copy(
                pack_ref.at[:, pl.ds((1 + t) * width, width)], up_w.at[:, cols], sems.at[1 + t]
            )
        )
        copies.append(
            pltpu.make_async_copy(
                pack_ref.at[:, pl.ds((1 + turns + t) * width, width)],
                down_w.at[t],
                sems.at[1 + turns + t],
            )
        )
    for copy in copies:
        copy.start()

    for g in range(GROUPS):
        own = [back_ref[g * ranks + r][:, 0:HD] for r in range(ranks)]
        shared = [back_ref[g * ranks + r][:, HD : 2 * HD] for r in range(ranks)]
        trio = [sum(own[1:half_ranks], own[0]), sum(own[half_ranks + 1 :], own[half_ranks])]
        trio.append(sum(shared[1:], shared[0]))
        attn_ref[:, g * PER_GROUP * HD : (g + 1) * PER_GROUP * HD] = jnp.concatenate(trio, axis=1)

    out_bias, attn_gain, attn_shift, down_bias, ffn_gain, ffn_shift = (
        vec_ref[k : k + 1, :] for k in range(2, 8)
    )
    copies[0].wait()
    branch = plain(attn_ref[...], out_w[...]) + out_bias
    normal, scale = normalized(tok_ref[...].astype(f32) + branch)
    mid = normal * attn_gain + attn_shift
    mid_low = mid.astype(bf16)
    mid_ref[...] = mid_low
    final = mid + down_bias
    for t in range(turns):
        cols = slice(t * width, (t + 1) * width)
        copies[1 + 2 * t].wait()
        pre = plain(mid_low, up_w[:, cols]) + vec_ref[8 + t : 9 + t, :]
        square = pre * pre
        bend = jnp.tanh(gelu_root * (pre + gelu_cubic * pre * square))
        rise = 0.5 * (1.0 + bend)
        slope_ref[:, cols] = rise + 0.5 * pre * (1.0 - bend * bend) * (
            gelu_root * (1.0 + 3.0 * gelu_cubic * square)
        )
        act = (pre * rise).astype(bf16)
        act_ref[:, cols] = act
        copies[2 + 2 * t].wait()
        final = final + plain(act, down_w[t])
    normal_two, scale_two = normalized(final)
    output_ref[...] = (normal_two * ffn_gain + ffn_shift).astype(bf16)
    cot = cot_ref[...].astype(f32)
    sums_ref[4:5, :] = column_sum(cot * normal_two)
    sums_ref[5:6, :] = column_sum(cot)
    grad_final = normalized_grad(normal_two, scale_two, cot * ffn_gain)
    down_low = grad_final.astype(bf16)
    down_ref[...] = down_low
    sums_ref[3:4, :] = column_sum(down_low)
    grad_mid = grad_final
    for t in range(turns):
        cols = slice(t * width, (t + 1) * width)
        grad_pre = (contract_cols(down_low, down_w[t]) * slope_ref[:, cols]).astype(bf16)
        pre_ref[:, cols] = grad_pre
        sums_ref[6 + t : 7 + t, :] = column_sum(grad_pre)
        grad_mid = grad_mid + contract_cols(grad_pre, up_w[:, cols])
    sums_ref[1:2, :] = column_sum(grad_mid * normal)
    sums_ref[2:3, :] = column_sum(grad_mid)
    resid = normalized_grad(normal, scale, grad_mid * attn_gain)
    resid_ref[...] = resid
    branch_low = resid.astype(bf16)
    branch_ref[...] = branch_low
    sums_ref[0:1, :] = column_sum(branch_low)
    grad_attn = contract_cols(branch_low, out_w[...]).astype(bf16)
    for j in range(count):
        first, shared = heads_of(j, ranks)
        dout_ref[j] = jnp.concatenate(
            [
                grad_attn[:, first * HD : (first + 1) * HD],
                grad_attn[:, shared * HD : (shared + 1) * HD],
            ],
            axis=1,
        )


def middle(ranks, back, tokens, cotangent, vectors, packed):
    count, (tok, width) = back.shape[0], tokens.shape
    turns = vectors.shape[0] - 8
    hidden = turns * width
    return call(
        functools.partial(middle_kernel, ranks),
        "middle",
        [
            shape((tok, width), bf16),
            shape((tok, width), f32),
            shape((count, tok, 128), bf16),
            shape((tok, width), bf16),
            shape((tok, width), bf16),
            shape((tok, hidden), bf16),
            shape((tok, width), bf16),
            shape((tok, hidden), bf16),
            shape((tok, width), bf16),
            shape((6 + turns, width), f32),
        ],
        [VMEM] * 4 + [ANY],
        [VMEM] * 10,
        4 * tok * width * (width + 2 * hidden),
        2 * width * (width + 2 * hidden),
        [
            pltpu.VMEM((width, width), bf16),
            pltpu.VMEM((width, hidden), bf16),
            pltpu.VMEM((turns, width, width), bf16),
            pltpu.VMEM((tok, hidden), f32),
            pltpu.SemaphoreType.DMA((1 + 2 * turns,)),
        ],
    )(back, tokens, cotangent, vectors, packed)


def weight_grad_kernel(pairs, where_ref, *refs):
    operands, outs, total_ref = refs[: 2 * len(pairs)], refs[2 * len(pairs) : -1], refs[-1]
    turn = pl.program_id(0)
    first = 0
    for k, turns in enumerate(pairs):

        def product(left_ref=operands[2 * k], right_ref=operands[2 * k + 1]):
            total_ref[...] = contract_rows(left_ref[...], right_ref[...])

        pl.when((turn >= first) & (turn < first + turns))(product)
        first += turns
    ny = len(outs) // 2
    rows = total_ref.shape[0] // (2 * ny)
    mine, core = where_ref[0], where_ref[1]
    for d in range(ny):
        base = lax.rem(mine + d, ny) * 2
        for ref, c in ((outs[d], core), (outs[ny + d], 1 - core)):
            ref[0] = total_ref[pl.ds(pl.multiple_of((base + c) * rows, 16), rows), :].astype(bf16)


def weight_grad(where, ny, *pairs):
    tok = pairs[0][0].shape[0]
    width = min(min(left.shape[1], right.shape[1]) for left, right in pairs)
    counts, specs, first = [], [], 0
    for pair in pairs:
        turns = max(operand.shape[1] for operand in pair) // width
        for operand in pair:
            if operand.shape[1] == width:
                specs.append(pl.BlockSpec((tok, width), lambda t: (0, 0)))
            else:
                specs.append(
                    pl.BlockSpec(
                        (tok, width),
                        lambda t, first=first, turns=turns: (0, jnp.clip(t - first, 0, turns - 1)),
                    )
                )
        counts.append(turns)
        first += turns
    rows = width // (2 * ny)
    parts = pl.pallas_call(
        functools.partial(weight_grad_kernel, counts),
        grid=(first,),
        out_shape=[shape((first, rows, width), bf16)] * (2 * ny),
        in_specs=[SMEM] + specs,
        out_specs=[pl.BlockSpec((1, rows, width), lambda t: (t, 0, 0))] * (2 * ny),
        scratch_shapes=[pltpu.VMEM((width, width), f32)],
        cost_estimate=pl.CostEstimate(
            flops=2 * tok * width * width * first,
            bytes_accessed=2 * width * width * first,
            transcendentals=0,
        ),
        compiler_params=pltpu.CompilerParams(vmem_limit_bytes=VMEM_BYTES),
        name="weight_grad",
    )(where, *[operand for pair in pairs for operand in pair])
    return parts[:ny], parts[ny:]


def swap(value, axis):
    return lax.all_to_all(value, axis, split_axis=0, concat_axis=0, tiled=True)


def shifted(value, axis, by):
    size = lax.axis_size(axis)
    return lax.ppermute(value, axis, [(i, (i + by) % size) for i in range(size)])


def far_first(size):
    return sorted(range(1, size), key=lambda d: -min(d, size - d))


def picked(value, axis, dim):
    size, here = lax.axis_size(axis), lax.axis_index(axis)

    def part(d):
        return lax.dynamic_index_in_dim(
            value, lax.rem(here + d, size), dim, keepdims=False
        ).astype(f32)

    return part


def split(value, nz, nx):
    return value.reshape(value.shape[:-2] + (nz, nx, value.shape[-2] // (nz * nx), value.shape[-1]))


def along_y(value):
    return lambda d: value[d]


def along_x(value):
    return picked(value, "x", value.ndim - 3)


def sends(parts, size):
    return [parts(d).astype(bf16) for d in far_first(size)]


def arrivals(sent, axis):
    return [shifted(part, axis, d) for d, part in zip(far_first(len(sent) + 1), sent)]


def plus(kept, got):
    return functools.reduce(lambda total, part: total + part.astype(f32), got, kept)


def summed(parts, axis):
    return plus(parts(0), arrivals(sends(parts, lax.axis_size(axis)), axis))


def body(
    tokens,
    qkv_weight,
    query_bias,
    value_bias,
    out_weight,
    out_bias,
    attn_gain,
    attn_shift,
    up_weight,
    up_bias,
    down_weight,
    down_bias,
    ffn_gain,
    ffn_shift,
    random_blocks,
    cotangent,
):
    ny, nc, nz, nx = (lax.axis_size(a) for a in ALL)
    count, devices = nz * nx, ny * nc * nz * nx
    ranks = count // GROUPS
    half_ranks = ranks // 2
    _, tok, width = tokens.shape
    blocks = tok // BLK
    plan = Plan(count, ranks, blocks)
    z, x = lax.axis_index("z"), lax.axis_index("x")
    ctx_index = z * nx + x
    rank = lax.rem(ctx_index, ranks).astype(jnp.int32).reshape(1)
    where = jnp.stack([lax.axis_index("y"), lax.axis_index("core")]).astype(jnp.int32)
    rows = qkv_weight.shape[0]
    hidden = up_weight.shape[1]
    turns = hidden // width
    flat_tokens = tokens.reshape(tok, width)

    packed = packed_weights(out_weight, up_weight, down_weight, devices)
    packed = lax.all_gather(packed, ALL, axis=0, tiled=True)

    def by_index(values):
        grouped = values.reshape(values.shape[:-2] + (GROUPS, PER_GROUP, values.shape[-1]))
        pairs = [
            jnp.stack([grouped[..., 0 if r < half_ranks else 1, :], grouped[..., 2, :]], axis=-2)
            for r in range(ranks)
        ]
        return jnp.moveaxis(jnp.stack(pairs, axis=-3), (-4, -3), (0, 1)).reshape(
            (count,) + values.shape[:-2] + (2, values.shape[-1])
        )

    weight_rows = by_index(qkv_weight.reshape(rows, 3, H, HD)).reshape(count, rows, SPAN)
    picks = by_index(random_blocks[0].astype(bf16)).reshape(count, 1, -1)
    entries = picks.shape[2]
    small = jnp.concatenate(
        [
            query_bias,
            value_bias,
            out_bias,
            attn_gain,
            attn_shift,
            down_bias,
            ffn_gain,
            ffn_shift,
            up_bias,
        ]
    )
    many = small.shape[0] // rows
    extra = -(-(rows + 2) // 8) * 8
    sent = jnp.concatenate(
        [
            weight_rows,
            jnp.pad(picks, ((0, 0), (0, 0), (0, SPAN - entries))),
            jnp.broadcast_to(jnp.pad(small, (0, SPAN - small.shape[0])), (count, 1, SPAN)),
            jnp.zeros((count, extra - rows - 2, SPAN), bf16),
        ],
        axis=1,
    )
    near = [d for d in range(1, nz) if min(d, nz - d) == 1]
    held = {0: flat_tokens}
    over = {}
    for e in range(1, nx):
        over[0, e] = shifted(flat_tokens, "x", e)
    for d in near:
        held[d] = shifted(flat_tokens, "z", d)
    for d in range(2, nz - 1):
        held[d] = shifted(tied(flat_tokens, over[0, 1]), "z", d)
    line = swap(sent, CTX)
    shifts = [0] + near + [d for d in far_first(nz) if d not in near]
    order = [(d, e) for e in range(nx) for d in shifts]
    pieces = []
    for d, e in order:
        if e and d:
            over[d, e] = shifted(held[d], "x", e)
        pieces.append(over[d, e] if e else held[d])
    owners = jnp.stack(
        [lax.rem(z + nz - d, nz) * nx + lax.rem(x + nx - e, nx) for d, e in order]
    ).astype(jnp.int32)
    targets = jnp.stack(
        [lax.rem(z + d, nz) * nx + lax.rem(x + e, nx) for d, e in order]
    ).astype(jnp.int32)
    rand = line[:, rows, :entries].astype(jnp.int32).reshape(-1)
    seqs = ny * nc
    full = swap(
        tied(jnp.broadcast_to(line[None], (seqs,) + line.shape), over[0, 1], *(over[d, 1] for d in near), *held.values()), SEQ
    )
    columns = full[:, :, :rows].reshape(width, SPAN)
    vectors = full[:, :, rows + 1, : small.shape[0]].astype(f32)
    vectors = vectors.reshape(devices, many, rows).transpose(1, 0, 2).reshape(many, width)
    bias_table = by_index(
        jnp.stack([vectors[0], jnp.zeros_like(vectors[0]), vectors[1]]).reshape(3, H, HD)
    ).reshape(count, 1, SPAN)
    bias = lax.dynamic_index_in_dim(bias_table, ctx_index, 0, keepdims=False)

    kv = qkv_project(owners, pieces, columns, bias)
    attended, lse = attn_forward(plan, rand, rank, kv)
    back = swap(attended.reshape(count, tok, 128), CTX)

    output, resid, dout, attn_low, mid_low, act_low, down_low, pre_low, branch_low, sums = middle(
        ranks, back, flat_tokens, cotangent.reshape(tok, width), vectors, packed
    )

    first_keep, first_send = weight_grad(where, ny, (act_low, down_low), (attn_low, branch_low))
    second_keep, second_send = weight_grad(where, ny, (mid_low, pre_low))
    first_got = [shifted(part, "core", 1) for part in first_send]
    second_got = [shifted(part, "core", 1) for part in second_send]

    def terms_of(parts, d):
        at = lax.rem(x + d, nx)
        parts = [lax.dynamic_index_in_dim(part, at, part.ndim - 3, keepdims=False) for part in parts]
        return functools.reduce(jnp.add, [part.astype(f32) for part in parts])

    def by_y(pair, d):
        return [split(part[d], nz, nx) for part in pair]

    first_pair, second_pair = (first_keep, first_got), (second_keep, second_got)
    first_sent = [
        functools.reduce(jnp.add, [part.astype(f32) for part in by_y(first_pair, d)]).astype(bf16)
        for d in far_first(ny)
    ]
    second_sent = [
        jnp.stack([terms_of(by_y(second_pair, d), e) for d in range(ny)]).astype(bf16)
        for e in far_first(nx)
    ]

    dout = swap(tied(dout, *first_sent), CTX).reshape(plan.rows, 128)
    second_sent, dout = lax.optimization_barrier((second_sent, dout))
    grads = attn_backward(plan, rand, rank, kv, dout, lse, [])
    first_more, second_more = arrivals(first_sent, "y"), arrivals(second_sent, "x")

    def first_part(e, pair):
        return terms_of(by_y(pair, 0) + first_more, e)

    def second_part(d, pair):
        return plus(terms_of(by_y(pair, d), 0), [part[d] for part in second_more])

    first_late = tied(first_pair, grads)
    first_sent = [first_part(e, first_late).astype(bf16) for e in far_first(nx)]
    second_more = [tied(part, *first_sent) for part in second_more]
    second_late = tied(second_pair, *first_sent)
    second_sent = [second_part(d, second_late).astype(bf16) for d in far_first(ny)]
    terms = token_grads(count, targets, tied(grads, *first_sent, *second_sent), columns, [])
    first_next, second_next = arrivals(first_sent, "x"), arrivals(second_sent, "y")
    column_grads, bias_grads = qkv_grads(
        owners, pieces, tied(grads, terms[0], *first_next, *second_next), []
    )

    line = jnp.concatenate(
        [
            plus(first_part(0, tied(first_late, terms[0])), first_next).astype(bf16).transpose(1, 0, 2, 3),
            plus(second_part(0, tied(second_late, terms[0])), second_next).astype(bf16).transpose(1, 0, 2, 3),
        ],
        axis=1,
    )
    line = swap(line, "z")

    def over_x(d, *others):
        return [
            shifted(tied(terms[e * nz + shifts.index(d)], *others), "x", e) for e in range(1, nx)
        ]

    line_order = far_first(nz)
    total = added(
        [
            [tied(terms[shifts.index(d)], column_grads)] + over_x(d)
            for d in line_order
        ],
        [],
    )
    total = [tied(part, line) for part in total]
    line_got = [shifted(part, "z", d) for d, part in zip(line_order, total)]
    own = plus(terms[0].astype(f32), over_x(0, *total))
    tokens_grad = plus(resid + own, line_got).reshape(1, tok, width)

    listed = sums.shape[0]
    vector_sums = sums.reshape(listed, ny, nc, count, rows).transpose(1, 2, 3, 0, 4)
    vector_sums = vector_sums.reshape(ny, nc, nz, nx, 1, listed * rows).astype(bf16)
    units = -(-(rows + 2) // rows)
    table = jnp.concatenate(
        [
            tied(column_grads, total[0]).reshape(ny, nc, nz, nx, rows, SPAN),
            jnp.broadcast_to(bias_grads.astype(bf16), (ny, nc, nz, nx, 1, SPAN)),
            jnp.pad(vector_sums, ((0, 0),) * 5 + ((0, SPAN - listed * rows),)),
            jnp.zeros((ny, nc, nz, nx, units * rows - rows - 2, SPAN), bf16),
        ],
        axis=4,
    )
    table = summed(picked(table, "core", 1), "core")
    table = summed(picked(table, "y", 0), "y").astype(bf16)
    mine = picked(table, "x", 1)
    own, other = mine(0).astype(bf16), shifted(mine(1).astype(bf16), "x", 1)
    table = jnp.where(x == 0, jnp.stack([own, other], 2), jnp.stack([other, own], 2))

    table = swap(table.reshape(nz, units * rows, nx * SPAN), "z")
    weight_sums = jnp.sum(line.astype(f32), axis=0)
    down_grad = weight_sums[:turns].reshape(turns * rows, width)
    out_grad = weight_sums[turns]
    up_grad = weight_sums[turns + 1 :].transpose(1, 0, 2).reshape(rows, hidden)
    up_grad = reordered(up_grad, turns, devices)
    qkv_grad, column_sums, sums = table_grads(ranks, rows, table)
    shards = sums[:, : listed * rows].reshape(listed, rows)
    device = (lax.axis_index("y") * nc + lax.axis_index("core")) * count + ctx_index
    query_bias_grad = lax.dynamic_slice_in_dim(column_sums[0], device * rows, rows)
    value_bias_grad = lax.dynamic_slice_in_dim(column_sums[2], device * rows, rows)

    return (
        output.reshape(1, tok, width),
        tokens_grad,
        qkv_grad,
        query_bias_grad,
        value_bias_grad,
        out_grad,
        shards[0],
        shards[1],
        shards[2],
        up_grad,
        shards[6:].reshape(-1),
        down_grad,
        shards[3],
        shards[4],
        shards[5],
    )


def solution(mesh):
    dp, ctx = (mesh.shape[a] for a in ("dp", "ctx"))
    fine = Mesh(mesh.devices.reshape(dp // 2, 2, ctx // 2, 2), ALL)
    token_spec = P(SEQ, CTX, None)
    matrix, vector = P(ALL, None), P(ALL)
    return jax.shard_map(
        body,
        mesh=fine,
        in_specs=(
            token_spec,
            matrix,
            vector,
            vector,
            matrix,
            vector,
            vector,
            vector,
            matrix,
            vector,
            matrix,
            vector,
            vector,
            vector,
            P(SEQ, CTX, None, None),
            token_spec,
        ),
        out_specs=(
            token_spec,
            token_spec,
            matrix,
            vector,
            vector,
            matrix,
            vector,
            vector,
            vector,
            matrix,
            vector,
            matrix,
            vector,
            vector,
            vector,
        ),
        check_vma=False,
    )
```

```python
import functools

import jax
import jax.numpy as jnp
from jax import lax
from jax.experimental import pallas as pl
from jax.experimental.pallas import tpu as pltpu
from jax.sharding import Mesh, PartitionSpec as P

H = 12
HD = 64
BLK = 64
RAND = 3
GROUPS = 4
PER_GROUP = 3
SPAN = 3 * 2 * HD
VMEM_BYTES = 56 * 1024 * 1024

bf16 = jnp.bfloat16
f32 = jnp.float32

norm_eps = 1e-06
gelu_root = 0.7978845608028654
gelu_cubic = 0.044715

ALL = ("y", "core", "z", "x")
SEQ = ("y", "core")
CTX = ("z", "x")

VMEM = pl.BlockSpec(memory_space=pltpu.VMEM)
SMEM = pl.BlockSpec(memory_space=pltpu.SMEM)
ANY = pl.BlockSpec(memory_space=pl.ANY)


def call(kernel, name, out_shape, in_specs, out_specs, flops, moved, scratch=(), after=()):
    def ordered(*refs):
        kernel(*refs[len(after) :])

    built = pl.pallas_call(
        ordered,
        out_shape=out_shape,
        in_specs=[ANY] * len(after) + in_specs,
        out_specs=out_specs,
        scratch_shapes=scratch,
        cost_estimate=pl.CostEstimate(flops=flops, bytes_accessed=moved, transcendentals=0),
        compiler_params=pltpu.CompilerParams(vmem_limit_bytes=VMEM_BYTES),
        name=name,
    )
    return functools.partial(built, *after)


def tied(value, *others):
    return lax.optimization_barrier((value,) + others)[0]


def shape(dims, kind):
    return jax.ShapeDtypeStruct(dims, kind)


def contract_rows(left_side, right_side):
    return lax.dot_general(
        left_side, right_side, (((0,), (0,)), ((), ())), preferred_element_type=f32
    )


def contract_cols(left_side, right_side):
    return lax.dot_general(
        left_side, right_side, (((1,), (1,)), ((), ())), preferred_element_type=f32
    )


def plain(left_side, right_side):
    return jnp.dot(left_side, right_side, preferred_element_type=f32)


def heads_of(index, ranks):
    group, rank = index // ranks, index % ranks
    first = PER_GROUP * group + (0 if rank < ranks // 2 else 1)
    return first, PER_GROUP * group + 2


def qkv_kernel(count, owner_ref, *refs):
    x_refs, w_ref, b_ref, out_ref = refs[:count], refs[count], refs[count + 1], refs[count + 2]
    tok = x_refs[0].shape[0]
    for k in range(count):
        rows = plain(x_refs[k][...], w_ref[...]) + b_ref[...]
        at = pl.ds(pl.multiple_of(owner_ref[k] * tok, BLK), tok)
        out_ref[at, :] = rows.astype(bf16)


def qkv_project(owners, pieces, weights, bias):
    count = len(pieces)
    tok, width = pieces[0].shape
    return call(
        functools.partial(qkv_kernel, count),
        "qkv_project",
        shape((count * tok, SPAN), bf16),
        [SMEM] + [VMEM] * (count + 2),
        VMEM,
        2 * count * tok * width * SPAN,
        4 * count * tok * width,
    )(owners, *pieces, weights, bias)


def token_grad_kernel(count, owner_ref, grad_ref, w_ref, *out_refs):
    tok = out_refs[0].shape[0]
    for k in range(count):
        at = pl.ds(pl.multiple_of(owner_ref[k] * tok, BLK), tok)
        out_refs[k][...] = contract_cols(grad_ref[at, :], w_ref[...]).astype(bf16)


def token_grads(count, owners, grads, weights, after):
    tok, width = grads.shape[0] // count, weights.shape[0]
    return call(
        functools.partial(token_grad_kernel, count),
        "token_grads",
        [shape((tok, width), bf16)] * count,
        [SMEM, VMEM, VMEM],
        [VMEM] * count,
        2 * count * tok * width * SPAN,
        4 * count * tok * width,
        after=after,
    )(owners, grads, weights)


def add_kernel(counts, *refs):
    at = sum(counts)
    for k, n in enumerate(counts):
        parts = [ref[...].astype(f32) for ref in refs[sum(counts[:k]) : sum(counts[: k + 1])]]
        refs[at + k][...] = functools.reduce(jnp.add, parts).astype(bf16)


def added(groups, after):
    counts = [len(group) for group in groups]
    size = groups[0][0].size
    return call(
        functools.partial(add_kernel, counts),
        "added",
        [shape(group[0].shape, bf16) for group in groups],
        [VMEM] * sum(counts),
        [VMEM] * len(groups),
        size * sum(counts),
        2 * size * sum(counts),
        after=after,
    )(*[part for group in groups for part in group])


def qkv_grad_kernel(count, owner_ref, *refs):
    x_refs, grad_ref, out_ref, bias_ref = refs[:count], refs[count], refs[count + 1], refs[count + 2]
    tok = x_refs[0].shape[0]
    total = None
    for k in range(count):
        at = pl.ds(pl.multiple_of(owner_ref[k] * tok, BLK), tok)
        part = contract_rows(x_refs[k][...], grad_ref[at, :])
        total = part if total is None else total + part
    out_ref[...] = total.astype(bf16)
    bias_ref[...] = jnp.sum(grad_ref[...].astype(f32), axis=0, keepdims=True)


def qkv_grads(owners, pieces, grads, after):
    count = len(pieces)
    tok, width = pieces[0].shape
    return call(
        functools.partial(qkv_grad_kernel, count),
        "qkv_grads",
        [shape((width, SPAN), bf16), shape((1, SPAN), f32)],
        [SMEM] + [VMEM] * (count + 1),
        [VMEM, VMEM],
        2 * count * tok * width * SPAN,
        4 * count * tok * width,
        after=after,
    )(owners, *pieces, grads)


class Plan:
    def __init__(self, count, ranks, blocks):
        self.count, self.ranks, self.blocks = count, ranks, blocks
        self.steps = (ranks // 2, ranks)
        self.owners = (count // self.steps[0], count // self.steps[1])
        self.total = count * blocks
        self.units = (self.owners[0] + self.owners[1]) * blocks
        self.rows = self.total * BLK
        self.chunk = min(self.rows, 2048)

    def at(self, block):
        return pl.ds(pl.multiple_of(block * BLK, BLK), BLK)

    def unit(self, half, turn, inner):
        return (half * self.owners[0] + turn) * self.blocks + inner

    def named(self, half, block, rand_ref):
        ids = [
            jnp.maximum(block - 1, 0),
            block,
            jnp.minimum(block + 1, self.total - 1),
            0,
            self.total - 1,
        ]
        for t in range(RAND):
            ids.append(rand_ref[(block * 2 + half) * RAND + t])
        return ids

    def flops(self, products):
        return 2 * products * self.units * BLK * 128 * 8 * BLK


def only_half(values, half):
    lane = lax.broadcasted_iota(jnp.int32, values.shape, 1)
    return jnp.where((lane < HD) == (half == 0), values, jnp.zeros_like(values))


def attn_forward_kernel(plan, rand_ref, rank_ref, kv_ref, out_ref, lse_ref):
    rank = rank_ref[0]
    out_ref[...] = jnp.zeros_like(out_ref)

    def emit(half, block, unit, attended, lse):
        out_ref[plan.at(block), half * HD : (half + 1) * HD] = attended[
            :, half * HD : (half + 1) * HD
        ].astype(bf16)
        lse_ref[plan.at(unit), :] = jnp.broadcast_to(lse, (BLK, 128))

    def query(half, block):
        return only_half(kv_ref[plan.at(block), 0:128], half) * 0.125

    for half in range(2):
        step = plan.steps[half]
        offset = lax.rem(rank, step) if step > 1 else 0

        def turn_body(turn, carry, half=half, step=step, offset=offset):
            inners = range(2 * plan.blocks)
            listed = [
                ((2 * turn + i // plan.blocks) * step + offset) * plan.blocks + i % plan.blocks
                for i in inners
            ]
            named = [plan.named(half, block, rand_ref) for block in listed]
            scores = []
            for inner, ids in zip(inners, named):
                keys = jnp.concatenate([kv_ref[plan.at(i), 128:256] for i in ids], axis=0)
                scores.append(contract_cols(query(half, listed[inner]), keys))
            probs, lses = [], []
            for part in scores:
                top = jnp.max(part, axis=-1, keepdims=True)
                grown = jnp.exp(part - top)
                total = jnp.sum(grown, axis=-1, keepdims=True)
                probs.append((grown * (1.0 / total)).astype(bf16))
                lses.append(top + jnp.log(total))
            for inner, ids in zip(inners, named):
                values = jnp.concatenate([kv_ref[plan.at(i), 256:384] for i in ids], axis=0)
                attended = plain(probs[inner], values)
                block = listed[inner]
                emit(half, block, plan.unit(half, 2 * turn, inner), attended, lses[inner])
            return carry

        lax.fori_loop(0, plan.owners[half] // 2, turn_body, 0)

    chunks = [pl.ds(c, plan.chunk) for c in range(0, plan.rows, plan.chunk)]
    for half in range(2):
        step = plan.steps[half]
        for block in (0, plan.total - 1):
            owner = block // plan.blocks

            def whole(half=half, step=step, owner=owner, block=block):
                q = query(half, block)
                scores = [contract_cols(q, kv_ref[c, 128:256]) for c in chunks]
                tops = [jnp.max(s, axis=-1, keepdims=True) for s in scores]
                top = functools.reduce(jnp.maximum, tops)
                grown = [jnp.exp(s - top) for s in scores]
                total = sum(jnp.sum(e, axis=-1, keepdims=True) for e in grown)
                scale = 1.0 / total
                attended = sum(
                    plain((e * scale).astype(bf16), kv_ref[c, 256:384])
                    for e, c in zip(grown, chunks)
                )
                unit = plan.unit(half, owner // step, block % plan.blocks)
                emit(half, block, unit, attended, top + jnp.log(total))

            if step == 1:
                whole()
            else:
                pl.when(lax.rem(rank, step) == owner % step)(whole)


def attn_forward(plan, rand, rank, kv):
    return call(
        functools.partial(attn_forward_kernel, plan),
        "attn_forward",
        (shape((plan.rows, 128), bf16), shape((plan.units * BLK, 128), f32)),
        [SMEM, SMEM, VMEM],
        (VMEM, VMEM),
        plan.flops(2),
        8 * plan.rows * 128,
    )(rand, rank, kv)


def attn_backward_kernel(
    plan, rand_ref, rank_ref, kv_ref, dout_ref, lse_ref, out_ref, sum_ref
):
    rank = rank_ref[0]
    out_ref[:, 0:128] = jnp.zeros((plan.rows, 128), bf16)
    sum_ref[...] = jnp.zeros_like(sum_ref)

    def operands(half, block, unit):
        q = only_half(kv_ref[plan.at(block), 0:128], half) * 0.125
        dout = only_half(dout_ref[plan.at(block), :], half)
        return q, dout, lse_ref[plan.at(unit), :][:, 0:1]

    def emit(half, block, grad_query):
        out_ref[plan.at(block), half * HD : (half + 1) * HD] = (
            grad_query[:, half * HD : (half + 1) * HD] * 0.125
        ).astype(bf16)

    for half in range(2):
        step = plan.steps[half]
        offset = lax.rem(rank, step) if step > 1 else 0

        def turn_body(turn, carry, half=half, step=step, offset=offset):
            inners = range(2 * plan.blocks)
            listed = [
                ((2 * turn + i // plan.blocks) * step + offset) * plan.blocks + i % plan.blocks
                for i in inners
            ]
            named = [plan.named(half, block, rand_ref) for block in listed]
            given, scores, grad_probs = [], [], []
            for inner, ids in zip(inners, named):
                block = listed[inner]
                q, dout, lse = operands(half, block, plan.unit(half, 2 * turn, inner))
                if inner % plan.blocks in (0, plan.blocks - 1):
                    edge = (block == 0) | (block == plan.total - 1)
                    dout = dout * jnp.where(edge, 0.0, 1.0).astype(bf16)
                given.append((q, dout, lse))
                keys = jnp.concatenate([kv_ref[plan.at(i), 128:256] for i in ids], axis=0)
                scores.append(contract_cols(q, keys))
            for inner, ids in zip(inners, named):
                values = jnp.concatenate([kv_ref[plan.at(i), 256:384] for i in ids], axis=0)
                grad_probs.append(contract_cols(given[inner][1], values))
            low_probs, grad_scores = [], []
            for inner in inners:
                probs = jnp.exp(scores[inner] - given[inner][2])
                delta = jnp.sum(probs * grad_probs[inner], axis=-1, keepdims=True)
                grad_scores.append((probs * (grad_probs[inner] - delta)).astype(bf16))
                low_probs.append(probs.astype(bf16))
            for inner, ids in zip(inners, named):
                keys = jnp.concatenate([kv_ref[plan.at(i), 128:256] for i in ids], axis=0)
                emit(half, listed[inner], plain(grad_scores[inner], keys))
            grad_keys = [contract_rows(grad_scores[i], given[i][0]) for i in inners]
            grad_values = [contract_rows(low_probs[i], given[i][1]) for i in inners]
            for inner, ids in zip(inners, named):
                for t, i in enumerate(ids):
                    sum_ref[plan.at(i), 0:128] += grad_keys[inner][t * BLK : (t + 1) * BLK]
                    sum_ref[plan.at(i), 128:256] += grad_values[inner][t * BLK : (t + 1) * BLK]
            return carry

        lax.fori_loop(0, plan.owners[half] // 2, turn_body, 0)

    chunks = [pl.ds(c, plan.chunk) for c in range(0, plan.rows, plan.chunk)]
    for half in range(2):
        step = plan.steps[half]
        for block in (0, plan.total - 1):
            owner = block // plan.blocks

            def whole(half=half, step=step, owner=owner, block=block):
                unit = plan.unit(half, owner // step, block % plan.blocks)
                q, dout, lse = operands(half, block, unit)
                probs = [jnp.exp(contract_cols(q, kv_ref[c, 128:256]) - lse) for c in chunks]
                grad_probs = [contract_cols(dout, kv_ref[c, 256:384]) for c in chunks]
                delta = sum(
                    jnp.sum(p * g, axis=-1, keepdims=True) for p, g in zip(probs, grad_probs)
                )
                grad_query = jnp.zeros((BLK, 128), f32)
                for p, g, c in zip(probs, grad_probs, chunks):
                    grad_scores = (p * (g - delta)).astype(bf16)
                    sum_ref[c, 0:128] += contract_rows(grad_scores, q)
                    sum_ref[c, 128:256] += contract_rows(p.astype(bf16), dout)
                    grad_query += plain(grad_scores, kv_ref[c, 128:256])
                emit(half, block, grad_query)

            if step == 1:
                whole()
            else:
                pl.when(lax.rem(rank, step) == owner % step)(whole)

    out_ref[:, 128:384] = sum_ref[...].astype(bf16)


def attn_backward(plan, rand, rank, kv, dout, lse, after):
    return call(
        functools.partial(attn_backward_kernel, plan),
        "attn_backward",
        shape((plan.rows, SPAN), bf16),
        [SMEM, SMEM, VMEM, VMEM, VMEM],
        VMEM,
        plan.flops(5),
        16 * plan.rows * 128,
        [pltpu.VMEM((plan.rows, 256), f32)],
        after,
    )(rand, rank, kv, dout, lse)


def table_kernel(ranks, rows, table_ref, grad_ref, bias_ref, sums_ref):
    nz, width = table_ref.shape[0], table_ref.shape[2]
    nx = width // SPAN
    tiles = [
        table_ref[k // nx][:, k % nx * SPAN : (k % nx + 1) * SPAN].astype(f32)
        for k in range(nz * nx)
    ]
    sums_ref[...] = functools.reduce(jnp.add, [tile[rows + 1 : rows + 2] for tile in tiles])
    for part in range(3):
        heads = []
        for g in range(GROUPS):
            own = [tiles[g * ranks + r][:, part * 128 : part * 128 + HD] for r in range(ranks)]
            shared = [tiles[g * ranks + r][:, part * 128 + HD : (part + 1) * 128] for r in range(ranks)]
            for group in (own[: ranks // 2], own[ranks // 2 :], shared):
                heads.append(functools.reduce(jnp.add, group))
        whole = jnp.concatenate(heads, axis=1)
        grad_ref[:, part * H * HD : (part + 1) * H * HD] = whole[0:rows]
        bias_ref[part : part + 1, :] = whole[rows : rows + 1]


def table_grads(ranks, rows, table):
    return call(
        functools.partial(table_kernel, ranks, rows),
        "table_grads",
        [shape((rows, 3 * H * HD), f32), shape((3, H * HD), f32), shape((1, SPAN), f32)],
        [VMEM],
        [VMEM] * 3,
        table.size,
        2 * table.size,
    )(table)


def reorder_kernel(outer, inner, rows, in_ref, out_ref):
    value = in_ref[...].astype(f32)
    out_ref[...] = jnp.concatenate(
        [
            value[:, (o * inner + i) * rows : (o * inner + i + 1) * rows]
            for i in range(inner)
            for o in range(outer)
        ],
        axis=1,
    ).astype(out_ref.dtype)


def reordered(value, outer, inner):
    rows, cols = value.shape
    run = cols // (outer * inner)
    if run < 8:
        return value.reshape(rows, outer, inner, run).transpose(0, 2, 1, 3).reshape(rows, cols)
    return call(
        functools.partial(reorder_kernel, outer, inner, run),
        "reorder",
        shape((rows, cols), value.dtype),
        [VMEM],
        VMEM,
        rows * cols,
        4 * rows * cols,
    )(value)


def pack_kernel(outer, inner, out_w_ref, up_ref, down_ref, packed_ref):
    rows, width = out_w_ref.shape
    packed_ref[:, 0:width] = out_w_ref[...]
    up = up_ref[...].astype(f32)
    down = down_ref[...].astype(f32)
    for i in range(inner):
        packed_ref[:, (1 + i) * width : (2 + i) * width] = jnp.concatenate(
            [
                up[:, (o * inner + i) * rows : (o * inner + i + 1) * rows]
                for o in range(outer)
            ],
            axis=1,
        ).astype(bf16)
        packed_ref[:, (1 + inner + i) * width : (2 + inner + i) * width] = down[
            i * rows : (i + 1) * rows
        ].astype(bf16)


def packed_weights(out_weight, up_weight, down_weight, devices):
    rows, width = out_weight.shape
    turns = up_weight.shape[1] // width
    if rows < 8:
        up = reordered(up_weight, devices, turns)
        down = down_weight.reshape(turns, rows, width).transpose(1, 0, 2)
        return jnp.concatenate([out_weight, up, down.reshape(rows, turns * width)], axis=1)
    return call(
        functools.partial(pack_kernel, devices, turns),
        "packed_weights",
        shape((rows, (1 + 2 * turns) * width), bf16),
        [VMEM] * 3,
        VMEM,
        rows * width,
        rows * width,
    )(out_weight, up_weight, down_weight)


def normalized(values):
    center = values - jnp.mean(values, axis=-1, keepdims=True)
    spread = jnp.mean(center * center, axis=-1, keepdims=True)
    scale = lax.rsqrt(spread + norm_eps)
    return center * scale, scale


def normalized_grad(normal, scale, grad):
    return scale * (
        grad
        - jnp.mean(grad, axis=-1, keepdims=True)
        - normal * jnp.mean(grad * normal, axis=-1, keepdims=True)
    )


def column_sum(values):
    return jnp.sum(values.astype(f32), axis=0, keepdims=True)


def middle_kernel(
    ranks,
    back_ref,
    tok_ref,
    cot_ref,
    vec_ref,
    pack_ref,
    output_ref,
    resid_ref,
    dout_ref,
    attn_ref,
    mid_ref,
    act_ref,
    down_ref,
    pre_ref,
    branch_ref,
    sums_ref,
    out_w,
    up_w,
    down_w,
    slope_ref,
    sems,
):
    count = back_ref.shape[0]
    width = tok_ref.shape[1]
    turns = up_w.shape[1] // width
    half_ranks = ranks // 2

    copies = [pltpu.make_async_copy(pack_ref.at[:, pl.ds(0, width)], out_w, sems.at[0])]
    for t in range(turns):
        cols = pl.ds(t * width, width)
        copies.append(
            pltpu.make_async_copy(
                pack_ref.at[:, pl.ds((1 + t) * width, width)], up_w.at[:, cols], sems.at[1 + t]
            )
        )
        copies.append(
            pltpu.make_async_copy(
                pack_ref.at[:, pl.ds((1 + turns + t) * width, width)],
                down_w.at[t],
                sems.at[1 + turns + t],
            )
        )
    for copy in copies:
        copy.start()

    for g in range(GROUPS):
        own = [back_ref[g * ranks + r][:, 0:HD] for r in range(ranks)]
        shared = [back_ref[g * ranks + r][:, HD : 2 * HD] for r in range(ranks)]
        trio = [sum(own[1:half_ranks], own[0]), sum(own[half_ranks + 1 :], own[half_ranks])]
        trio.append(sum(shared[1:], shared[0]))
        attn_ref[:, g * PER_GROUP * HD : (g + 1) * PER_GROUP * HD] = jnp.concatenate(trio, axis=1)

    out_bias, attn_gain, attn_shift, down_bias, ffn_gain, ffn_shift = (
        vec_ref[k : k + 1, :] for k in range(2, 8)
    )
    copies[0].wait()
    branch = plain(attn_ref[...], out_w[...]) + out_bias
    normal, scale = normalized(tok_ref[...].astype(f32) + branch)
    mid = normal * attn_gain + attn_shift
    mid_low = mid.astype(bf16)
    mid_ref[...] = mid_low
    final = mid + down_bias
    for t in range(turns):
        cols = slice(t * width, (t + 1) * width)
        copies[1 + 2 * t].wait()
        pre = plain(mid_low, up_w[:, cols]) + vec_ref[8 + t : 9 + t, :]
        square = pre * pre
        bend = jnp.tanh(gelu_root * (pre + gelu_cubic * pre * square))
        rise = 0.5 * (1.0 + bend)
        slope_ref[:, cols] = rise + 0.5 * pre * (1.0 - bend * bend) * (
            gelu_root * (1.0 + 3.0 * gelu_cubic * square)
        )
        act = (pre * rise).astype(bf16)
        act_ref[:, cols] = act
        copies[2 + 2 * t].wait()
        final = final + plain(act, down_w[t])
    normal_two, scale_two = normalized(final)
    output_ref[...] = (normal_two * ffn_gain + ffn_shift).astype(bf16)
    cot = cot_ref[...].astype(f32)
    sums_ref[4:5, :] = column_sum(cot * normal_two)
    sums_ref[5:6, :] = column_sum(cot)
    grad_final = normalized_grad(normal_two, scale_two, cot * ffn_gain)
    down_low = grad_final.astype(bf16)
    down_ref[...] = down_low
    sums_ref[3:4, :] = column_sum(down_low)
    grad_mid = grad_final
    for t in range(turns):
        cols = slice(t * width, (t + 1) * width)
        grad_pre = (contract_cols(down_low, down_w[t]) * slope_ref[:, cols]).astype(bf16)
        pre_ref[:, cols] = grad_pre
        sums_ref[6 + t : 7 + t, :] = column_sum(grad_pre)
        grad_mid = grad_mid + contract_cols(grad_pre, up_w[:, cols])
    sums_ref[1:2, :] = column_sum(grad_mid * normal)
    sums_ref[2:3, :] = column_sum(grad_mid)
    resid = normalized_grad(normal, scale, grad_mid * attn_gain)
    resid_ref[...] = resid
    branch_low = resid.astype(bf16)
    branch_ref[...] = branch_low
    sums_ref[0:1, :] = column_sum(branch_low)
    grad_attn = contract_cols(branch_low, out_w[...]).astype(bf16)
    for j in range(count):
        first, shared = heads_of(j, ranks)
        dout_ref[j] = jnp.concatenate(
            [
                grad_attn[:, first * HD : (first + 1) * HD],
                grad_attn[:, shared * HD : (shared + 1) * HD],
            ],
            axis=1,
        )


def middle(ranks, back, tokens, cotangent, vectors, packed):
    count, (tok, width) = back.shape[0], tokens.shape
    turns = vectors.shape[0] - 8
    hidden = turns * width
    return call(
        functools.partial(middle_kernel, ranks),
        "middle",
        [
            shape((tok, width), bf16),
            shape((tok, width), f32),
            shape((count, tok, 128), bf16),
            shape((tok, width), bf16),
            shape((tok, width), bf16),
            shape((tok, hidden), bf16),
            shape((tok, width), bf16),
            shape((tok, hidden), bf16),
            shape((tok, width), bf16),
            shape((6 + turns, width), f32),
        ],
        [VMEM] * 4 + [ANY],
        [VMEM] * 10,
        4 * tok * width * (width + 2 * hidden),
        2 * width * (width + 2 * hidden),
        [
            pltpu.VMEM((width, width), bf16),
            pltpu.VMEM((width, hidden), bf16),
            pltpu.VMEM((turns, width, width), bf16),
            pltpu.VMEM((tok, hidden), f32),
            pltpu.SemaphoreType.DMA((1 + 2 * turns,)),
        ],
    )(back, tokens, cotangent, vectors, packed)


def weight_grad_kernel(pairs, where_ref, *refs):
    operands, outs, total_ref = refs[: 2 * len(pairs)], refs[2 * len(pairs) : -1], refs[-1]
    turn = pl.program_id(0)
    first = 0
    for k, turns in enumerate(pairs):

        def product(left_ref=operands[2 * k], right_ref=operands[2 * k + 1]):
            total_ref[...] = contract_rows(left_ref[...], right_ref[...])

        pl.when((turn >= first) & (turn < first + turns))(product)
        first += turns
    ny = len(outs) // 2
    rows = total_ref.shape[0] // (2 * ny)
    mine, core = where_ref[0], where_ref[1]
    for d in range(ny):
        base = lax.rem(mine + d, ny) * 2
        for ref, c in ((outs[d], core), (outs[ny + d], 1 - core)):
            ref[0] = total_ref[pl.ds(pl.multiple_of((base + c) * rows, 16), rows), :].astype(bf16)


def weight_grad(where, ny, *pairs):
    tok = pairs[0][0].shape[0]
    width = min(min(left.shape[1], right.shape[1]) for left, right in pairs)
    counts, specs, first = [], [], 0
    for pair in pairs:
        turns = max(operand.shape[1] for operand in pair) // width
        for operand in pair:
            if operand.shape[1] == width:
                specs.append(pl.BlockSpec((tok, width), lambda t: (0, 0)))
            else:
                specs.append(
                    pl.BlockSpec(
                        (tok, width),
                        lambda t, first=first, turns=turns: (0, jnp.clip(t - first, 0, turns - 1)),
                    )
                )
        counts.append(turns)
        first += turns
    rows = width // (2 * ny)
    parts = pl.pallas_call(
        functools.partial(weight_grad_kernel, counts),
        grid=(first,),
        out_shape=[shape((first, rows, width), bf16)] * (2 * ny),
        in_specs=[SMEM] + specs,
        out_specs=[pl.BlockSpec((1, rows, width), lambda t: (t, 0, 0))] * (2 * ny),
        scratch_shapes=[pltpu.VMEM((width, width), f32)],
        cost_estimate=pl.CostEstimate(
            flops=2 * tok * width * width * first,
            bytes_accessed=2 * width * width * first,
            transcendentals=0,
        ),
        compiler_params=pltpu.CompilerParams(vmem_limit_bytes=VMEM_BYTES),
        name="weight_grad",
    )(where, *[operand for pair in pairs for operand in pair])
    return parts[:ny], parts[ny:]


def swap(value, axis):
    return lax.all_to_all(value, axis, split_axis=0, concat_axis=0, tiled=True)


def shifted(value, axis, by):
    size = lax.axis_size(axis)
    return lax.ppermute(value, axis, [(i, (i + by) % size) for i in range(size)])


def far_first(size):
    return sorted(range(1, size), key=lambda d: -min(d, size - d))


def picked(value, axis, dim):
    size, here = lax.axis_size(axis), lax.axis_index(axis)

    def part(d):
        return lax.dynamic_index_in_dim(
            value, lax.rem(here + d, size), dim, keepdims=False
        ).astype(f32)

    return part


def split(value, nz, nx):
    return value.reshape(value.shape[:-2] + (nz, nx, value.shape[-2] // (nz * nx), value.shape[-1]))


def along_y(value):
    return lambda d: value[d]


def along_x(value):
    return picked(value, "x", value.ndim - 3)


def sends(parts, size):
    return [parts(d).astype(bf16) for d in far_first(size)]


def arrivals(sent, axis):
    return [shifted(part, axis, d) for d, part in zip(far_first(len(sent) + 1), sent)]


def plus(kept, got):
    return functools.reduce(lambda total, part: total + part.astype(f32), got, kept)


def summed(parts, axis):
    return plus(parts(0), arrivals(sends(parts, lax.axis_size(axis)), axis))


def body(
    tokens,
    qkv_weight,
    query_bias,
    value_bias,
    out_weight,
    out_bias,
    attn_gain,
    attn_shift,
    up_weight,
    up_bias,
    down_weight,
    down_bias,
    ffn_gain,
    ffn_shift,
    random_blocks,
    cotangent,
):
    ny, nc, nz, nx = (lax.axis_size(a) for a in ALL)
    count, devices = nz * nx, ny * nc * nz * nx
    ranks = count // GROUPS
    half_ranks = ranks // 2
    _, tok, width = tokens.shape
    blocks = tok // BLK
    plan = Plan(count, ranks, blocks)
    z, x = lax.axis_index("z"), lax.axis_index("x")
    ctx_index = z * nx + x
    rank = lax.rem(ctx_index, ranks).astype(jnp.int32).reshape(1)
    where = jnp.stack([lax.axis_index("y"), lax.axis_index("core")]).astype(jnp.int32)
    rows = qkv_weight.shape[0]
    hidden = up_weight.shape[1]
    turns = hidden // width
    flat_tokens = tokens.reshape(tok, width)

    packed = packed_weights(out_weight, up_weight, down_weight, devices)
    packed = lax.all_gather(packed, ALL, axis=0, tiled=True)

    def by_index(values):
        grouped = values.reshape(values.shape[:-2] + (GROUPS, PER_GROUP, values.shape[-1]))
        pairs = [
            jnp.stack([grouped[..., 0 if r < half_ranks else 1, :], grouped[..., 2, :]], axis=-2)
            for r in range(ranks)
        ]
        return jnp.moveaxis(jnp.stack(pairs, axis=-3), (-4, -3), (0, 1)).reshape(
            (count,) + values.shape[:-2] + (2, values.shape[-1])
        )

    weight_rows = by_index(qkv_weight.reshape(rows, 3, H, HD)).reshape(count, rows, SPAN)
    picks = by_index(random_blocks[0].astype(bf16)).reshape(count, 1, -1)
    entries = picks.shape[2]
    small = jnp.concatenate(
        [
            query_bias,
            value_bias,
            out_bias,
            attn_gain,
            attn_shift,
            down_bias,
            ffn_gain,
            ffn_shift,
            up_bias,
        ]
    )
    many = small.shape[0] // rows
    extra = -(-(rows + 2) // 8) * 8
    sent = jnp.concatenate(
        [
            weight_rows,
            jnp.pad(picks, ((0, 0), (0, 0), (0, SPAN - entries))),
            jnp.broadcast_to(jnp.pad(small, (0, SPAN - small.shape[0])), (count, 1, SPAN)),
            jnp.zeros((count, extra - rows - 2, SPAN), bf16),
        ],
        axis=1,
    )
    near = [d for d in range(1, nz) if min(d, nz - d) == 1]
    held = {0: flat_tokens}
    over = {}
    for e in range(1, nx):
        over[0, e] = shifted(flat_tokens, "x", e)
    for d in near:
        held[d] = shifted(flat_tokens, "z", d)
    for d in range(2, nz - 1):
        held[d] = shifted(tied(flat_tokens, over[0, 1]), "z", d)
    line = swap(sent, CTX)
    shifts = [0] + near + [d for d in far_first(nz) if d not in near]
    order = [(d, e) for e in range(nx) for d in shifts]
    pieces = []
    for d, e in order:
        if e and d:
            over[d, e] = shifted(held[d], "x", e)
        pieces.append(over[d, e] if e else held[d])
    owners = jnp.stack(
        [lax.rem(z + nz - d, nz) * nx + lax.rem(x + nx - e, nx) for d, e in order]
    ).astype(jnp.int32)
    targets = jnp.stack(
        [lax.rem(z + d, nz) * nx + lax.rem(x + e, nx) for d, e in order]
    ).astype(jnp.int32)
    rand = line[:, rows, :entries].astype(jnp.int32).reshape(-1)
    seqs = ny * nc
    full = swap(
        tied(jnp.broadcast_to(line[None], (seqs,) + line.shape), over[0, 1], *(over[d, 1] for d in near), *held.values()), SEQ
    )
    columns = full[:, :, :rows].reshape(width, SPAN)
    vectors = full[:, :, rows + 1, : small.shape[0]].astype(f32)
    vectors = vectors.reshape(devices, many, rows).transpose(1, 0, 2).reshape(many, width)
    bias_table = by_index(
        jnp.stack([vectors[0], jnp.zeros_like(vectors[0]), vectors[1]]).reshape(3, H, HD)
    ).reshape(count, 1, SPAN)
    bias = lax.dynamic_index_in_dim(bias_table, ctx_index, 0, keepdims=False)

    kv = qkv_project(owners, pieces, columns, bias)
    attended, lse = attn_forward(plan, rand, rank, kv)
    back = swap(attended.reshape(count, tok, 128), CTX)

    output, resid, dout, attn_low, mid_low, act_low, down_low, pre_low, branch_low, sums = middle(
        ranks, back, flat_tokens, cotangent.reshape(tok, width), vectors, packed
    )

    first_keep, first_send = weight_grad(where, ny, (act_low, down_low), (attn_low, branch_low))
    second_keep, second_send = weight_grad(where, ny, (mid_low, pre_low))
    first_got = [shifted(part, "core", 1) for part in first_send]
    second_got = [shifted(part, "core", 1) for part in second_send]

    def terms_of(parts, d):
        at = lax.rem(x + d, nx)
        parts = [lax.dynamic_index_in_dim(part, at, part.ndim - 3, keepdims=False) for part in parts]
        return functools.reduce(jnp.add, [part.astype(f32) for part in parts])

    def by_y(pair, d):
        return [split(part[d], nz, nx) for part in pair]

    first_pair, second_pair = (first_keep, first_got), (second_keep, second_got)
    first_sent = [
        functools.reduce(jnp.add, [part.astype(f32) for part in by_y(first_pair, d)]).astype(bf16)
        for d in far_first(ny)
    ]
    second_sent = [
        jnp.stack([terms_of(by_y(second_pair, d), e) for d in range(ny)]).astype(bf16)
        for e in far_first(nx)
    ]

    dout = swap(tied(dout, *first_sent), CTX).reshape(plan.rows, 128)
    second_sent, dout = lax.optimization_barrier((second_sent, dout))
    grads = attn_backward(plan, rand, rank, kv, dout, lse, [])
    first_more, second_more = arrivals(first_sent, "y"), arrivals(second_sent, "x")

    def first_part(e, pair):
        return terms_of(by_y(pair, 0) + first_more, e)

    def second_part(d, pair):
        return plus(terms_of(by_y(pair, d), 0), [part[d] for part in second_more])

    first_late = tied(first_pair, grads)
    first_sent = [first_part(e, first_late).astype(bf16) for e in far_first(nx)]
    second_more = [tied(part, *first_sent) for part in second_more]
    second_late = tied(second_pair, *first_sent)
    second_sent = [second_part(d, second_late).astype(bf16) for d in far_first(ny)]
    terms = token_grads(count, targets, tied(grads, *first_sent, *second_sent), columns, [])
    first_next, second_next = arrivals(first_sent, "x"), arrivals(second_sent, "y")
    column_grads, bias_grads = qkv_grads(
        owners, pieces, tied(grads, terms[0], *first_next, *second_next), []
    )

    def over_x(d, *others):
        return [
            shifted(tied(terms[e * nz + shifts.index(d)], *others), "x", e) for e in range(1, nx)
        ]

    line_order = far_first(nz)
    across = {d: over_x(d) for d in line_order}

    line = jnp.concatenate(
        [
            plus(first_part(0, tied(first_late, terms[0])), first_next).astype(bf16).transpose(1, 0, 2, 3),
            plus(second_part(0, tied(second_late, terms[0])), second_next).astype(bf16).transpose(1, 0, 2, 3),
        ],
        axis=1,
    )
    line = swap(tied(line, *across[line_order[0]]), "z")

    total = added(
        [
            [tied(terms[shifts.index(d)], column_grads)] + across[d]
            for d in line_order
        ],
        [],
    )
    early = total[0]
    total = [tied(part, line) for part in total]
    line_got = [shifted(part, "z", d) for d, part in zip(line_order, total)]
    own = plus(terms[0].astype(f32), over_x(0, *total))
    tokens_grad = plus(resid + own, line_got).reshape(1, tok, width)

    listed = sums.shape[0]
    vector_sums = sums.reshape(listed, ny, nc, count, rows).transpose(1, 2, 3, 0, 4)
    vector_sums = vector_sums.reshape(ny, nc, nz, nx, 1, listed * rows).astype(bf16)
    units = -(-(rows + 2) // rows)
    table = jnp.concatenate(
        [
            tied(column_grads, early).reshape(ny, nc, nz, nx, rows, SPAN),
            jnp.broadcast_to(bias_grads.astype(bf16), (ny, nc, nz, nx, 1, SPAN)),
            jnp.pad(vector_sums, ((0, 0),) * 5 + ((0, SPAN - listed * rows),)),
            jnp.zeros((ny, nc, nz, nx, units * rows - rows - 2, SPAN), bf16),
        ],
        axis=4,
    )
    table = tied(summed(picked(table, "core", 1), "core"), line)
    table = summed(picked(table, "y", 0), "y").astype(bf16)
    mine = picked(table, "x", 1)
    own, other = mine(0).astype(bf16), shifted(mine(1).astype(bf16), "x", 1)
    table = jnp.where(x == 0, jnp.stack([own, other], 2), jnp.stack([other, own], 2))

    table = swap(table.reshape(nz, units * rows, nx * SPAN), "z")
    weight_sums = jnp.sum(line.astype(f32), axis=0)
    down_grad = weight_sums[:turns].reshape(turns * rows, width)
    out_grad = weight_sums[turns]
    up_grad = weight_sums[turns + 1 :].transpose(1, 0, 2).reshape(rows, hidden)
    up_grad = reordered(up_grad, turns, devices)
    qkv_grad, column_sums, sums = table_grads(ranks, rows, table)
    shards = sums[:, : listed * rows].reshape(listed, rows)
    device = (lax.axis_index("y") * nc + lax.axis_index("core")) * count + ctx_index
    query_bias_grad = lax.dynamic_slice_in_dim(column_sums[0], device * rows, rows)
    value_bias_grad = lax.dynamic_slice_in_dim(column_sums[2], device * rows, rows)

    return (
        output.reshape(1, tok, width),
        tokens_grad,
        qkv_grad,
        query_bias_grad,
        value_bias_grad,
        out_grad,
        shards[0],
        shards[1],
        shards[2],
        up_grad,
        shards[6:].reshape(-1),
        down_grad,
        shards[3],
        shards[4],
        shards[5],
    )


def solution(mesh):
    dp, ctx = (mesh.shape[a] for a in ("dp", "ctx"))
    fine = Mesh(mesh.devices.reshape(dp // 2, 2, ctx // 2, 2), ALL)
    token_spec = P(SEQ, CTX, None)
    matrix, vector = P(ALL, None), P(ALL)
    return jax.shard_map(
        body,
        mesh=fine,
        in_specs=(
            token_spec,
            matrix,
            vector,
            vector,
            matrix,
            vector,
            vector,
            vector,
            matrix,
            vector,
            matrix,
            vector,
            vector,
            vector,
            P(SEQ, CTX, None, None),
            token_spec,
        ),
        out_specs=(
            token_spec,
            token_spec,
            matrix,
            vector,
            vector,
            matrix,
            vector,
            vector,
            vector,
            matrix,
            vector,
            matrix,
            vector,
            vector,
            vector,
        ),
        check_vma=False,
    )
```

```python
import functools

import jax
import jax.numpy as jnp
from jax import lax
from jax.experimental import pallas as pl
from jax.experimental.pallas import tpu as pltpu
from jax.sharding import Mesh, PartitionSpec as P

H = 12
HD = 64
BLK = 64
RAND = 3
GROUPS = 4
PER_GROUP = 3
SPAN = 3 * 2 * HD
VMEM_BYTES = 56 * 1024 * 1024

bf16 = jnp.bfloat16
f32 = jnp.float32

norm_eps = 1e-06
gelu_root = 0.7978845608028654
gelu_cubic = 0.044715

ALL = ("y", "core", "z", "x")
SEQ = ("y", "core")
CTX = ("z", "x")

VMEM = pl.BlockSpec(memory_space=pltpu.VMEM)
SMEM = pl.BlockSpec(memory_space=pltpu.SMEM)
ANY = pl.BlockSpec(memory_space=pl.ANY)


def call(kernel, name, out_shape, in_specs, out_specs, flops, moved, scratch=(), after=()):
    def ordered(*refs):
        kernel(*refs[len(after) :])

    built = pl.pallas_call(
        ordered,
        out_shape=out_shape,
        in_specs=[ANY] * len(after) + in_specs,
        out_specs=out_specs,
        scratch_shapes=scratch,
        cost_estimate=pl.CostEstimate(flops=flops, bytes_accessed=moved, transcendentals=0),
        compiler_params=pltpu.CompilerParams(vmem_limit_bytes=VMEM_BYTES),
        name=name,
    )
    return functools.partial(built, *after)


def tied(value, *others):
    return lax.optimization_barrier((value,) + others)[0]


def shape(dims, kind):
    return jax.ShapeDtypeStruct(dims, kind)


def contract_rows(left_side, right_side):
    return lax.dot_general(
        left_side, right_side, (((0,), (0,)), ((), ())), preferred_element_type=f32
    )


def contract_cols(left_side, right_side):
    return lax.dot_general(
        left_side, right_side, (((1,), (1,)), ((), ())), preferred_element_type=f32
    )


def plain(left_side, right_side):
    return jnp.dot(left_side, right_side, preferred_element_type=f32)


def heads_of(index, ranks):
    group, rank = index // ranks, index % ranks
    first = PER_GROUP * group + (0 if rank < ranks // 2 else 1)
    return first, PER_GROUP * group + 2


def qkv_kernel(count, owner_ref, *refs):
    x_refs, w_ref, b_ref, out_ref = refs[:count], refs[count], refs[count + 1], refs[count + 2]
    tok = x_refs[0].shape[0]
    for k in range(count):
        rows = plain(x_refs[k][...], w_ref[...]) + b_ref[...]
        at = pl.ds(pl.multiple_of(owner_ref[k] * tok, BLK), tok)
        out_ref[at, :] = rows.astype(bf16)


def qkv_project(owners, pieces, weights, bias):
    count = len(pieces)
    tok, width = pieces[0].shape
    return call(
        functools.partial(qkv_kernel, count),
        "qkv_project",
        shape((count * tok, SPAN), bf16),
        [SMEM] + [VMEM] * (count + 2),
        VMEM,
        2 * count * tok * width * SPAN,
        4 * count * tok * width,
    )(owners, *pieces, weights, bias)


def token_grad_kernel(count, owner_ref, grad_ref, w_ref, *out_refs):
    tok = out_refs[0].shape[0]
    for k in range(count):
        at = pl.ds(pl.multiple_of(owner_ref[k] * tok, BLK), tok)
        out_refs[k][...] = contract_cols(grad_ref[at, :], w_ref[...]).astype(bf16)


def token_grads(count, owners, grads, weights, after):
    tok, width = grads.shape[0] // count, weights.shape[0]
    return call(
        functools.partial(token_grad_kernel, count),
        "token_grads",
        [shape((tok, width), bf16)] * count,
        [SMEM, VMEM, VMEM],
        [VMEM] * count,
        2 * count * tok * width * SPAN,
        4 * count * tok * width,
        after=after,
    )(owners, grads, weights)


def add_kernel(counts, *refs):
    at = sum(counts)
    for k, n in enumerate(counts):
        parts = [ref[...].astype(f32) for ref in refs[sum(counts[:k]) : sum(counts[: k + 1])]]
        refs[at + k][...] = functools.reduce(jnp.add, parts).astype(bf16)


def added(groups, after):
    counts = [len(group) for group in groups]
    size = groups[0][0].size
    return call(
        functools.partial(add_kernel, counts),
        "added",
        [shape(group[0].shape, bf16) for group in groups],
        [VMEM] * sum(counts),
        [VMEM] * len(groups),
        size * sum(counts),
        2 * size * sum(counts),
        after=after,
    )(*[part for group in groups for part in group])


def qkv_grad_kernel(count, owner_ref, *refs):
    x_refs, grad_ref, out_ref, bias_ref = refs[:count], refs[count], refs[count + 1], refs[count + 2]
    tok = x_refs[0].shape[0]
    total = None
    for k in range(count):
        at = pl.ds(pl.multiple_of(owner_ref[k] * tok, BLK), tok)
        part = contract_rows(x_refs[k][...], grad_ref[at, :])
        total = part if total is None else total + part
    out_ref[...] = total.astype(bf16)
    bias_ref[...] = jnp.sum(grad_ref[...].astype(f32), axis=0, keepdims=True)


def qkv_grads(owners, pieces, grads, after):
    count = len(pieces)
    tok, width = pieces[0].shape
    return call(
        functools.partial(qkv_grad_kernel, count),
        "qkv_grads",
        [shape((width, SPAN), bf16), shape((1, SPAN), f32)],
        [SMEM] + [VMEM] * (count + 1),
        [VMEM, VMEM],
        2 * count * tok * width * SPAN,
        4 * count * tok * width,
        after=after,
    )(owners, *pieces, grads)


class Plan:
    def __init__(self, count, ranks, blocks):
        self.count, self.ranks, self.blocks = count, ranks, blocks
        self.steps = (ranks // 2, ranks)
        self.owners = (count // self.steps[0], count // self.steps[1])
        self.total = count * blocks
        self.units = (self.owners[0] + self.owners[1]) * blocks
        self.rows = self.total * BLK
        self.chunk = min(self.rows, 2048)

    def at(self, block):
        return pl.ds(pl.multiple_of(block * BLK, BLK), BLK)

    def unit(self, half, turn, inner):
        return (half * self.owners[0] + turn) * self.blocks + inner

    def named(self, half, block, rand_ref):
        ids = [
            jnp.maximum(block - 1, 0),
            block,
            jnp.minimum(block + 1, self.total - 1),
            0,
            self.total - 1,
        ]
        for t in range(RAND):
            ids.append(rand_ref[(block * 2 + half) * RAND + t])
        return ids

    def flops(self, products):
        return 2 * products * self.units * BLK * 128 * 8 * BLK


def only_half(values, half):
    lane = lax.broadcasted_iota(jnp.int32, values.shape, 1)
    return jnp.where((lane < HD) == (half == 0), values, jnp.zeros_like(values))


def attn_forward_kernel(plan, rand_ref, rank_ref, kv_ref, out_ref, lse_ref):
    rank = rank_ref[0]
    out_ref[...] = jnp.zeros_like(out_ref)

    def emit(half, block, unit, attended, lse):
        out_ref[plan.at(block), half * HD : (half + 1) * HD] = attended[
            :, half * HD : (half + 1) * HD
        ].astype(bf16)
        lse_ref[plan.at(unit), :] = jnp.broadcast_to(lse, (BLK, 128))

    def query(half, block):
        return only_half(kv_ref[plan.at(block), 0:128], half) * 0.125

    for half in range(2):
        step = plan.steps[half]
        offset = lax.rem(rank, step) if step > 1 else 0

        def turn_body(turn, carry, half=half, step=step, offset=offset):
            inners = range(2 * plan.blocks)
            listed = [
                ((2 * turn + i // plan.blocks) * step + offset) * plan.blocks + i % plan.blocks
                for i in inners
            ]
            named = [plan.named(half, block, rand_ref) for block in listed]
            scores = []
            for inner, ids in zip(inners, named):
                keys = jnp.concatenate([kv_ref[plan.at(i), 128:256] for i in ids], axis=0)
                scores.append(contract_cols(query(half, listed[inner]), keys))
            probs, lses = [], []
            for part in scores:
                top = jnp.max(part, axis=-1, keepdims=True)
                grown = jnp.exp(part - top)
                total = jnp.sum(grown, axis=-1, keepdims=True)
                probs.append((grown * (1.0 / total)).astype(bf16))
                lses.append(top + jnp.log(total))
            for inner, ids in zip(inners, named):
                values = jnp.concatenate([kv_ref[plan.at(i), 256:384] for i in ids], axis=0)
                attended = plain(probs[inner], values)
                block = listed[inner]
                emit(half, block, plan.unit(half, 2 * turn, inner), attended, lses[inner])
            return carry

        lax.fori_loop(0, plan.owners[half] // 2, turn_body, 0)

    chunks = [pl.ds(c, plan.chunk) for c in range(0, plan.rows, plan.chunk)]
    for half in range(2):
        step = plan.steps[half]
        for block in (0, plan.total - 1):
            owner = block // plan.blocks

            def whole(half=half, step=step, owner=owner, block=block):
                q = query(half, block)
                scores = [contract_cols(q, kv_ref[c, 128:256]) for c in chunks]
                tops = [jnp.max(s, axis=-1, keepdims=True) for s in scores]
                top = functools.reduce(jnp.maximum, tops)
                grown = [jnp.exp(s - top) for s in scores]
                total = sum(jnp.sum(e, axis=-1, keepdims=True) for e in grown)
                scale = 1.0 / total
                attended = sum(
                    plain((e * scale).astype(bf16), kv_ref[c, 256:384])
                    for e, c in zip(grown, chunks)
                )
                unit = plan.unit(half, owner // step, block % plan.blocks)
                emit(half, block, unit, attended, top + jnp.log(total))

            if step == 1:
                whole()
            else:
                pl.when(lax.rem(rank, step) == owner % step)(whole)


def attn_forward(plan, rand, rank, kv):
    return call(
        functools.partial(attn_forward_kernel, plan),
        "attn_forward",
        (shape((plan.rows, 128), bf16), shape((plan.units * BLK, 128), f32)),
        [SMEM, SMEM, VMEM],
        (VMEM, VMEM),
        plan.flops(2),
        8 * plan.rows * 128,
    )(rand, rank, kv)


def attn_backward_kernel(
    plan, rand_ref, rank_ref, kv_ref, dout_ref, lse_ref, out_ref, sum_ref
):
    rank = rank_ref[0]
    out_ref[:, 0:128] = jnp.zeros((plan.rows, 128), bf16)
    sum_ref[...] = jnp.zeros_like(sum_ref)

    def operands(half, block, unit):
        q = only_half(kv_ref[plan.at(block), 0:128], half) * 0.125
        dout = only_half(dout_ref[plan.at(block), :], half)
        return q, dout, lse_ref[plan.at(unit), :][:, 0:1]

    def emit(half, block, grad_query):
        out_ref[plan.at(block), half * HD : (half + 1) * HD] = (
            grad_query[:, half * HD : (half + 1) * HD] * 0.125
        ).astype(bf16)

    for half in range(2):
        step = plan.steps[half]
        offset = lax.rem(rank, step) if step > 1 else 0

        def turn_body(turn, carry, half=half, step=step, offset=offset):
            inners = range(2 * plan.blocks)
            listed = [
                ((2 * turn + i // plan.blocks) * step + offset) * plan.blocks + i % plan.blocks
                for i in inners
            ]
            named = [plan.named(half, block, rand_ref) for block in listed]
            given, scores, grad_probs = [], [], []
            for inner, ids in zip(inners, named):
                block = listed[inner]
                q, dout, lse = operands(half, block, plan.unit(half, 2 * turn, inner))
                if inner % plan.blocks in (0, plan.blocks - 1):
                    edge = (block == 0) | (block == plan.total - 1)
                    dout = dout * jnp.where(edge, 0.0, 1.0).astype(bf16)
                given.append((q, dout, lse))
                keys = jnp.concatenate([kv_ref[plan.at(i), 128:256] for i in ids], axis=0)
                scores.append(contract_cols(q, keys))
            for inner, ids in zip(inners, named):
                values = jnp.concatenate([kv_ref[plan.at(i), 256:384] for i in ids], axis=0)
                grad_probs.append(contract_cols(given[inner][1], values))
            low_probs, grad_scores = [], []
            for inner in inners:
                probs = jnp.exp(scores[inner] - given[inner][2])
                delta = jnp.sum(probs * grad_probs[inner], axis=-1, keepdims=True)
                grad_scores.append((probs * (grad_probs[inner] - delta)).astype(bf16))
                low_probs.append(probs.astype(bf16))
            for inner, ids in zip(inners, named):
                keys = jnp.concatenate([kv_ref[plan.at(i), 128:256] for i in ids], axis=0)
                emit(half, listed[inner], plain(grad_scores[inner], keys))
            grad_keys = [contract_rows(grad_scores[i], given[i][0]) for i in inners]
            grad_values = [contract_rows(low_probs[i], given[i][1]) for i in inners]
            for inner, ids in zip(inners, named):
                for t, i in enumerate(ids):
                    sum_ref[plan.at(i), 0:128] += grad_keys[inner][t * BLK : (t + 1) * BLK]
                    sum_ref[plan.at(i), 128:256] += grad_values[inner][t * BLK : (t + 1) * BLK]
            return carry

        lax.fori_loop(0, plan.owners[half] // 2, turn_body, 0)

    chunks = [pl.ds(c, plan.chunk) for c in range(0, plan.rows, plan.chunk)]
    for half in range(2):
        step = plan.steps[half]
        for block in (0, plan.total - 1):
            owner = block // plan.blocks

            def whole(half=half, step=step, owner=owner, block=block):
                unit = plan.unit(half, owner // step, block % plan.blocks)
                q, dout, lse = operands(half, block, unit)
                probs = [jnp.exp(contract_cols(q, kv_ref[c, 128:256]) - lse) for c in chunks]
                grad_probs = [contract_cols(dout, kv_ref[c, 256:384]) for c in chunks]
                delta = sum(
                    jnp.sum(p * g, axis=-1, keepdims=True) for p, g in zip(probs, grad_probs)
                )
                grad_query = jnp.zeros((BLK, 128), f32)
                for p, g, c in zip(probs, grad_probs, chunks):
                    grad_scores = (p * (g - delta)).astype(bf16)
                    sum_ref[c, 0:128] += contract_rows(grad_scores, q)
                    sum_ref[c, 128:256] += contract_rows(p.astype(bf16), dout)
                    grad_query += plain(grad_scores, kv_ref[c, 128:256])
                emit(half, block, grad_query)

            if step == 1:
                whole()
            else:
                pl.when(lax.rem(rank, step) == owner % step)(whole)

    out_ref[:, 128:384] = sum_ref[...].astype(bf16)


def attn_backward(plan, rand, rank, kv, dout, lse, after):
    return call(
        functools.partial(attn_backward_kernel, plan),
        "attn_backward",
        shape((plan.rows, SPAN), bf16),
        [SMEM, SMEM, VMEM, VMEM, VMEM],
        VMEM,
        plan.flops(5),
        16 * plan.rows * 128,
        [pltpu.VMEM((plan.rows, 256), f32)],
        after,
    )(rand, rank, kv, dout, lse)


def table_kernel(ranks, rows, table_ref, grad_ref, bias_ref, sums_ref, last_ref):
    nz, width = table_ref.shape[0], table_ref.shape[2]
    nx = width // SPAN
    tiles = [
        table_ref[k // nx][:, k % nx * SPAN : (k % nx + 1) * SPAN].astype(f32)
        for k in range(nz * nx)
    ]
    total = functools.reduce(jnp.add, [tile[rows + 1 : rows + 2] for tile in tiles])
    listed, last = sums_ref.shape[0], last_ref.shape[1]
    for k in range(listed):
        sums_ref[k : k + 1, :] = total[:, k * rows : (k + 1) * rows]
    last_ref[...] = total[:, listed * rows : listed * rows + last]
    for part in range(3):
        heads = []
        for g in range(GROUPS):
            own = [tiles[g * ranks + r][:, part * 128 : part * 128 + HD] for r in range(ranks)]
            shared = [tiles[g * ranks + r][:, part * 128 + HD : (part + 1) * 128] for r in range(ranks)]
            for group in (own[: ranks // 2], own[ranks // 2 :], shared):
                heads.append(functools.reduce(jnp.add, group))
        whole = jnp.concatenate(heads, axis=1)
        grad_ref[:, part * H * HD : (part + 1) * H * HD] = whole[0:rows]
        bias_ref[part : part + 1, :] = whole[rows : rows + 1]


def table_grads(ranks, rows, listed, table):
    return call(
        functools.partial(table_kernel, ranks, rows),
        "table_grads",
        [
            shape((rows, 3 * H * HD), f32),
            shape((3, H * HD), f32),
            shape((6, rows), f32),
            shape((1, (listed - 6) * rows), f32),
        ],
        [VMEM],
        [VMEM] * 4,
        table.size,
        2 * table.size,
    )(table)


def reorder_kernel(outer, inner, rows, in_ref, out_ref):
    value = in_ref[...].astype(f32)
    out_ref[...] = jnp.concatenate(
        [
            value[:, (o * inner + i) * rows : (o * inner + i + 1) * rows]
            for i in range(inner)
            for o in range(outer)
        ],
        axis=1,
    ).astype(out_ref.dtype)


def reordered(value, outer, inner):
    rows, cols = value.shape
    run = cols // (outer * inner)
    if run < 8:
        return value.reshape(rows, outer, inner, run).transpose(0, 2, 1, 3).reshape(rows, cols)
    return call(
        functools.partial(reorder_kernel, outer, inner, run),
        "reorder",
        shape((rows, cols), value.dtype),
        [VMEM],
        VMEM,
        rows * cols,
        4 * rows * cols,
    )(value)


def pack_kernel(outer, inner, out_w_ref, up_ref, down_ref, packed_ref):
    rows, width = out_w_ref.shape
    packed_ref[:, 0:width] = out_w_ref[...]
    up = up_ref[...].astype(f32)
    down = down_ref[...].astype(f32)
    for i in range(inner):
        packed_ref[:, (1 + i) * width : (2 + i) * width] = jnp.concatenate(
            [
                up[:, (o * inner + i) * rows : (o * inner + i + 1) * rows]
                for o in range(outer)
            ],
            axis=1,
        ).astype(bf16)
        packed_ref[:, (1 + inner + i) * width : (2 + inner + i) * width] = down[
            i * rows : (i + 1) * rows
        ].astype(bf16)


def packed_weights(out_weight, up_weight, down_weight, devices):
    rows, width = out_weight.shape
    turns = up_weight.shape[1] // width
    if rows < 8:
        up = reordered(up_weight, devices, turns)
        down = down_weight.reshape(turns, rows, width).transpose(1, 0, 2)
        return jnp.concatenate([out_weight, up, down.reshape(rows, turns * width)], axis=1)
    return call(
        functools.partial(pack_kernel, devices, turns),
        "packed_weights",
        shape((rows, (1 + 2 * turns) * width), bf16),
        [VMEM] * 3,
        VMEM,
        rows * width,
        rows * width,
    )(out_weight, up_weight, down_weight)


def normalized(values):
    center = values - jnp.mean(values, axis=-1, keepdims=True)
    spread = jnp.mean(center * center, axis=-1, keepdims=True)
    scale = lax.rsqrt(spread + norm_eps)
    return center * scale, scale


def normalized_grad(normal, scale, grad):
    return scale * (
        grad
        - jnp.mean(grad, axis=-1, keepdims=True)
        - normal * jnp.mean(grad * normal, axis=-1, keepdims=True)
    )


def column_sum(values):
    return jnp.sum(values.astype(f32), axis=0, keepdims=True)


def middle_kernel(
    ranks,
    back_ref,
    tok_ref,
    cot_ref,
    vec_ref,
    pack_ref,
    output_ref,
    resid_ref,
    dout_ref,
    attn_ref,
    mid_ref,
    act_ref,
    down_ref,
    pre_ref,
    branch_ref,
    sums_ref,
    out_w,
    up_w,
    down_w,
    slope_ref,
    sems,
):
    count = back_ref.shape[0]
    width = tok_ref.shape[1]
    turns = up_w.shape[1] // width
    half_ranks = ranks // 2

    copies = [pltpu.make_async_copy(pack_ref.at[:, pl.ds(0, width)], out_w, sems.at[0])]
    for t in range(turns):
        cols = pl.ds(t * width, width)
        copies.append(
            pltpu.make_async_copy(
                pack_ref.at[:, pl.ds((1 + t) * width, width)], up_w.at[:, cols], sems.at[1 + t]
            )
        )
        copies.append(
            pltpu.make_async_copy(
                pack_ref.at[:, pl.ds((1 + turns + t) * width, width)],
                down_w.at[t],
                sems.at[1 + turns + t],
            )
        )
    for copy in copies:
        copy.start()

    for g in range(GROUPS):
        own = [back_ref[g * ranks + r][:, 0:HD] for r in range(ranks)]
        shared = [back_ref[g * ranks + r][:, HD : 2 * HD] for r in range(ranks)]
        trio = [sum(own[1:half_ranks], own[0]), sum(own[half_ranks + 1 :], own[half_ranks])]
        trio.append(sum(shared[1:], shared[0]))
        attn_ref[:, g * PER_GROUP * HD : (g + 1) * PER_GROUP * HD] = jnp.concatenate(trio, axis=1)

    out_bias, attn_gain, attn_shift, down_bias, ffn_gain, ffn_shift = (
        vec_ref[k : k + 1, :] for k in range(2, 8)
    )
    copies[0].wait()
    branch = plain(attn_ref[...], out_w[...]) + out_bias
    normal, scale = normalized(tok_ref[...].astype(f32) + branch)
    mid = normal * attn_gain + attn_shift
    mid_low = mid.astype(bf16)
    mid_ref[...] = mid_low
    final = mid + down_bias
    for t in range(turns):
        cols = slice(t * width, (t + 1) * width)
        copies[1 + 2 * t].wait()
        pre = plain(mid_low, up_w[:, cols]) + vec_ref[8 + t : 9 + t, :]
        square = pre * pre
        bend = jnp.tanh(gelu_root * (pre + gelu_cubic * pre * square))
        rise = 0.5 * (1.0 + bend)
        slope_ref[:, cols] = rise + 0.5 * pre * (1.0 - bend * bend) * (
            gelu_root * (1.0 + 3.0 * gelu_cubic * square)
        )
        act = (pre * rise).astype(bf16)
        act_ref[:, cols] = act
        copies[2 + 2 * t].wait()
        final = final + plain(act, down_w[t])
    normal_two, scale_two = normalized(final)
    output_ref[...] = (normal_two * ffn_gain + ffn_shift).astype(bf16)
    cot = cot_ref[...].astype(f32)
    sums_ref[4:5, :] = column_sum(cot * normal_two)
    sums_ref[5:6, :] = column_sum(cot)
    grad_final = normalized_grad(normal_two, scale_two, cot * ffn_gain)
    down_low = grad_final.astype(bf16)
    down_ref[...] = down_low
    sums_ref[3:4, :] = column_sum(down_low)
    grad_mid = grad_final
    for t in range(turns):
        cols = slice(t * width, (t + 1) * width)
        grad_pre = (contract_cols(down_low, down_w[t]) * slope_ref[:, cols]).astype(bf16)
        pre_ref[:, cols] = grad_pre
        sums_ref[6 + t : 7 + t, :] = column_sum(grad_pre)
        grad_mid = grad_mid + contract_cols(grad_pre, up_w[:, cols])
    sums_ref[1:2, :] = column_sum(grad_mid * normal)
    sums_ref[2:3, :] = column_sum(grad_mid)
    resid = normalized_grad(normal, scale, grad_mid * attn_gain)
    resid_ref[...] = resid
    branch_low = resid.astype(bf16)
    branch_ref[...] = branch_low
    sums_ref[0:1, :] = column_sum(branch_low)
    grad_attn = contract_cols(branch_low, out_w[...]).astype(bf16)
    for j in range(count):
        first, shared = heads_of(j, ranks)
        dout_ref[j] = jnp.concatenate(
            [
                grad_attn[:, first * HD : (first + 1) * HD],
                grad_attn[:, shared * HD : (shared + 1) * HD],
            ],
            axis=1,
        )


def middle(ranks, back, tokens, cotangent, vectors, packed):
    count, (tok, width) = back.shape[0], tokens.shape
    turns = vectors.shape[0] - 8
    hidden = turns * width
    return call(
        functools.partial(middle_kernel, ranks),
        "middle",
        [
            shape((tok, width), bf16),
            shape((tok, width), f32),
            shape((count, tok, 128), bf16),
            shape((tok, width), bf16),
            shape((tok, width), bf16),
            shape((tok, hidden), bf16),
            shape((tok, width), bf16),
            shape((tok, hidden), bf16),
            shape((tok, width), bf16),
            shape((6 + turns, width), f32),
        ],
        [VMEM] * 4 + [ANY],
        [VMEM] * 10,
        4 * tok * width * (width + 2 * hidden),
        2 * width * (width + 2 * hidden),
        [
            pltpu.VMEM((width, width), bf16),
            pltpu.VMEM((width, hidden), bf16),
            pltpu.VMEM((turns, width, width), bf16),
            pltpu.VMEM((tok, hidden), f32),
            pltpu.SemaphoreType.DMA((1 + 2 * turns,)),
        ],
    )(back, tokens, cotangent, vectors, packed)


def weight_grad_kernel(pairs, where_ref, *refs):
    operands, outs, total_ref = refs[: 2 * len(pairs)], refs[2 * len(pairs) : -1], refs[-1]
    turn = pl.program_id(0)
    first = 0
    for k, turns in enumerate(pairs):

        def product(left_ref=operands[2 * k], right_ref=operands[2 * k + 1]):
            total_ref[...] = contract_rows(left_ref[...], right_ref[...])

        pl.when((turn >= first) & (turn < first + turns))(product)
        first += turns
    ny = len(outs) // 2
    rows = total_ref.shape[0] // (2 * ny)
    mine, core = where_ref[0], where_ref[1]
    for d in range(ny):
        base = lax.rem(mine + d, ny) * 2
        for ref, c in ((outs[d], core), (outs[ny + d], 1 - core)):
            ref[0] = total_ref[pl.ds(pl.multiple_of((base + c) * rows, 16), rows), :].astype(bf16)


def weight_grad(where, ny, *pairs):
    tok = pairs[0][0].shape[0]
    width = min(min(left.shape[1], right.shape[1]) for left, right in pairs)
    counts, specs, first = [], [], 0
    for pair in pairs:
        turns = max(operand.shape[1] for operand in pair) // width
        for operand in pair:
            if operand.shape[1] == width:
                specs.append(pl.BlockSpec((tok, width), lambda t: (0, 0)))
            else:
                specs.append(
                    pl.BlockSpec(
                        (tok, width),
                        lambda t, first=first, turns=turns: (0, jnp.clip(t - first, 0, turns - 1)),
                    )
                )
        counts.append(turns)
        first += turns
    rows = width // (2 * ny)
    parts = pl.pallas_call(
        functools.partial(weight_grad_kernel, counts),
        grid=(first,),
        out_shape=[shape((first, rows, width), bf16)] * (2 * ny),
        in_specs=[SMEM] + specs,
        out_specs=[pl.BlockSpec((1, rows, width), lambda t: (t, 0, 0))] * (2 * ny),
        scratch_shapes=[pltpu.VMEM((width, width), f32)],
        cost_estimate=pl.CostEstimate(
            flops=2 * tok * width * width * first,
            bytes_accessed=2 * width * width * first,
            transcendentals=0,
        ),
        compiler_params=pltpu.CompilerParams(vmem_limit_bytes=VMEM_BYTES),
        name="weight_grad",
    )(where, *[operand for pair in pairs for operand in pair])
    return parts[:ny], parts[ny:]


def swap(value, axis):
    return lax.all_to_all(value, axis, split_axis=0, concat_axis=0, tiled=True)


def shifted(value, axis, by):
    size = lax.axis_size(axis)
    return lax.ppermute(value, axis, [(i, (i + by) % size) for i in range(size)])


def far_first(size):
    return sorted(range(1, size), key=lambda d: -min(d, size - d))


def picked(value, axis, dim):
    size, here = lax.axis_size(axis), lax.axis_index(axis)

    def part(d):
        return lax.dynamic_index_in_dim(
            value, lax.rem(here + d, size), dim, keepdims=False
        ).astype(f32)

    return part


def split(value, nz, nx):
    return value.reshape(value.shape[:-2] + (nz, nx, value.shape[-2] // (nz * nx), value.shape[-1]))


def along_y(value):
    return lambda d: value[d]


def along_x(value):
    return picked(value, "x", value.ndim - 3)


def sends(parts, size):
    return [parts(d).astype(bf16) for d in far_first(size)]


def arrivals(sent, axis):
    return [shifted(part, axis, d) for d, part in zip(far_first(len(sent) + 1), sent)]


def plus(kept, got):
    return functools.reduce(lambda total, part: total + part.astype(f32), got, kept)


def summed(parts, axis):
    return plus(parts(0), arrivals(sends(parts, lax.axis_size(axis)), axis))


def body(
    tokens,
    qkv_weight,
    query_bias,
    value_bias,
    out_weight,
    out_bias,
    attn_gain,
    attn_shift,
    up_weight,
    up_bias,
    down_weight,
    down_bias,
    ffn_gain,
    ffn_shift,
    random_blocks,
    cotangent,
):
    ny, nc, nz, nx = (lax.axis_size(a) for a in ALL)
    count, devices = nz * nx, ny * nc * nz * nx
    ranks = count // GROUPS
    half_ranks = ranks // 2
    _, tok, width = tokens.shape
    blocks = tok // BLK
    plan = Plan(count, ranks, blocks)
    z, x = lax.axis_index("z"), lax.axis_index("x")
    ctx_index = z * nx + x
    rank = lax.rem(ctx_index, ranks).astype(jnp.int32).reshape(1)
    where = jnp.stack([lax.axis_index("y"), lax.axis_index("core")]).astype(jnp.int32)
    rows = qkv_weight.shape[0]
    hidden = up_weight.shape[1]
    turns = hidden // width
    flat_tokens = tokens.reshape(tok, width)

    packed = packed_weights(out_weight, up_weight, down_weight, devices)
    packed = lax.all_gather(packed, ALL, axis=0, tiled=True)

    def by_index(values):
        grouped = values.reshape(values.shape[:-2] + (GROUPS, PER_GROUP, values.shape[-1]))
        pairs = [
            jnp.stack([grouped[..., 0 if r < half_ranks else 1, :], grouped[..., 2, :]], axis=-2)
            for r in range(ranks)
        ]
        return jnp.moveaxis(jnp.stack(pairs, axis=-3), (-4, -3), (0, 1)).reshape(
            (count,) + values.shape[:-2] + (2, values.shape[-1])
        )

    weight_rows = by_index(qkv_weight.reshape(rows, 3, H, HD)).reshape(count, rows, SPAN)
    picks = by_index(random_blocks[0].astype(bf16)).reshape(count, 1, -1)
    entries = picks.shape[2]
    small = jnp.concatenate(
        [
            query_bias,
            value_bias,
            out_bias,
            attn_gain,
            attn_shift,
            down_bias,
            ffn_gain,
            ffn_shift,
            up_bias,
        ]
    )
    many = small.shape[0] // rows
    extra = -(-(rows + 2) // 8) * 8
    sent = jnp.concatenate(
        [
            weight_rows,
            jnp.pad(picks, ((0, 0), (0, 0), (0, SPAN - entries))),
            jnp.broadcast_to(jnp.pad(small, (0, SPAN - small.shape[0])), (count, 1, SPAN)),
            jnp.zeros((count, extra - rows - 2, SPAN), bf16),
        ],
        axis=1,
    )
    near = [d for d in range(1, nz) if min(d, nz - d) == 1]
    held = {0: flat_tokens}
    over = {}
    for e in range(1, nx):
        over[0, e] = shifted(flat_tokens, "x", e)
    for d in near:
        held[d] = shifted(flat_tokens, "z", d)
    for d in range(2, nz - 1):
        held[d] = shifted(tied(flat_tokens, over[0, 1]), "z", d)
    line = swap(sent, CTX)
    shifts = [0] + near + [d for d in far_first(nz) if d not in near]
    order = [(d, e) for e in range(nx) for d in shifts]
    pieces = []
    for d, e in order:
        if e and d:
            over[d, e] = shifted(held[d], "x", e)
        pieces.append(over[d, e] if e else held[d])
    owners = jnp.stack(
        [lax.rem(z + nz - d, nz) * nx + lax.rem(x + nx - e, nx) for d, e in order]
    ).astype(jnp.int32)
    targets = jnp.stack(
        [lax.rem(z + d, nz) * nx + lax.rem(x + e, nx) for d, e in order]
    ).astype(jnp.int32)
    rand = line[:, rows, :entries].astype(jnp.int32).reshape(-1)
    seqs = ny * nc
    full = swap(
        tied(jnp.broadcast_to(line[None], (seqs,) + line.shape), over[0, 1], *(over[d, 1] for d in near), *held.values()), SEQ
    )
    columns = full[:, :, :rows].reshape(width, SPAN)
    vectors = full[:, :, rows + 1, : small.shape[0]].astype(f32)
    vectors = vectors.reshape(devices, many, rows).transpose(1, 0, 2).reshape(many, width)
    bias_table = by_index(
        jnp.stack([vectors[0], jnp.zeros_like(vectors[0]), vectors[1]]).reshape(3, H, HD)
    ).reshape(count, 1, SPAN)
    bias = lax.dynamic_index_in_dim(bias_table, ctx_index, 0, keepdims=False)

    kv = qkv_project(owners, pieces, columns, bias)
    attended, lse = attn_forward(plan, rand, rank, kv)
    back = swap(attended.reshape(count, tok, 128), CTX)

    output, resid, dout, attn_low, mid_low, act_low, down_low, pre_low, branch_low, sums = middle(
        ranks, back, flat_tokens, cotangent.reshape(tok, width), vectors, packed
    )

    first_keep, first_send = weight_grad(where, ny, (act_low, down_low), (attn_low, branch_low))
    second_keep, second_send = weight_grad(where, ny, (mid_low, pre_low))
    first_got = [shifted(part, "core", 1) for part in first_send]
    second_got = [shifted(part, "core", 1) for part in second_send]

    def terms_of(parts, d):
        at = lax.rem(x + d, nx)
        parts = [lax.dynamic_index_in_dim(part, at, part.ndim - 3, keepdims=False) for part in parts]
        return functools.reduce(jnp.add, [part.astype(f32) for part in parts])

    def by_y(pair, d):
        return [split(part[d], nz, nx) for part in pair]

    first_pair, second_pair = (first_keep, first_got), (second_keep, second_got)
    first_sent = [
        functools.reduce(jnp.add, [part.astype(f32) for part in by_y(first_pair, d)]).astype(bf16)
        for d in far_first(ny)
    ]
    second_sent = [
        jnp.stack([terms_of(by_y(second_pair, d), e) for d in range(ny)]).astype(bf16)
        for e in far_first(nx)
    ]

    dout = swap(tied(dout, *first_sent), CTX).reshape(plan.rows, 128)
    second_sent, dout = lax.optimization_barrier((second_sent, dout))
    grads = attn_backward(plan, rand, rank, kv, dout, lse, [])
    first_more, second_more = arrivals(first_sent, "y"), arrivals(second_sent, "x")

    def first_part(e, pair):
        return terms_of(by_y(pair, 0) + first_more, e)

    def second_part(d, pair):
        return plus(terms_of(by_y(pair, d), 0), [part[d] for part in second_more])

    first_late = tied(first_pair, grads)
    first_sent = [first_part(e, first_late).astype(bf16) for e in far_first(nx)]
    second_more = [tied(part, *first_sent) for part in second_more]
    second_late = tied(second_pair, *first_sent)
    second_sent = [second_part(d, second_late).astype(bf16) for d in far_first(ny)]
    terms = token_grads(count, targets, tied(grads, *first_sent, *second_sent), columns, [])
    first_next, second_next = arrivals(first_sent, "x"), arrivals(second_sent, "y")
    column_grads, bias_grads = qkv_grads(
        owners, pieces, tied(grads, terms[0], *first_next, *second_next), []
    )

    def over_x(d, *others):
        return [
            shifted(tied(terms[e * nz + shifts.index(d)], *others), "x", e) for e in range(1, nx)
        ]

    line_order = far_first(nz)
    across = {d: over_x(d) for d in line_order}

    line = jnp.concatenate(
        [
            plus(first_part(0, tied(first_late, terms[0])), first_next).astype(bf16).transpose(1, 0, 2, 3),
            plus(second_part(0, tied(second_late, terms[0])), second_next).astype(bf16).transpose(1, 0, 2, 3),
        ],
        axis=1,
    )
    line = swap(tied(line, *across[line_order[0]]), "z")

    total = added(
        [
            [tied(terms[shifts.index(d)], column_grads)] + across[d]
            for d in line_order
        ],
        [],
    )
    early = total[0]
    total = [tied(part, line) for part in total]
    line_got = [shifted(part, "z", d) for d, part in zip(line_order, total)]
    own = plus(terms[0].astype(f32), over_x(0, *total))
    tokens_grad = plus(resid + own, line_got).reshape(1, tok, width)

    listed = sums.shape[0]
    vector_sums = sums.reshape(listed, ny, nc, count, rows).transpose(1, 2, 3, 0, 4)
    vector_sums = vector_sums.reshape(ny, nc, nz, nx, 1, listed * rows).astype(bf16)
    units = -(-(rows + 2) // rows)
    table = jnp.concatenate(
        [
            tied(column_grads, early).reshape(ny, nc, nz, nx, rows, SPAN),
            jnp.broadcast_to(bias_grads.astype(bf16), (ny, nc, nz, nx, 1, SPAN)),
            jnp.pad(vector_sums, ((0, 0),) * 5 + ((0, SPAN - listed * rows),)),
            jnp.zeros((ny, nc, nz, nx, units * rows - rows - 2, SPAN), bf16),
        ],
        axis=4,
    )
    table = tied(summed(picked(table, "core", 1), "core"), line)
    table = summed(picked(table, "y", 0), "y").astype(bf16)
    mine = picked(table, "x", 1)
    own, other = mine(0).astype(bf16), shifted(mine(1).astype(bf16), "x", 1)
    table = jnp.where(x == 0, jnp.stack([own, other], 2), jnp.stack([other, own], 2))

    weight_sums = jnp.sum(line.astype(f32), axis=0)
    down_grad = weight_sums[:turns].reshape(turns * rows, width)
    out_grad = weight_sums[turns]
    up_grad = weight_sums[turns + 1 :].transpose(1, 0, 2).reshape(rows, hidden)
    up_grad = reordered(up_grad, turns, devices)
    table = tied(table.reshape(nz, units * rows, nx * SPAN), up_grad, out_grad, down_grad)
    table = swap(table, "z")
    qkv_grad, column_sums, shards, up_bias_grad = table_grads(ranks, rows, listed, table)
    device = (lax.axis_index("y") * nc + lax.axis_index("core")) * count + ctx_index
    query_bias_grad = lax.dynamic_slice_in_dim(column_sums[0], device * rows, rows)
    value_bias_grad = lax.dynamic_slice_in_dim(column_sums[2], device * rows, rows)

    return (
        output.reshape(1, tok, width),
        tokens_grad,
        qkv_grad,
        query_bias_grad,
        value_bias_grad,
        out_grad,
        shards[0],
        shards[1],
        shards[2],
        up_grad,
        up_bias_grad.reshape(-1),
        down_grad,
        shards[3],
        shards[4],
        shards[5],
    )


def solution(mesh):
    dp, ctx = (mesh.shape[a] for a in ("dp", "ctx"))
    fine = Mesh(mesh.devices.reshape(dp // 2, 2, ctx // 2, 2), ALL)
    token_spec = P(SEQ, CTX, None)
    matrix, vector = P(ALL, None), P(ALL)
    return jax.shard_map(
        body,
        mesh=fine,
        in_specs=(
            token_spec,
            matrix,
            vector,
            vector,
            matrix,
            vector,
            vector,
            vector,
            matrix,
            vector,
            matrix,
            vector,
            vector,
            vector,
            P(SEQ, CTX, None, None),
            token_spec,
        ),
        out_specs=(
            token_spec,
            token_spec,
            matrix,
            vector,
            vector,
            matrix,
            vector,
            vector,
            vector,
            matrix,
            vector,
            matrix,
            vector,
            vector,
            vector,
        ),
        check_vma=False,
    )
```

```python
import functools

import jax
import jax.numpy as jnp
from jax import lax
from jax.experimental import pallas as pl
from jax.experimental.pallas import tpu as pltpu
from jax.sharding import Mesh, PartitionSpec as P

H = 12
HD = 64
BLK = 64
RAND = 3
GROUPS = 4
PER_GROUP = 3
SPAN = 3 * 2 * HD
VMEM_BYTES = 56 * 1024 * 1024

bf16 = jnp.bfloat16
f32 = jnp.float32

norm_eps = 1e-06
gelu_root = 0.7978845608028654
gelu_cubic = 0.044715

ALL = ("y", "core", "z", "x")
SEQ = ("y", "core")
CTX = ("z", "x")

VMEM = pl.BlockSpec(memory_space=pltpu.VMEM)
SMEM = pl.BlockSpec(memory_space=pltpu.SMEM)
ANY = pl.BlockSpec(memory_space=pl.ANY)


def call(kernel, name, out_shape, in_specs, out_specs, flops, moved, scratch=(), after=()):
    def ordered(*refs):
        kernel(*refs[len(after) :])

    built = pl.pallas_call(
        ordered,
        out_shape=out_shape,
        in_specs=[ANY] * len(after) + in_specs,
        out_specs=out_specs,
        scratch_shapes=scratch,
        cost_estimate=pl.CostEstimate(flops=flops, bytes_accessed=moved, transcendentals=0),
        compiler_params=pltpu.CompilerParams(vmem_limit_bytes=VMEM_BYTES),
        name=name,
    )
    return functools.partial(built, *after)


def tied(value, *others):
    return lax.optimization_barrier((value,) + others)[0]


def shape(dims, kind):
    return jax.ShapeDtypeStruct(dims, kind)


def contract_rows(left_side, right_side):
    return lax.dot_general(
        left_side, right_side, (((0,), (0,)), ((), ())), preferred_element_type=f32
    )


def contract_cols(left_side, right_side):
    return lax.dot_general(
        left_side, right_side, (((1,), (1,)), ((), ())), preferred_element_type=f32
    )


def plain(left_side, right_side):
    return jnp.dot(left_side, right_side, preferred_element_type=f32)


def heads_of(index, ranks):
    group, rank = index // ranks, index % ranks
    first = PER_GROUP * group + (0 if rank < ranks // 2 else 1)
    return first, PER_GROUP * group + 2


def qkv_kernel(count, owner_ref, *refs):
    x_refs, w_ref, b_ref, out_ref = refs[:count], refs[count], refs[count + 1], refs[count + 2]
    tok = x_refs[0].shape[0]
    for k in range(count):
        rows = plain(x_refs[k][...], w_ref[...]) + b_ref[...]
        at = pl.ds(pl.multiple_of(owner_ref[k] * tok, BLK), tok)
        out_ref[at, :] = rows.astype(bf16)


def qkv_project(owners, pieces, weights, bias):
    count = len(pieces)
    tok, width = pieces[0].shape
    return call(
        functools.partial(qkv_kernel, count),
        "qkv_project",
        shape((count * tok, SPAN), bf16),
        [SMEM] + [VMEM] * (count + 2),
        VMEM,
        2 * count * tok * width * SPAN,
        4 * count * tok * width,
    )(owners, *pieces, weights, bias)


def token_grad_kernel(count, owner_ref, grad_ref, w_ref, *out_refs):
    tok = out_refs[0].shape[0]
    for k in range(count):
        at = pl.ds(pl.multiple_of(owner_ref[k] * tok, BLK), tok)
        out_refs[k][...] = contract_cols(grad_ref[at, :], w_ref[...]).astype(bf16)


def token_grads(count, owners, grads, weights, after):
    tok, width = grads.shape[0] // count, weights.shape[0]
    return call(
        functools.partial(token_grad_kernel, count),
        "token_grads",
        [shape((tok, width), bf16)] * count,
        [SMEM, VMEM, VMEM],
        [VMEM] * count,
        2 * count * tok * width * SPAN,
        4 * count * tok * width,
        after=after,
    )(owners, grads, weights)


def add_kernel(counts, *refs):
    at = sum(counts)
    for k, n in enumerate(counts):
        parts = [ref[...].astype(f32) for ref in refs[sum(counts[:k]) : sum(counts[: k + 1])]]
        refs[at + k][...] = functools.reduce(jnp.add, parts).astype(bf16)


def added(groups, after):
    counts = [len(group) for group in groups]
    size = groups[0][0].size
    return call(
        functools.partial(add_kernel, counts),
        "added",
        [shape(group[0].shape, bf16) for group in groups],
        [VMEM] * sum(counts),
        [VMEM] * len(groups),
        size * sum(counts),
        2 * size * sum(counts),
        after=after,
    )(*[part for group in groups for part in group])


def qkv_grad_kernel(count, owner_ref, *refs):
    x_refs, grad_ref, out_ref, bias_ref = refs[:count], refs[count], refs[count + 1], refs[count + 2]
    tok = x_refs[0].shape[0]
    total = None
    for k in range(count):
        at = pl.ds(pl.multiple_of(owner_ref[k] * tok, BLK), tok)
        part = contract_rows(x_refs[k][...], grad_ref[at, :])
        total = part if total is None else total + part
    out_ref[...] = total.astype(bf16)
    bias_ref[...] = jnp.sum(grad_ref[...].astype(f32), axis=0, keepdims=True)


def qkv_grads(owners, pieces, grads, after):
    count = len(pieces)
    tok, width = pieces[0].shape
    return call(
        functools.partial(qkv_grad_kernel, count),
        "qkv_grads",
        [shape((width, SPAN), bf16), shape((1, SPAN), f32)],
        [SMEM] + [VMEM] * (count + 1),
        [VMEM, VMEM],
        2 * count * tok * width * SPAN,
        4 * count * tok * width,
        after=after,
    )(owners, *pieces, grads)


class Plan:
    def __init__(self, count, ranks, blocks):
        self.count, self.ranks, self.blocks = count, ranks, blocks
        self.steps = (ranks // 2, ranks)
        self.owners = (count // self.steps[0], count // self.steps[1])
        self.total = count * blocks
        self.units = (self.owners[0] + self.owners[1]) * blocks
        self.rows = self.total * BLK
        self.chunk = min(self.rows, 2048)

    def at(self, block):
        return pl.ds(pl.multiple_of(block * BLK, BLK), BLK)

    def unit(self, half, turn, inner):
        return (half * self.owners[0] + turn) * self.blocks + inner

    def named(self, half, block, rand_ref):
        ids = [
            jnp.maximum(block - 1, 0),
            block,
            jnp.minimum(block + 1, self.total - 1),
            0,
            self.total - 1,
        ]
        for t in range(RAND):
            ids.append(rand_ref[(block * 2 + half) * RAND + t])
        return ids

    def flops(self, products):
        return 2 * products * self.units * BLK * 128 * 8 * BLK


def only_half(values, half):
    lane = lax.broadcasted_iota(jnp.int32, values.shape, 1)
    return jnp.where((lane < HD) == (half == 0), values, jnp.zeros_like(values))


def attn_forward_kernel(plan, rand_ref, rank_ref, kv_ref, out_ref, lse_ref):
    rank = rank_ref[0]
    out_ref[...] = jnp.zeros_like(out_ref)

    def emit(half, block, unit, attended, lse):
        out_ref[plan.at(block), half * HD : (half + 1) * HD] = attended[
            :, half * HD : (half + 1) * HD
        ].astype(bf16)
        lse_ref[plan.at(unit), :] = jnp.broadcast_to(lse, (BLK, 128))

    def query(half, block):
        return only_half(kv_ref[plan.at(block), 0:128], half) * 0.125

    for half in range(2):
        step = plan.steps[half]
        offset = lax.rem(rank, step) if step > 1 else 0

        def turn_body(turn, carry, half=half, step=step, offset=offset):
            inners = range(2 * plan.blocks)
            listed = [
                ((2 * turn + i // plan.blocks) * step + offset) * plan.blocks + i % plan.blocks
                for i in inners
            ]
            named = [plan.named(half, block, rand_ref) for block in listed]
            scores = []
            for inner, ids in zip(inners, named):
                keys = jnp.concatenate([kv_ref[plan.at(i), 128:256] for i in ids], axis=0)
                scores.append(contract_cols(query(half, listed[inner]), keys))
            probs, lses = [], []
            for part in scores:
                top = jnp.max(part, axis=-1, keepdims=True)
                grown = jnp.exp(part - top)
                total = jnp.sum(grown, axis=-1, keepdims=True)
                probs.append((grown * (1.0 / total)).astype(bf16))
                lses.append(top + jnp.log(total))
            for inner, ids in zip(inners, named):
                values = jnp.concatenate([kv_ref[plan.at(i), 256:384] for i in ids], axis=0)
                attended = plain(probs[inner], values)
                block = listed[inner]
                emit(half, block, plan.unit(half, 2 * turn, inner), attended, lses[inner])
            return carry

        lax.fori_loop(0, plan.owners[half] // 2, turn_body, 0)

    chunks = [pl.ds(c, plan.chunk) for c in range(0, plan.rows, plan.chunk)]
    for half in range(2):
        step = plan.steps[half]
        for block in (0, plan.total - 1):
            owner = block // plan.blocks

            def whole(half=half, step=step, owner=owner, block=block):
                q = query(half, block)
                scores = [contract_cols(q, kv_ref[c, 128:256]) for c in chunks]
                tops = [jnp.max(s, axis=-1, keepdims=True) for s in scores]
                top = functools.reduce(jnp.maximum, tops)
                grown = [jnp.exp(s - top) for s in scores]
                total = sum(jnp.sum(e, axis=-1, keepdims=True) for e in grown)
                scale = 1.0 / total
                attended = sum(
                    plain((e * scale).astype(bf16), kv_ref[c, 256:384])
                    for e, c in zip(grown, chunks)
                )
                unit = plan.unit(half, owner // step, block % plan.blocks)
                emit(half, block, unit, attended, top + jnp.log(total))

            if step == 1:
                whole()
            else:
                pl.when(lax.rem(rank, step) == owner % step)(whole)


def attn_forward(plan, rand, rank, kv):
    return call(
        functools.partial(attn_forward_kernel, plan),
        "attn_forward",
        (shape((plan.rows, 128), bf16), shape((plan.units * BLK, 128), f32)),
        [SMEM, SMEM, VMEM],
        (VMEM, VMEM),
        plan.flops(2),
        8 * plan.rows * 128,
    )(rand, rank, kv)


def attn_backward_kernel(
    plan, rand_ref, rank_ref, kv_ref, dout_ref, lse_ref, out_ref, sum_ref
):
    rank = rank_ref[0]
    out_ref[:, 0:128] = jnp.zeros((plan.rows, 128), bf16)
    sum_ref[...] = jnp.zeros_like(sum_ref)

    def operands(half, block, unit):
        q = only_half(kv_ref[plan.at(block), 0:128], half) * 0.125
        dout = only_half(dout_ref[plan.at(block), :], half)
        return q, dout, lse_ref[plan.at(unit), :][:, 0:1]

    def emit(half, block, grad_query):
        out_ref[plan.at(block), half * HD : (half + 1) * HD] = (
            grad_query[:, half * HD : (half + 1) * HD] * 0.125
        ).astype(bf16)

    for half in range(2):
        step = plan.steps[half]
        offset = lax.rem(rank, step) if step > 1 else 0

        def turn_body(turn, carry, half=half, step=step, offset=offset):
            inners = range(2 * plan.blocks)
            listed = [
                ((2 * turn + i // plan.blocks) * step + offset) * plan.blocks + i % plan.blocks
                for i in inners
            ]
            named = [plan.named(half, block, rand_ref) for block in listed]
            given, scores, grad_probs = [], [], []
            for inner, ids in zip(inners, named):
                block = listed[inner]
                q, dout, lse = operands(half, block, plan.unit(half, 2 * turn, inner))
                if inner % plan.blocks in (0, plan.blocks - 1):
                    edge = (block == 0) | (block == plan.total - 1)
                    dout = dout * jnp.where(edge, 0.0, 1.0).astype(bf16)
                given.append((q, dout, lse))
                keys = jnp.concatenate([kv_ref[plan.at(i), 128:256] for i in ids], axis=0)
                scores.append(contract_cols(q, keys))
            for inner, ids in zip(inners, named):
                values = jnp.concatenate([kv_ref[plan.at(i), 256:384] for i in ids], axis=0)
                grad_probs.append(contract_cols(given[inner][1], values))
            low_probs, grad_scores = [], []
            for inner in inners:
                probs = jnp.exp(scores[inner] - given[inner][2])
                delta = jnp.sum(probs * grad_probs[inner], axis=-1, keepdims=True)
                grad_scores.append((probs * (grad_probs[inner] - delta)).astype(bf16))
                low_probs.append(probs.astype(bf16))
            for inner, ids in zip(inners, named):
                keys = jnp.concatenate([kv_ref[plan.at(i), 128:256] for i in ids], axis=0)
                emit(half, listed[inner], plain(grad_scores[inner], keys))
            grad_keys = [contract_rows(grad_scores[i], given[i][0]) for i in inners]
            grad_values = [contract_rows(low_probs[i], given[i][1]) for i in inners]
            for inner, ids in zip(inners, named):
                for t, i in enumerate(ids):
                    sum_ref[plan.at(i), 0:128] += grad_keys[inner][t * BLK : (t + 1) * BLK]
                    sum_ref[plan.at(i), 128:256] += grad_values[inner][t * BLK : (t + 1) * BLK]
            return carry

        lax.fori_loop(0, plan.owners[half] // 2, turn_body, 0)

    chunks = [pl.ds(c, plan.chunk) for c in range(0, plan.rows, plan.chunk)]
    for half in range(2):
        step = plan.steps[half]
        for block in (0, plan.total - 1):
            owner = block // plan.blocks

            def whole(half=half, step=step, owner=owner, block=block):
                unit = plan.unit(half, owner // step, block % plan.blocks)
                q, dout, lse = operands(half, block, unit)
                probs = [jnp.exp(contract_cols(q, kv_ref[c, 128:256]) - lse) for c in chunks]
                grad_probs = [contract_cols(dout, kv_ref[c, 256:384]) for c in chunks]
                delta = sum(
                    jnp.sum(p * g, axis=-1, keepdims=True) for p, g in zip(probs, grad_probs)
                )
                grad_query = jnp.zeros((BLK, 128), f32)
                for p, g, c in zip(probs, grad_probs, chunks):
                    grad_scores = (p * (g - delta)).astype(bf16)
                    sum_ref[c, 0:128] += contract_rows(grad_scores, q)
                    sum_ref[c, 128:256] += contract_rows(p.astype(bf16), dout)
                    grad_query += plain(grad_scores, kv_ref[c, 128:256])
                emit(half, block, grad_query)

            if step == 1:
                whole()
            else:
                pl.when(lax.rem(rank, step) == owner % step)(whole)

    out_ref[:, 128:384] = sum_ref[...].astype(bf16)


def attn_backward(plan, rand, rank, kv, dout, lse, after):
    return call(
        functools.partial(attn_backward_kernel, plan),
        "attn_backward",
        shape((plan.rows, SPAN), bf16),
        [SMEM, SMEM, VMEM, VMEM, VMEM],
        VMEM,
        plan.flops(5),
        16 * plan.rows * 128,
        [pltpu.VMEM((plan.rows, 256), f32)],
        after,
    )(rand, rank, kv, dout, lse)


def table_kernel(ranks, rows, table_ref, grad_ref, *refs):
    bias_refs, sums_refs, last_ref = refs[:2], refs[2:-1], refs[-1]
    nz, width = table_ref.shape[0], table_ref.shape[2]
    nx = width // SPAN
    tiles = [
        table_ref[k // nx][:, k % nx * SPAN : (k % nx + 1) * SPAN].astype(f32)
        for k in range(nz * nx)
    ]
    total = functools.reduce(jnp.add, [tile[rows + 1 : rows + 2] for tile in tiles])
    listed, last = len(sums_refs), last_ref.shape[1]
    for k in range(listed):
        sums_refs[k][...] = total[:, k * rows : (k + 1) * rows]
    last_ref[...] = total[:, listed * rows : listed * rows + last]
    for part in range(3):
        heads = []
        for g in range(GROUPS):
            own = [tiles[g * ranks + r][:, part * 128 : part * 128 + HD] for r in range(ranks)]
            shared = [tiles[g * ranks + r][:, part * 128 + HD : (part + 1) * 128] for r in range(ranks)]
            for group in (own[: ranks // 2], own[ranks // 2 :], shared):
                heads.append(functools.reduce(jnp.add, group))
        whole = jnp.concatenate(heads, axis=1)
        grad_ref[:, part * H * HD : (part + 1) * H * HD] = whole[0:rows]
        if part != 1:
            bias_refs[part // 2][...] = whole[rows : rows + 1]


def table_grads(ranks, rows, listed, table):
    return call(
        functools.partial(table_kernel, ranks, rows),
        "table_grads",
        [
            shape((rows, 3 * H * HD), f32),
            *[shape((1, H * HD), f32)] * 2,
            *[shape((1, rows), f32)] * 6,
            shape((1, (listed - 6) * rows), f32),
        ],
        [VMEM],
        [VMEM] * 10,
        table.size,
        2 * table.size,
    )(table)


def reorder_kernel(outer, inner, rows, in_ref, out_ref):
    value = in_ref[...].astype(f32)
    out_ref[...] = jnp.concatenate(
        [
            value[:, (o * inner + i) * rows : (o * inner + i + 1) * rows]
            for i in range(inner)
            for o in range(outer)
        ],
        axis=1,
    ).astype(out_ref.dtype)


def reordered(value, outer, inner):
    rows, cols = value.shape
    run = cols // (outer * inner)
    if run < 8:
        return value.reshape(rows, outer, inner, run).transpose(0, 2, 1, 3).reshape(rows, cols)
    return call(
        functools.partial(reorder_kernel, outer, inner, run),
        "reorder",
        shape((rows, cols), value.dtype),
        [VMEM],
        VMEM,
        rows * cols,
        4 * rows * cols,
    )(value)


def pack_kernel(outer, inner, out_w_ref, up_ref, down_ref, packed_ref):
    rows, width = out_w_ref.shape
    packed_ref[:, 0:width] = out_w_ref[...]
    up = up_ref[...].astype(f32)
    down = down_ref[...].astype(f32)
    for i in range(inner):
        packed_ref[:, (1 + i) * width : (2 + i) * width] = jnp.concatenate(
            [
                up[:, (o * inner + i) * rows : (o * inner + i + 1) * rows]
                for o in range(outer)
            ],
            axis=1,
        ).astype(bf16)
        packed_ref[:, (1 + inner + i) * width : (2 + inner + i) * width] = down[
            i * rows : (i + 1) * rows
        ].astype(bf16)


def packed_weights(out_weight, up_weight, down_weight, devices):
    rows, width = out_weight.shape
    turns = up_weight.shape[1] // width
    if rows < 8:
        up = reordered(up_weight, devices, turns)
        down = down_weight.reshape(turns, rows, width).transpose(1, 0, 2)
        return jnp.concatenate([out_weight, up, down.reshape(rows, turns * width)], axis=1)
    return call(
        functools.partial(pack_kernel, devices, turns),
        "packed_weights",
        shape((rows, (1 + 2 * turns) * width), bf16),
        [VMEM] * 3,
        VMEM,
        rows * width,
        rows * width,
    )(out_weight, up_weight, down_weight)


def normalized(values):
    center = values - jnp.mean(values, axis=-1, keepdims=True)
    spread = jnp.mean(center * center, axis=-1, keepdims=True)
    scale = lax.rsqrt(spread + norm_eps)
    return center * scale, scale


def normalized_grad(normal, scale, grad):
    return scale * (
        grad
        - jnp.mean(grad, axis=-1, keepdims=True)
        - normal * jnp.mean(grad * normal, axis=-1, keepdims=True)
    )


def column_sum(values):
    return jnp.sum(values.astype(f32), axis=0, keepdims=True)


def middle_kernel(
    ranks,
    back_ref,
    tok_ref,
    cot_ref,
    vec_ref,
    pack_ref,
    output_ref,
    resid_ref,
    dout_ref,
    attn_ref,
    mid_ref,
    act_ref,
    down_ref,
    pre_ref,
    branch_ref,
    sums_ref,
    out_w,
    up_w,
    down_w,
    slope_ref,
    sems,
):
    count = back_ref.shape[0]
    width = tok_ref.shape[1]
    turns = up_w.shape[1] // width
    half_ranks = ranks // 2

    copies = [pltpu.make_async_copy(pack_ref.at[:, pl.ds(0, width)], out_w, sems.at[0])]
    for t in range(turns):
        cols = pl.ds(t * width, width)
        copies.append(
            pltpu.make_async_copy(
                pack_ref.at[:, pl.ds((1 + t) * width, width)], up_w.at[:, cols], sems.at[1 + t]
            )
        )
        copies.append(
            pltpu.make_async_copy(
                pack_ref.at[:, pl.ds((1 + turns + t) * width, width)],
                down_w.at[t],
                sems.at[1 + turns + t],
            )
        )
    for copy in copies:
        copy.start()

    for g in range(GROUPS):
        own = [back_ref[g * ranks + r][:, 0:HD] for r in range(ranks)]
        shared = [back_ref[g * ranks + r][:, HD : 2 * HD] for r in range(ranks)]
        trio = [sum(own[1:half_ranks], own[0]), sum(own[half_ranks + 1 :], own[half_ranks])]
        trio.append(sum(shared[1:], shared[0]))
        attn_ref[:, g * PER_GROUP * HD : (g + 1) * PER_GROUP * HD] = jnp.concatenate(trio, axis=1)

    out_bias, attn_gain, attn_shift, down_bias, ffn_gain, ffn_shift = (
        vec_ref[k : k + 1, :] for k in range(2, 8)
    )
    copies[0].wait()
    branch = plain(attn_ref[...], out_w[...]) + out_bias
    normal, scale = normalized(tok_ref[...].astype(f32) + branch)
    mid = normal * attn_gain + attn_shift
    mid_low = mid.astype(bf16)
    mid_ref[...] = mid_low
    final = mid + down_bias
    for t in range(turns):
        cols = slice(t * width, (t + 1) * width)
        copies[1 + 2 * t].wait()
        pre = plain(mid_low, up_w[:, cols]) + vec_ref[8 + t : 9 + t, :]
        square = pre * pre
        bend = jnp.tanh(gelu_root * (pre + gelu_cubic * pre * square))
        rise = 0.5 * (1.0 + bend)
        slope_ref[:, cols] = rise + 0.5 * pre * (1.0 - bend * bend) * (
            gelu_root * (1.0 + 3.0 * gelu_cubic * square)
        )
        act = (pre * rise).astype(bf16)
        act_ref[:, cols] = act
        copies[2 + 2 * t].wait()
        final = final + plain(act, down_w[t])
    normal_two, scale_two = normalized(final)
    output_ref[...] = (normal_two * ffn_gain + ffn_shift).astype(bf16)
    cot = cot_ref[...].astype(f32)
    sums_ref[4:5, :] = column_sum(cot * normal_two)
    sums_ref[5:6, :] = column_sum(cot)
    grad_final = normalized_grad(normal_two, scale_two, cot * ffn_gain)
    down_low = grad_final.astype(bf16)
    down_ref[...] = down_low
    sums_ref[3:4, :] = column_sum(down_low)
    grad_mid = grad_final
    for t in range(turns):
        cols = slice(t * width, (t + 1) * width)
        grad_pre = (contract_cols(down_low, down_w[t]) * slope_ref[:, cols]).astype(bf16)
        pre_ref[:, cols] = grad_pre
        sums_ref[6 + t : 7 + t, :] = column_sum(grad_pre)
        grad_mid = grad_mid + contract_cols(grad_pre, up_w[:, cols])
    sums_ref[1:2, :] = column_sum(grad_mid * normal)
    sums_ref[2:3, :] = column_sum(grad_mid)
    resid = normalized_grad(normal, scale, grad_mid * attn_gain)
    resid_ref[...] = resid
    branch_low = resid.astype(bf16)
    branch_ref[...] = branch_low
    sums_ref[0:1, :] = column_sum(branch_low)
    grad_attn = contract_cols(branch_low, out_w[...]).astype(bf16)
    for j in range(count):
        first, shared = heads_of(j, ranks)
        dout_ref[j] = jnp.concatenate(
            [
                grad_attn[:, first * HD : (first + 1) * HD],
                grad_attn[:, shared * HD : (shared + 1) * HD],
            ],
            axis=1,
        )


def middle(ranks, back, tokens, cotangent, vectors, packed):
    count, (tok, width) = back.shape[0], tokens.shape
    turns = vectors.shape[0] - 8
    hidden = turns * width
    return call(
        functools.partial(middle_kernel, ranks),
        "middle",
        [
            shape((tok, width), bf16),
            shape((tok, width), f32),
            shape((count, tok, 128), bf16),
            shape((tok, width), bf16),
            shape((tok, width), bf16),
            shape((tok, hidden), bf16),
            shape((tok, width), bf16),
            shape((tok, hidden), bf16),
            shape((tok, width), bf16),
            shape((6 + turns, width), f32),
        ],
        [VMEM] * 4 + [ANY],
        [VMEM] * 10,
        4 * tok * width * (width + 2 * hidden),
        2 * width * (width + 2 * hidden),
        [
            pltpu.VMEM((width, width), bf16),
            pltpu.VMEM((width, hidden), bf16),
            pltpu.VMEM((turns, width, width), bf16),
            pltpu.VMEM((tok, hidden), f32),
            pltpu.SemaphoreType.DMA((1 + 2 * turns,)),
        ],
    )(back, tokens, cotangent, vectors, packed)


def weight_grad_kernel(pairs, where_ref, *refs):
    operands, outs, total_ref = refs[: 2 * len(pairs)], refs[2 * len(pairs) : -1], refs[-1]
    turn = pl.program_id(0)
    first = 0
    for k, turns in enumerate(pairs):

        def product(left_ref=operands[2 * k], right_ref=operands[2 * k + 1]):
            total_ref[...] = contract_rows(left_ref[...], right_ref[...])

        pl.when((turn >= first) & (turn < first + turns))(product)
        first += turns
    ny = len(outs) // 2
    rows = total_ref.shape[0] // (2 * ny)
    mine, core = where_ref[0], where_ref[1]
    for d in range(ny):
        base = lax.rem(mine + d, ny) * 2
        for ref, c in ((outs[d], core), (outs[ny + d], 1 - core)):
            ref[0] = total_ref[pl.ds(pl.multiple_of((base + c) * rows, 16), rows), :].astype(bf16)


def weight_grad(where, ny, *pairs):
    tok = pairs[0][0].shape[0]
    width = min(min(left.shape[1], right.shape[1]) for left, right in pairs)
    counts, specs, first = [], [], 0
    for pair in pairs:
        turns = max(operand.shape[1] for operand in pair) // width
        for operand in pair:
            if operand.shape[1] == width:
                specs.append(pl.BlockSpec((tok, width), lambda t: (0, 0)))
            else:
                specs.append(
                    pl.BlockSpec(
                        (tok, width),
                        lambda t, first=first, turns=turns: (0, jnp.clip(t - first, 0, turns - 1)),
                    )
                )
        counts.append(turns)
        first += turns
    rows = width // (2 * ny)
    parts = pl.pallas_call(
        functools.partial(weight_grad_kernel, counts),
        grid=(first,),
        out_shape=[shape((first, rows, width), bf16)] * (2 * ny),
        in_specs=[SMEM] + specs,
        out_specs=[pl.BlockSpec((1, rows, width), lambda t: (t, 0, 0))] * (2 * ny),
        scratch_shapes=[pltpu.VMEM((width, width), f32)],
        cost_estimate=pl.CostEstimate(
            flops=2 * tok * width * width * first,
            bytes_accessed=2 * width * width * first,
            transcendentals=0,
        ),
        compiler_params=pltpu.CompilerParams(vmem_limit_bytes=VMEM_BYTES),
        name="weight_grad",
    )(where, *[operand for pair in pairs for operand in pair])
    return parts[:ny], parts[ny:]


def swap(value, axis):
    return lax.all_to_all(value, axis, split_axis=0, concat_axis=0, tiled=True)


def shifted(value, axis, by):
    size = lax.axis_size(axis)
    return lax.ppermute(value, axis, [(i, (i + by) % size) for i in range(size)])


def far_first(size):
    return sorted(range(1, size), key=lambda d: -min(d, size - d))


def picked(value, axis, dim):
    size, here = lax.axis_size(axis), lax.axis_index(axis)

    def part(d):
        return lax.dynamic_index_in_dim(
            value, lax.rem(here + d, size), dim, keepdims=False
        ).astype(f32)

    return part


def split(value, nz, nx):
    return value.reshape(value.shape[:-2] + (nz, nx, value.shape[-2] // (nz * nx), value.shape[-1]))


def along_y(value):
    return lambda d: value[d]


def along_x(value):
    return picked(value, "x", value.ndim - 3)


def sends(parts, size):
    return [parts(d).astype(bf16) for d in far_first(size)]


def arrivals(sent, axis):
    return [shifted(part, axis, d) for d, part in zip(far_first(len(sent) + 1), sent)]


def plus(kept, got):
    return functools.reduce(lambda total, part: total + part.astype(f32), got, kept)


def summed(parts, axis):
    return plus(parts(0), arrivals(sends(parts, lax.axis_size(axis)), axis))


def body(
    tokens,
    qkv_weight,
    query_bias,
    value_bias,
    out_weight,
    out_bias,
    attn_gain,
    attn_shift,
    up_weight,
    up_bias,
    down_weight,
    down_bias,
    ffn_gain,
    ffn_shift,
    random_blocks,
    cotangent,
):
    ny, nc, nz, nx = (lax.axis_size(a) for a in ALL)
    count, devices = nz * nx, ny * nc * nz * nx
    ranks = count // GROUPS
    half_ranks = ranks // 2
    _, tok, width = tokens.shape
    blocks = tok // BLK
    plan = Plan(count, ranks, blocks)
    z, x = lax.axis_index("z"), lax.axis_index("x")
    ctx_index = z * nx + x
    rank = lax.rem(ctx_index, ranks).astype(jnp.int32).reshape(1)
    where = jnp.stack([lax.axis_index("y"), lax.axis_index("core")]).astype(jnp.int32)
    rows = qkv_weight.shape[0]
    hidden = up_weight.shape[1]
    turns = hidden // width
    flat_tokens = tokens.reshape(tok, width)

    packed = packed_weights(out_weight, up_weight, down_weight, devices)
    packed = lax.all_gather(packed, ALL, axis=0, tiled=True)

    def by_index(values):
        grouped = values.reshape(values.shape[:-2] + (GROUPS, PER_GROUP, values.shape[-1]))
        pairs = [
            jnp.stack([grouped[..., 0 if r < half_ranks else 1, :], grouped[..., 2, :]], axis=-2)
            for r in range(ranks)
        ]
        return jnp.moveaxis(jnp.stack(pairs, axis=-3), (-4, -3), (0, 1)).reshape(
            (count,) + values.shape[:-2] + (2, values.shape[-1])
        )

    weight_rows = by_index(qkv_weight.reshape(rows, 3, H, HD)).reshape(count, rows, SPAN)
    picks = by_index(random_blocks[0].astype(bf16)).reshape(count, 1, -1)
    entries = picks.shape[2]
    small = jnp.concatenate(
        [
            query_bias,
            value_bias,
            out_bias,
            attn_gain,
            attn_shift,
            down_bias,
            ffn_gain,
            ffn_shift,
            up_bias,
        ]
    )
    many = small.shape[0] // rows
    extra = -(-(rows + 2) // 8) * 8
    sent = jnp.concatenate(
        [
            weight_rows,
            jnp.pad(picks, ((0, 0), (0, 0), (0, SPAN - entries))),
            jnp.broadcast_to(jnp.pad(small, (0, SPAN - small.shape[0])), (count, 1, SPAN)),
            jnp.zeros((count, extra - rows - 2, SPAN), bf16),
        ],
        axis=1,
    )
    near = [d for d in range(1, nz) if min(d, nz - d) == 1]
    held = {0: flat_tokens}
    over = {}
    for e in range(1, nx):
        over[0, e] = shifted(flat_tokens, "x", e)
    for d in near:
        held[d] = shifted(flat_tokens, "z", d)
    for d in range(2, nz - 1):
        held[d] = shifted(tied(flat_tokens, over[0, 1]), "z", d)
    line = swap(sent, CTX)
    shifts = [0] + near + [d for d in far_first(nz) if d not in near]
    order = [(d, e) for e in range(nx) for d in shifts]
    pieces = []
    for d, e in order:
        if e and d:
            over[d, e] = shifted(held[d], "x", e)
        pieces.append(over[d, e] if e else held[d])
    owners = jnp.stack(
        [lax.rem(z + nz - d, nz) * nx + lax.rem(x + nx - e, nx) for d, e in order]
    ).astype(jnp.int32)
    targets = jnp.stack(
        [lax.rem(z + d, nz) * nx + lax.rem(x + e, nx) for d, e in order]
    ).astype(jnp.int32)
    rand = line[:, rows, :entries].astype(jnp.int32).reshape(-1)
    seqs = ny * nc
    full = swap(
        tied(jnp.broadcast_to(line[None], (seqs,) + line.shape), over[0, 1], *(over[d, 1] for d in near), *held.values()), SEQ
    )
    columns = full[:, :, :rows].reshape(width, SPAN)
    vectors = full[:, :, rows + 1, : small.shape[0]].astype(f32)
    vectors = vectors.reshape(devices, many, rows).transpose(1, 0, 2).reshape(many, width)
    bias_table = by_index(
        jnp.stack([vectors[0], jnp.zeros_like(vectors[0]), vectors[1]]).reshape(3, H, HD)
    ).reshape(count, 1, SPAN)
    bias = lax.dynamic_index_in_dim(bias_table, ctx_index, 0, keepdims=False)

    kv = qkv_project(owners, pieces, columns, bias)
    attended, lse = attn_forward(plan, rand, rank, kv)
    back = swap(attended.reshape(count, tok, 128), CTX)

    output, resid, dout, attn_low, mid_low, act_low, down_low, pre_low, branch_low, sums = middle(
        ranks, back, flat_tokens, cotangent.reshape(tok, width), vectors, packed
    )

    first_keep, first_send = weight_grad(where, ny, (act_low, down_low), (attn_low, branch_low))
    second_keep, second_send = weight_grad(where, ny, (mid_low, pre_low))
    first_got = [shifted(part, "core", 1) for part in first_send]
    second_got = [shifted(part, "core", 1) for part in second_send]

    def terms_of(parts, d):
        at = lax.rem(x + d, nx)
        parts = [lax.dynamic_index_in_dim(part, at, part.ndim - 3, keepdims=False) for part in parts]
        return functools.reduce(jnp.add, [part.astype(f32) for part in parts])

    def by_y(pair, d):
        return [split(part[d], nz, nx) for part in pair]

    first_pair, second_pair = (first_keep, first_got), (second_keep, second_got)
    first_sent = [
        functools.reduce(jnp.add, [part.astype(f32) for part in by_y(first_pair, d)]).astype(bf16)
        for d in far_first(ny)
    ]
    second_sent = [
        jnp.stack([terms_of(by_y(second_pair, d), e) for d in range(ny)]).astype(bf16)
        for e in far_first(nx)
    ]

    dout = swap(tied(dout, *first_sent), CTX).reshape(plan.rows, 128)
    second_sent, dout = lax.optimization_barrier((second_sent, dout))
    grads = attn_backward(plan, rand, rank, kv, dout, lse, [])
    first_more, second_more = arrivals(first_sent, "y"), arrivals(second_sent, "x")

    def first_part(e, pair):
        return terms_of(by_y(pair, 0) + first_more, e)

    def second_part(d, pair):
        return plus(terms_of(by_y(pair, d), 0), [part[d] for part in second_more])

    first_late = tied(first_pair, grads)
    first_sent = [first_part(e, first_late).astype(bf16) for e in far_first(nx)]
    second_more = [tied(part, *first_sent) for part in second_more]
    second_late = tied(second_pair, *first_sent)
    second_sent = [second_part(d, second_late).astype(bf16) for d in far_first(ny)]
    terms = token_grads(count, targets, tied(grads, *first_sent, *second_sent), columns, [])
    first_next, second_next = arrivals(first_sent, "x"), arrivals(second_sent, "y")
    column_grads, bias_grads = qkv_grads(
        owners, pieces, tied(grads, terms[0], *first_next, *second_next), []
    )

    def over_x(d, *others):
        return [
            shifted(tied(terms[e * nz + shifts.index(d)], *others), "x", e) for e in range(1, nx)
        ]

    line_order = far_first(nz)
    across = {d: over_x(d) for d in line_order}

    line = jnp.concatenate(
        [
            plus(first_part(0, tied(first_late, terms[0])), first_next).astype(bf16).transpose(1, 0, 2, 3),
            plus(second_part(0, tied(second_late, terms[0])), second_next).astype(bf16).transpose(1, 0, 2, 3),
        ],
        axis=1,
    )
    line = swap(tied(line, *across[line_order[0]]), "z")

    total = added(
        [
            [tied(terms[shifts.index(d)], column_grads)] + across[d]
            for d in line_order
        ],
        [],
    )
    early = total[0]
    total = [tied(part, line) for part in total]
    line_got = [shifted(part, "z", d) for d, part in zip(line_order, total)]
    own = plus(terms[0].astype(f32), over_x(0, *total))
    tokens_grad = plus(resid + own, line_got).reshape(1, tok, width)

    listed = sums.shape[0]
    vector_sums = sums.reshape(listed, ny, nc, count, rows).transpose(1, 2, 3, 0, 4)
    vector_sums = vector_sums.reshape(ny, nc, nz, nx, 1, listed * rows).astype(bf16)
    units = -(-(rows + 2) // rows)
    table = jnp.concatenate(
        [
            tied(column_grads, early).reshape(ny, nc, nz, nx, rows, SPAN),
            jnp.broadcast_to(bias_grads.astype(bf16), (ny, nc, nz, nx, 1, SPAN)),
            jnp.pad(vector_sums, ((0, 0),) * 5 + ((0, SPAN - listed * rows),)),
            jnp.zeros((ny, nc, nz, nx, units * rows - rows - 2, SPAN), bf16),
        ],
        axis=4,
    )
    table = tied(summed(picked(table, "core", 1), "core"), line)
    table = summed(picked(table, "y", 0), "y").astype(bf16)
    mine = picked(table, "x", 1)
    own, other = mine(0).astype(bf16), shifted(mine(1).astype(bf16), "x", 1)
    table = jnp.where(x == 0, jnp.stack([own, other], 2), jnp.stack([other, own], 2))

    weight_sums = jnp.sum(line.astype(f32), axis=0)
    down_grad = weight_sums[:turns].reshape(turns * rows, width)
    out_grad = weight_sums[turns]
    up_grad = weight_sums[turns + 1 :].transpose(1, 0, 2).reshape(rows, hidden)
    up_grad = reordered(up_grad, turns, devices)
    table = tied(table.reshape(nz, units * rows, nx * SPAN), up_grad, out_grad, down_grad)
    table = swap(table, "z")
    qkv_grad, query_sums, value_sums, *shards, up_bias_grad = table_grads(ranks, rows, listed, table)
    shards = [shard.reshape(rows) for shard in shards]
    device = (lax.axis_index("y") * nc + lax.axis_index("core")) * count + ctx_index
    query_bias_grad = lax.dynamic_slice_in_dim(query_sums[0], device * rows, rows)
    value_bias_grad = lax.dynamic_slice_in_dim(value_sums[0], device * rows, rows)

    return (
        output.reshape(1, tok, width),
        tokens_grad,
        qkv_grad,
        query_bias_grad,
        value_bias_grad,
        out_grad,
        shards[0],
        shards[1],
        shards[2],
        up_grad,
        up_bias_grad.reshape(-1),
        down_grad,
        shards[3],
        shards[4],
        shards[5],
    )


def solution(mesh):
    dp, ctx = (mesh.shape[a] for a in ("dp", "ctx"))
    fine = Mesh(mesh.devices.reshape(dp // 2, 2, ctx // 2, 2), ALL)
    token_spec = P(SEQ, CTX, None)
    matrix, vector = P(ALL, None), P(ALL)
    return jax.shard_map(
        body,
        mesh=fine,
        in_specs=(
            token_spec,
            matrix,
            vector,
            vector,
            matrix,
            vector,
            vector,
            vector,
            matrix,
            vector,
            matrix,
            vector,
            vector,
            vector,
            P(SEQ, CTX, None, None),
            token_spec,
        ),
        out_specs=(
            token_spec,
            token_spec,
            matrix,
            vector,
            vector,
            matrix,
            vector,
            vector,
            vector,
            matrix,
            vector,
            matrix,
            vector,
            vector,
            vector,
        ),
        check_vma=False,
    )
```
